256 devices in a mesh: seq: 8 (over y, core), doc: 32 (over x, z).
Axes of the slice: x: 4, y: 4, z: 8, core: 2. Of those that a mesh axis runs over, the one named last changes fastest.
Arguments:
- queries: bfloat16 [32, 1024, 2048], P('doc', 'seq'), may hold values from -6 to 6
- keys: bfloat16 [32, 1024, 2048], P('doc', 'seq'), may hold values from -6 to 6
- values: bfloat16 [32, 1024, 2048], P('doc', 'seq'), may hold values from -6 to 6
- w_out: bfloat16 [2048, 2048], P('doc'), may hold values from -0.5 to 0.5
- norm_gain: float32 [2048], replicated, may hold values from 0.1 to 1.9
- w_vocab: bfloat16 [2048, 28672], P(None, 'doc')
- targets: int32 [32, 1024], P('doc', 'seq'), may hold values from 0 to 28671
- domains: int32 [32], replicated, may hold values from 0 to 6, as said below
Outputs:
- projected: bfloat16 [32, 1024, 2048], P('doc', 'seq')
- token_loss: float32 [32, 1024], P('doc', 'seq')
- domain_mean: float32 [7], replicated
The draws below stay inside these ranges and needn't reach their ends.
Inputs may be any that keep to these rules, and one draw needn't show every extreme that they name: Every one of the 7 domains has at least one document.
All inputs are finite; a program needn't handle non-finite values.
Results may differ from the reference program's by a relative error of at most 0.007.
Values may be sent and summed in bfloat16 or wider, within the bound.
A program may use at most 64 MiB of HBM per device.

```python
import math
import jax
import jax.numpy as jnp
import numpy as np
from jax import lax

HEADS = 16
HD = 128
D = 2048
VOCAB = 28672
DOMAINS = 7
BLOCK = 128
LENGTH = 1024
DOCS = 32


def draw_domains(key, part):
    domain_ids = jax.random.randint(jax.random.fold_in(key, 11), (DOCS,), 0, DOMAINS)
    shuffled = jax.random.permutation(jax.random.fold_in(key, 12), DOCS)
    domain_ids = domain_ids.at[shuffled[:DOMAINS]].set(jnp.arange(DOMAINS, dtype=jnp.int32))
    return domain_ids.astype(jnp.int32)


def draw_w_vocab(key, part):
    columns = jax.random.normal(jax.random.fold_in(key, 21), (D, VOCAB), jnp.float32) * (3.0 / math.sqrt(D))
    return columns.astype(jnp.bfloat16)


def plant(array, stream_key, least, high):
    longest = array.shape.index(max(array.shape))
    spots = []
    for shift in (0, 1):
        where = [jax.random.randint(jax.random.fold_in(stream_key, axis), (), 0, length) for axis, length in enumerate(array.shape)]
        where[longest] = (where[longest] + shift) % array.shape[longest]
        spots.append(tuple(where))
    return array.at[spots[0]].set(least).at[spots[1]].set(high)


def block_scale(rng, dims, pieces, least, top_value):
    def one(dim, shards_of):
        steps = jax.random.uniform(jax.random.fold_in(jax.random.fold_in(rng, 6), dim), (shards_of,), jnp.float32, least / len(pieces), top_value / len(pieces))
        return jnp.repeat(jnp.exp(steps), dims[dim] // shards_of).reshape((-1,) + (1,) * (len(dims) - dim - 1))

    level = one(*pieces[0])
    for cut in pieces[1:]:
        level = level * one(*cut)
    return level


def rank_bounds(amount, slope):
    portions = [(1 << 20) // math.isqrt(standing ** slope) + 1 for standing in range(1, amount + 1)]
    scale = 1 + sum(portions) // (1 << 30)
    return np.cumsum(np.array([max(1, weight // scale) for weight in portions]))


def ranked_ids(rng, shape, number_of, slope):
    listing = rank_bounds(number_of, slope)
    pick = jax.random.randint(jax.random.fold_in(rng, 1), shape, 0, int(listing[number_of - 1]))
    rank = jnp.searchsorted(jnp.asarray(listing, jnp.int32), pick, side="right")
    return jax.random.permutation(jax.random.fold_in(rng, 2), number_of)[rank].astype(jnp.int32)


def gaussian(stream_key, dims, deviation, reach, cuts=(), kind=jnp.bfloat16):
    gain = block_scale(stream_key, dims, cuts, -0.22, 0.18) if cuts else 1.0
    array = jax.random.normal(stream_key, dims, jnp.float32) * deviation * gain
    return jnp.minimum(jnp.maximum(array, -reach), reach).astype(kind)


def setup_inputs(seed: int = 0) -> dict:
    arg_keys = jax.random.split(jax.random.key(seed), 9)
    return {
        "queries": gaussian(arg_keys[0], (DOCS, LENGTH, D), 1.0, 6.0, ((0, 32), (1, 8))),
        "keys": gaussian(arg_keys[1], (DOCS, LENGTH, D), 1.0, 6.0, ((0, 32), (1, 8))),
        "values": gaussian(arg_keys[2], (DOCS, LENGTH, D), 1.0, 6.0, ((0, 32), (1, 8))),
        "w_out": gaussian(arg_keys[3], (D, D), (D // 16) ** -0.5, 0.5, ((0, 32),)),
        "norm_gain": jnp.clip(1.0 + 0.18 * jax.random.normal(arg_keys[4], (D,), jnp.float32), 0.1, 1.9),
        "w_vocab": draw_w_vocab(jax.random.fold_in(arg_keys[8], 71), 0),
        "targets": plant(ranked_ids(arg_keys[6], (DOCS, LENGTH), VOCAB, 2), jax.random.fold_in(arg_keys[6], 3), 0, VOCAB - 1).astype(jnp.int32),
        "domains": draw_domains(jax.random.fold_in(arg_keys[8], 71), 0),
    }


def features(inputs):
    return (1.0 + jax.nn.elu(inputs.astype(jnp.float32))).astype(jnp.bfloat16)

def attend_doc(doc_arrays):
    query_rows, key_rows, value_rows = doc_arrays
    blocks = LENGTH // BLOCK
    query_feat = features(query_rows).reshape(blocks, BLOCK, HEADS, HD)
    key_feat = features(key_rows).reshape(blocks, BLOCK, HEADS, HD)
    value_blk = value_rows.reshape(blocks, BLOCK, HEADS, HD)
    causal = jnp.tril(jnp.ones((BLOCK, BLOCK), dtype=bool))
    high = lax.Precision.HIGHEST

    def block_step(carry, inputs):
        state, key_sum = carry
        blk_query, blk_key, blk_value = inputs
        query_wide = blk_query.astype(jnp.float32)
        key_wide = blk_key.astype(jnp.float32)
        value_wide = blk_value.astype(jnp.float32)
        scores = jnp.einsum('thf,shf->hts', query_wide, key_wide, precision=high)
        probs = jnp.where(causal[None], scores, 0.0).astype(jnp.bfloat16)
        state_low = lax.optimization_barrier(state.astype(jnp.bfloat16))
        numer = jnp.einsum('hts,she->the', probs.astype(jnp.float32), value_wide, precision=high)
        numer = numer + jnp.einsum('thf,hfe->the', query_wide, state_low.astype(jnp.float32), precision=high)
        denom = lax.optimization_barrier(jnp.sum(probs.astype(jnp.float32), axis=2)).T
        denom = denom + jnp.einsum('thf,hf->th', query_wide, key_sum, precision=high)
        outputs = (numer / denom[:, :, None]).astype(jnp.bfloat16)
        state = state + jnp.einsum('shf,she->hfe', key_wide, value_wide, precision=high)
        key_sum = key_sum + lax.optimization_barrier(jnp.sum(key_wide, axis=0))
        return ((state, key_sum), outputs)
    start = (jnp.zeros((HEADS, HD, HD), jnp.float32), jnp.zeros((HEADS, HD), jnp.float32))
    _, outputs = lax.scan(block_step, start, (query_feat, key_feat, value_blk))
    return outputs.reshape(LENGTH, HEADS * HD)

def reference(queries, keys, values, w_out, norm_gain, w_vocab, targets, domains):
    attended = lax.map(attend_doc, (queries, keys, values))

    def project(rows):
        return jnp.dot(rows, w_out, preferred_element_type=jnp.float32).astype(jnp.bfloat16)
    projected = lax.map(project, attended)
    wide = projected.astype(jnp.float32)
    normed = (wide * lax.rsqrt(lax.optimization_barrier(jnp.mean(wide * wide, axis=-1, keepdims=True)) + 1e-05) * norm_gain).astype(jnp.bfloat16)
    vocab_wide = w_vocab.astype(jnp.float32)

    def doc_loss(doc_arrays):
        normed_rows, target_rows = doc_arrays
        logits = jnp.dot(normed_rows.astype(jnp.float32), vocab_wide, precision=lax.Precision.HIGHEST)
        log_total = jax.nn.logsumexp(logits, axis=-1)
        target_hit = jnp.take_along_axis(logits, target_rows[:, None].astype(jnp.int32), axis=1)[:, 0]
        return log_total - target_hit
    token_loss = lax.map(doc_loss, (normed, targets))
    doc_sums = lax.optimization_barrier(jnp.sum(token_loss, axis=1))
    onehot = (domains[:, None] == jnp.arange(DOMAINS, dtype=jnp.int32)[None, :]).astype(jnp.float32)
    totals = lax.optimization_barrier(jnp.sum(doc_sums[:, None] * onehot, axis=0))
    counts = lax.optimization_barrier(jnp.sum(onehot, axis=0)) * LENGTH
    return (projected, token_loss, totals / counts)
```

```python
import jax
import jax.numpy as jnp
from jax import lax
from jax.sharding import PartitionSpec as P

HEADS = 16
HD = 128
DOMAINS = 7
BLOCK = 128


def features(inputs):
    return (1.0 + jax.nn.elu(inputs.astype(jnp.float32))).astype(jnp.bfloat16)


def attend_blocks(query_feat, key_feat, value_blk, block_states, block_keys, state_in, sum_in):
    causal = jnp.tril(jnp.ones((BLOCK, BLOCK), dtype=bool))

    def block_step(carry, inputs):
        state, key_sum = carry
        blk_query, blk_key, blk_value, blk_state, blk_keysum = inputs
        scores = jnp.einsum("thf,shf->hts", blk_query, blk_key, preferred_element_type=jnp.float32)
        probs = jnp.where(causal[None], scores, 0.0).astype(jnp.bfloat16)
        numer = jnp.einsum("hts,she->the", probs, blk_value, preferred_element_type=jnp.float32)
        numer = numer + jnp.einsum(
            "thf,hfe->the",
            blk_query,
            state.astype(jnp.bfloat16),
            preferred_element_type=jnp.float32,
        )
        denom = jnp.sum(probs, axis=2, dtype=jnp.float32).T
        denom = denom + jnp.einsum(
            "thf,hf->th", blk_query.astype(jnp.float32), key_sum, precision=lax.Precision.HIGHEST
        )
        outputs = (numer / denom[:, :, None]).astype(jnp.bfloat16)
        return ((state + blk_state, key_sum + blk_keysum), outputs)

    _, outputs = lax.scan(
        block_step, (state_in, sum_in), (query_feat, key_feat, value_blk, block_states, block_keys)
    )
    return outputs


def on_device(queries, keys, values, w_out, norm_gain, w_vocab, targets, domains):
    tokens = queries.shape[1]
    blocks = tokens // BLOCK
    width = HEADS * HD
    query_feat = features(queries[0]).reshape(blocks, BLOCK, HEADS, HD)
    key_feat = features(keys[0]).reshape(blocks, BLOCK, HEADS, HD)
    value_blk = values[0].reshape(blocks, BLOCK, HEADS, HD)
    block_states = jnp.einsum(
        "bshf,bshe->bhfe", key_feat, value_blk, preferred_element_type=jnp.float32
    )
    block_keys = jnp.sum(key_feat, axis=1, dtype=jnp.float32)
    state_local = jnp.sum(block_states, axis=0)
    sum_local = jnp.sum(block_keys, axis=0)
    seq_count, seq_mine = (lax.axis_size("seq"), lax.axis_index("seq"))
    pieces = lax.all_gather(state_local.astype(jnp.bfloat16), "seq")
    sums = lax.all_gather(sum_local, "seq")
    earlier = (jnp.arange(seq_count) < seq_mine).astype(jnp.float32)
    state_in = jnp.sum(pieces.astype(jnp.float32) * earlier[:, None, None, None], axis=0)
    sum_in = jnp.sum(sums * earlier[:, None, None], axis=0)
    attended = attend_blocks(
        query_feat, key_feat, value_blk, block_states, block_keys, state_in, sum_in
    ).reshape(tokens, width)
    projected = jnp.dot(
        attended,
        lax.all_gather(w_out, "doc", axis=0, tiled=True),
        preferred_element_type=jnp.float32,
    ).astype(jnp.bfloat16)
    wide = projected.astype(jnp.float32)
    normed = (
        wide * lax.rsqrt(jnp.mean(wide * wide, axis=-1, keepdims=True) + 1e-05) * norm_gain
    ).astype(jnp.bfloat16)
    vocab_local = w_vocab.shape[1]
    all_targets = lax.all_gather(targets, "doc", axis=0, tiled=True)
    local_ids = all_targets - lax.axis_index("doc") * vocab_local
    vocab_iota = jnp.arange(vocab_local, dtype=jnp.int32)
    logits = jnp.einsum(
        "ntd,dv->ntv",
        lax.all_gather(normed[None], "doc", axis=0, tiled=True),
        w_vocab,
        preferred_element_type=jnp.float32,
    )
    maxima = jnp.max(logits, axis=-1)
    totals = jnp.sum(jnp.exp(logits - maxima[:, :, None]), axis=-1)
    target_hit = jnp.sum(
        jnp.where(vocab_iota[None, None, :] == local_ids[:, :, None], logits, 0.0), axis=-1
    )
    onehot = (domains[:, None] == jnp.arange(DOMAINS, dtype=jnp.int32)[None, :]).astype(jnp.float32)
    stats = jnp.stack((maxima, totals, target_hit), axis=1)
    stats = lax.all_to_all(stats, "doc", 0, 0, tiled=True)
    top = jnp.max(stats[:, 0], axis=0)
    summed = jnp.sum(stats[:, 1] * jnp.exp(stats[:, 0] - top[None]), axis=0)
    own_losses = (top + jnp.log(summed) - jnp.sum(stats[:, 2], axis=0))[None]
    mine = lax.dynamic_index_in_dim(onehot, lax.axis_index("doc"), 0, False)
    domain_sums = lax.psum(jnp.sum(own_losses) * mine, ("seq", "doc"))
    counts = jnp.sum(onehot, axis=0) * (tokens * lax.axis_size("seq"))
    return (projected[None], own_losses, domain_sums / counts)


def solution(mesh):
    return jax.shard_map(
        on_device,
        mesh=mesh,
        in_specs=(
            P("doc", "seq", None),
            P("doc", "seq", None),
            P("doc", "seq", None),
            P("doc", None),
            P(),
            P(None, "doc"),
            P("doc", "seq"),
            P(),
        ),
        out_specs=(P("doc", "seq", None), P("doc", "seq"), P()),
        check_vma=False,
    )
```

```python
import functools

import jax
import jax.numpy as jnp
from jax import lax
from jax.experimental import pallas as pl
from jax.experimental.pallas import tpu as pltpu
from jax.sharding import PartitionSpec as P

HEADS = 16
HD = 128
DOMAINS = 7
BLOCK = 128
D = 2048
SHARD = 896
DOCS = 32
TILE = 256
NX, NY, NZ = 4, 4, 8
MESH = pl.DeviceIdType.MESH


class Place:
    def __init__(self):
        seq, doc = lax.axis_index("seq"), lax.axis_index("doc")
        self.y, self.c = lax.div(seq, 2), lax.rem(seq, 2)
        self.x, self.z = lax.div(doc, NZ), lax.rem(doc, NZ)
        self.pos = self.x * NY + self.y

    def at(self, x=None, y=None, z=None, c=None):
        x = self.x if x is None else x
        y = self.y if y is None else y
        z = self.z if z is None else z
        c = self.c if c is None else c
        return {"seq": y * 2 + c, "doc": x * NZ + z}

    def step(self, axis, by):
        if axis == "x":
            return self.at(x=lax.rem(self.x + by + NX, NX))
        if axis == "y":
            return self.at(y=lax.rem(self.y + by + NY, NY))
        return self.at(z=lax.rem(self.z + by + NZ, NZ))

    def slot(self, dx, dy):
        return lax.rem(self.x + dx + NX, NX) * NY + lax.rem(self.y + dy + NY, NY)

    def plane_peer(self, i):
        other = lax.rem(self.pos + i, NX * NY)
        return other, self.at(x=lax.div(other, NY), y=lax.rem(other, NY))

    def column_peer(self, i):
        mine = self.z * 2 + self.c
        other = lax.rem(mine + i, NZ * 2)
        return other, self.at(z=lax.div(other, 2), c=lax.rem(other, 2))


def remote(src, dst, send, recv, to):
    return pltpu.make_async_remote_copy(
        src_ref=src, dst_ref=dst, send_sem=send, recv_sem=recv, device_id=to, device_id_type=MESH
    )


def entry_barrier(here):
    barrier = pltpu.get_barrier_semaphore()

    def greet(i, _):
        pl.semaphore_signal(barrier, 1, device_id=here.plane_peer(i)[1], device_id_type=MESH)
        pl.semaphore_signal(barrier, 1, device_id=here.column_peer(i)[1], device_id_type=MESH)
        return 0

    lax.fori_loop(1, 16, greet, 0)
    pl.semaphore_wait(barrier, 30)


class VocabRing:
    def __init__(self, here, w_hbm, wv, near, send, recv, psend, precv):
        self.here, self.w, self.wv, self.near = here, w_hbm, wv, near
        self.send, self.recv, self.psend, self.precv = send, recv, psend, precv
        self.first = pl.multiple_of(here.c * (D // 2), D // 2)
        self.column = pl.multiple_of(jnp.minimum(here.y * TILE, SHARD - TILE), 128)

    def rows(self, part):
        if part == "lo":
            return pl.ds(self.first, D // 4)
        if part == "hi":
            return pl.ds(self.first + D // 4, D // 4)
        return pl.ds(self.first, D // 2)

    def slot(self, off):
        return lax.rem(self.here.z + off + NZ, NZ)

    def hop(self, k, by, at_receiver):
        part = "all" if k < 4 else ("lo" if by > 0 else "hi")
        off = -by * (k if at_receiver else k - 1)
        dst = self.wv.at[self.slot(off), self.rows(part)]
        src = self.w.at[self.rows(part), pl.ds(self.column, TILE)] if (k == 1 and not at_receiver) else dst
        n = 0 if by > 0 else 1
        return remote(src, dst, self.send.at[n, k - 1], self.recv.at[n, k - 1], self.here.step("z", by))

    def share(self, k, by, at_receiver):
        part = "all" if k < 4 else ("lo" if by > 0 else "hi")
        off = -by * k
        rows = self.rows(part)
        if at_receiver:
            start = pl.multiple_of((1 - self.here.c) * (D // 2), D // 2)
            rows = {"all": pl.ds(start, D // 2), "lo": pl.ds(start, D // 4), "hi": pl.ds(start + D // 4, D // 4)}[part]
        ref = self.wv.at[self.slot(off), rows]
        n = 0 if by > 0 else 1
        return remote(ref, ref, self.psend.at[n, k - 1], self.precv.at[n, k - 1], self.here.at(c=1 - self.here.c))

    def own(self):
        return pltpu.make_async_copy(self.w.at[:, pl.ds(self.column, TILE)], self.wv.at[self.here.z], self.near)

    def begin(self):
        for by in (1, -1):
            self.hop(1, by, False).start()
        self.own().start()

    def advance(self, k):
        for by in (1, -1):
            self.hop(k, by, True).wait_recv()
            if k < 4:
                self.hop(k + 1, by, False).start()
            self.share(k, by, False).start()

    def finish_recv(self):
        self.own().wait()
        for k in range(1, 5):
            for by in (1, -1):
                self.share(k, by, True).wait_recv()

    def finish_send(self):
        for k in range(1, 5):
            for by in (1, -1):
                self.hop(k, by, False).wait_send()
                self.share(k, by, False).wait_send()


HALF = {
    "A1+": (0, 0, "all", "A", 1),
    "A1-": (0, 0, "all", "A", -1),
    "B1+o": (0, 0, "all", "B", 1),
    "B1-o": (0, 0, "all", "B", -1),
    "A2+": (-1, 0, "lo", "A", 1),
    "A2-": (1, 0, "hi", "A", -1),
    "B1+m": (-1, 0, "all", "B", 1),
    "B1-m": (-1, 0, "all", "B", -1),
    "B1+p": (1, 0, "all", "B", 1),
    "B1-p": (1, 0, "all", "B", -1),
    "B1+l": (-2, 0, "lo", "B", 1),
    "B1-l": (-2, 0, "lo", "B", -1),
    "B1+h": (2, 0, "hi", "B", 1),
    "B1-h": (2, 0, "hi", "B", -1),
    "B2+o": (0, -1, "lo", "B", 1),
    "B2-o": (0, 1, "hi", "B", -1),
    "B2+p": (1, -1, "all", "B", 1),
    "B2-m": (-1, 1, "all", "B", -1),
    "B2+l": (-2, -1, "lo", "B", 1),
    "B2-h": (2, 1, "hi", "B", -1),
}
ORDER = list(HALF)


class PlaneGather:
    def __init__(self, here, buf, rows, send, recv):
        self.here, self.buf, self.height, self.send_sem, self.recv_sem = here, buf, rows, send, recv

    def copy(self, half, name, at_receiver):
        a, b, part, axis, by = HALF[name]
        if at_receiver:
            a, b = (a - by, b) if axis == "A" else (a, b - by)
        first, second = ("x", "y") if half == 0 else ("y", "x")
        slot = self.here.slot(a, b) if half == 0 else self.here.slot(b, a)
        unit = self.height // 4
        row, count = {"all": (0, 2 * unit), "lo": (0, unit), "hi": (unit, unit)}[part]
        ref = self.buf.at[slot, pl.ds(half * 2 * unit + row, count)]
        n = half * len(ORDER) + ORDER.index(name)
        return remote(
            ref, ref, self.send_sem.at[n], self.recv_sem.at[n], self.here.step(first if axis == "A" else second, by)
        )

    def send(self, *names):
        for name in names:
            for half in (0, 1):
                self.copy(half, name, False).start()

    def take(self, *names):
        for name in names:
            for half in (0, 1):
                self.copy(half, name, True).wait_recv()

    def begin(self):
        self.send("A1+", "A1-", "B1+o", "B1-o")

    def event(self, e):
        if e == 1:
            self.take("A1+", "A1-")
            self.send("A2+", "A2-", "B1+m", "B1-m", "B1+p", "B1-p")
        elif e == 2:
            self.take("B1+o", "B1-o")
            self.send("B2+o", "B2-o")
        elif e == 3:
            self.take("A2+", "A2-")
            self.send("B1+l", "B1-l", "B1+h", "B1-h")
        elif e == 4:
            self.take("B1+p", "B1-p", "B1+m", "B1-m")
            self.send("B2+p", "B2-m")
        elif e == 5:
            self.take("B2+o", "B2-o")
        elif e == 6:
            self.take("B1+l", "B1-l", "B1+h", "B1-h")
            self.send("B2+l", "B2-h")
        elif e == 7:
            self.take("B2+p", "B2-m")
        else:
            self.take("B2+l", "B2-h")

    def finish_send(self):
        for name in ORDER:
            for half in (0, 1):
                self.copy(half, name, False).wait_send()


SOURCES = (
    ((0, 0), (-1, 0)),
    ((1, 0), (0, -1)),
    ((0, 1), (-1, -1)),
    ((-1, 1), (1, -1)),
    ((1, 1), (2, 0)),
    ((0, 2), (2, -1)),
    ((2, 1), (-1, 2)),
    ((1, 2), (2, 2)),
)
EVENTS = ((1, 2), (3,), (4,), (), (5,), (6, 7), (), (8,))


def pick(table, i):
    value = table[0]
    for n in range(1, len(table)):
        value = jnp.where(i == n, table[n], value)
    return value


def stats_of(here, acts, wv, tcol, p1, p2):
    rows = 2 * BLOCK
    lane = lax.broadcasted_iota(jnp.int32, (rows, 128), 1)
    whole = here.y < NY - 1
    column = jnp.minimum(here.y * TILE, SHARD - TILE)
    wanted = jnp.concatenate([tcol[p1], tcol[p2]], axis=0) - lane.astype(jnp.float32)

    def tile(n, carry):
        top, total, hit = carry
        left = jnp.concatenate([acts[p1], acts[p2]], axis=0)
        logits = jnp.dot(left, wv[n], preferred_element_type=jnp.float32)
        base = ((here.x * NZ + n) * SHARD + column).astype(jnp.float32)
        one, two = logits[:, :128], logits[:, 128:]
        now = jnp.maximum(top, jnp.maximum(jnp.where(whole, one, two), two))
        add = jnp.exp(one - now)
        total = total * jnp.exp(top - now) + jnp.exp(two - now) + jnp.where(whole, add, 0.0)
        hit = hit + jnp.where(wanted == jnp.where(whole, base, -1e6), one, 0.0)
        hit = hit + jnp.where(wanted == base + 128.0, two, 0.0)
        return now, total, hit

    start = (
        jnp.full((rows, 128), -jnp.inf, jnp.float32),
        jnp.zeros((rows, 128), jnp.float32),
        jnp.zeros((rows, 128), jnp.float32),
    )
    top, total, hit = lax.fori_loop(0, NZ, tile, start)
    peak = jnp.max(top, axis=1, keepdims=True)
    total = jnp.sum(total * jnp.exp(top - peak), axis=1, keepdims=True)
    hit = jnp.sum(hit, axis=1, keepdims=True)
    return jnp.where(lane == 0, peak, jnp.where(lane == 1, total, jnp.where(lane == 2, hit, 0.0)))


def vocab_part(here, gather, ring, acts, wv, tg, tcol, out_stats, in_stats, ssend, srecv, tsend, trecv):
    def columns(slot):
        wide = jnp.broadcast_to(tg[slot].astype(jnp.float32), (BLOCK, BLOCK))
        tcol[slot] = wide.T

    def take_targets(i, _):
        slot, peer = here.plane_peer(i)
        remote(tg.at[slot], tg.at[slot], tsend.at[i], trecv.at[slot], peer).wait_recv()
        columns(slot)
        return 0

    def batch(i, _):
        for n, events in enumerate(EVENTS):
            if events or n == 0:

                @pl.when(i == n)
                def _():
                    if n == 0:
                        columns(here.pos)
                        lax.fori_loop(1, 16, take_targets, 0)
                    for e in events:
                        gather.event(e)
                    if n == 0:
                        ring.finish_recv()

        slots = []
        for half in (0, 1):
            dx = pick([pair[half][0] for pair in SOURCES], i)
            dy = pick([pair[half][1] for pair in SOURCES], i)
            slots.append(here.slot(dx, dy))
        table = stats_of(here, acts, wv, tcol, *slots)
        for half in (0, 1):
            slot = slots[half]
            out_stats[slot] = table[half * BLOCK : (half + 1) * BLOCK].T[:8]

        def give(half):
            slot = slots[half]
            to = here.at(x=lax.div(slot, NY), y=lax.rem(slot, NY))
            remote(out_stats.at[slot], in_stats.at[here.pos], ssend.at[slot], srecv.at[here.pos], to).start()

        @pl.when(i > 0)
        def _():
            give(0)

        give(1)
        return 0

    lax.fori_loop(0, len(SOURCES), batch, 0)


def losses_of(here, out_stats, in_stats, ssend, srecv):
    in_stats[here.pos] = out_stats[here.pos]

    def take(i, _):
        slot, peer = here.plane_peer(i)
        remote(out_stats.at[slot], in_stats.at[slot], ssend.at[slot], srecv.at[slot], peer).wait_recv()
        return 0

    lax.fori_loop(1, 16, take, 0)
    stats = [in_stats[n] for n in range(16)]
    top = functools.reduce(jnp.maximum, [s[0:1] for s in stats])
    total = sum(s[1:2] * jnp.exp(s[0:1] - top) for s in stats)
    hit = sum(s[2:3] for s in stats)
    return top + jnp.log(total) - hit


def domain_part(here, losses, domains, dom, dsend, drecv):
    lane = lax.broadcasted_iota(jnp.int32, (8, 128), 1)
    mine = domains[here.x * NZ + here.z]
    value = jnp.broadcast_to(jnp.sum(losses, axis=1, keepdims=True), (8, 128))
    value = jnp.where(lane == mine, value, 0.0)
    for stage in (0, 1):
        peers = here.plane_peer if stage == 0 else here.column_peer
        own = here.pos if stage == 0 else here.z * 2 + here.c
        dom[stage, own] = value

        def give(i, _):
            slot, peer = peers(i)
            remote(dom.at[stage, own], dom.at[stage, own], dsend.at[stage, i], drecv.at[stage, own], peer).start()
            return 0

        def take(i, _):
            slot, peer = peers(i)
            remote(dom.at[stage, slot], dom.at[stage, slot], dsend.at[stage, i], drecv.at[stage, slot], peer).wait_recv()
            return 0

        lax.fori_loop(1, 16, give, 0)
        lax.fori_loop(1, 16, take, 0)
        value = sum(dom[stage, n] for n in range(16))
    counts = jnp.zeros((8, 128), jnp.float32)
    for n in range(DOCS):
        counts = counts + jnp.where(lane == domains[n], 1.0, 0.0)
    return value / jnp.maximum(counts * (NY * 2 * BLOCK), 1.0)


def finish_sends(here, out_stats, in_stats, ssend, srecv, tg, tsend, trecv, dom, dsend, drecv):
    def one(i, _):
        slot, peer = here.plane_peer(i)
        remote(out_stats.at[slot], in_stats.at[slot], ssend.at[slot], srecv.at[slot], peer).wait_send()
        remote(tg.at[slot], tg.at[slot], tsend.at[i], trecv.at[slot], peer).wait_send()
        for stage in (0, 1):
            remote(dom.at[stage, slot], dom.at[stage, slot], dsend.at[stage, i], drecv.at[stage, slot], peer).wait_send()
        return 0

    lax.fori_loop(1, 16, one, 0)


def back_kernel(
    normed, targets, domains, w_hbm, loss_ref, mean_ref,
    acts, wv, tg, tcol, out_stats, in_stats, dom,
    near, gsend, grecv, rsend, rrecv, rpsend, rprecv, tsend, trecv, ssend, srecv, dsend, drecv,
):
    here = Place()
    acts[here.pos] = normed[...]
    tg[here.pos] = targets[...]
    entry_barrier(here)
    ring = VocabRing(here, w_hbm, wv, near, rsend, rrecv, rpsend, rprecv)
    gather = PlaneGather(here, acts, BLOCK, gsend, grecv)
    gather.begin()
    ring.begin()

    def give_targets(i, _):
        slot, peer = here.plane_peer(i)
        mine = tg.at[here.pos]
        remote(mine, mine, tsend.at[i], trecv.at[here.pos], peer).start()
        return 0

    lax.fori_loop(1, 16, give_targets, 0)
    for k in range(1, 5):
        ring.advance(k)
    vocab_part(here, gather, ring, acts, wv, tg, tcol, out_stats, in_stats, ssend, srecv, tsend, trecv)
    losses = losses_of(here, out_stats, in_stats, ssend, srecv)
    loss_ref[...] = losses
    mean_ref[...] = domain_part(here, losses, domains, dom, dsend, drecv)
    gather.finish_send()
    ring.finish_send()
    finish_sends(here, out_stats, in_stats, ssend, srecv, tg, tsend, trecv, dom, dsend, drecv)


def back(normed, targets, domains, w_vocab):
    vmem = pl.BlockSpec(memory_space=pltpu.VMEM)
    dma = pltpu.SemaphoreType.DMA
    return pl.pallas_call(
        back_kernel,
        out_shape=(jax.ShapeDtypeStruct((1, BLOCK), jnp.float32), jax.ShapeDtypeStruct((8, 128), jnp.float32)),
        in_specs=[vmem, vmem, pl.BlockSpec(memory_space=pltpu.SMEM), pl.BlockSpec(memory_space=pl.ANY)],
        out_specs=(vmem, vmem),
        scratch_shapes=[
            pltpu.VMEM((16, BLOCK, D), jnp.bfloat16),
            pltpu.VMEM((NZ, D, TILE), jnp.bfloat16),
            pltpu.VMEM((16, 1, BLOCK), jnp.int32),
            pltpu.VMEM((16, BLOCK, BLOCK), jnp.float32),
            pltpu.VMEM((16, 8, 128), jnp.float32),
            pltpu.VMEM((16, 8, 128), jnp.float32),
            pltpu.VMEM((2, 16, 8, 128), jnp.float32),
            dma(()),
            dma((40,)),
            dma((40,)),
            dma((2, 4)),
            dma((2, 4)),
            dma((2, 4)),
            dma((2, 4)),
            dma((16,)),
            dma((16,)),
            dma((16,)),
            dma((16,)),
            dma((2, 16)),
            dma((2, 16)),
        ],
        compiler_params=pltpu.CompilerParams(
            collective_id=0, has_side_effects=True, vmem_limit_bytes=60 * 1024 * 1024
        ),
    )(normed, targets, domains, w_vocab)


def features(inputs):
    return (1.0 + jax.nn.elu(inputs.astype(jnp.float32))).astype(jnp.bfloat16)


def attend_blocks(query_feat, key_feat, value_blk, block_states, block_keys, state_in, sum_in):
    causal = jnp.tril(jnp.ones((BLOCK, BLOCK), dtype=bool))

    def block_step(carry, inputs):
        state, key_sum = carry
        blk_query, blk_key, blk_value, blk_state, blk_keysum = inputs
        scores = jnp.einsum("thf,shf->hts", blk_query, blk_key, preferred_element_type=jnp.float32)
        probs = jnp.where(causal[None], scores, 0.0).astype(jnp.bfloat16)
        numer = jnp.einsum("hts,she->the", probs, blk_value, preferred_element_type=jnp.float32)
        numer = numer + jnp.einsum(
            "thf,hfe->the",
            blk_query,
            state.astype(jnp.bfloat16),
            preferred_element_type=jnp.float32,
        )
        denom = jnp.sum(probs, axis=2, dtype=jnp.float32).T
        denom = denom + jnp.einsum(
            "thf,hf->th", blk_query.astype(jnp.float32), key_sum, precision=lax.Precision.HIGHEST
        )
        outputs = (numer / denom[:, :, None]).astype(jnp.bfloat16)
        return ((state + blk_state, key_sum + blk_keysum), outputs)

    _, outputs = lax.scan(
        block_step, (state_in, sum_in), (query_feat, key_feat, value_blk, block_states, block_keys)
    )
    return outputs


def on_device(queries, keys, values, w_out, norm_gain, w_vocab, targets, domains):
    tokens = queries.shape[1]
    blocks = tokens // BLOCK
    width = HEADS * HD
    query_feat = features(queries[0]).reshape(blocks, BLOCK, HEADS, HD)
    key_feat = features(keys[0]).reshape(blocks, BLOCK, HEADS, HD)
    value_blk = values[0].reshape(blocks, BLOCK, HEADS, HD)
    block_states = jnp.einsum(
        "bshf,bshe->bhfe", key_feat, value_blk, preferred_element_type=jnp.float32
    )
    block_keys = jnp.sum(key_feat, axis=1, dtype=jnp.float32)
    state_local = jnp.sum(block_states, axis=0)
    sum_local = jnp.sum(block_keys, axis=0)
    seq_count, seq_mine = (lax.axis_size("seq"), lax.axis_index("seq"))
    pieces = lax.all_gather(state_local.astype(jnp.bfloat16), "seq")
    sums = lax.all_gather(sum_local, "seq")
    earlier = (jnp.arange(seq_count) < seq_mine).astype(jnp.float32)
    state_in = jnp.sum(pieces.astype(jnp.float32) * earlier[:, None, None, None], axis=0)
    sum_in = jnp.sum(sums * earlier[:, None, None], axis=0)
    attended = attend_blocks(
        query_feat, key_feat, value_blk, block_states, block_keys, state_in, sum_in
    ).reshape(tokens, width)
    projected = jnp.dot(
        attended,
        lax.all_gather(w_out, "doc", axis=0, tiled=True),
        preferred_element_type=jnp.float32,
    ).astype(jnp.bfloat16)
    wide = projected.astype(jnp.float32)
    normed = (
        wide * lax.rsqrt(jnp.mean(wide * wide, axis=-1, keepdims=True) + 1e-05) * norm_gain
    ).astype(jnp.bfloat16)
    own_losses, means = back(normed, targets, domains, w_vocab)
    return (projected[None], own_losses, means[0, :DOMAINS])


def solution(mesh):
    return jax.shard_map(
        on_device,
        mesh=mesh,
        in_specs=(
            P("doc", "seq", None),
            P("doc", "seq", None),
            P("doc", "seq", None),
            P("doc", None),
            P(),
            P(None, "doc"),
            P("doc", "seq"),
            P(),
        ),
        out_specs=(P("doc", "seq", None), P("doc", "seq"), P()),
        check_vma=False,
    )
```

```python
import functools

import jax
import jax.numpy as jnp
from jax import lax
from jax.experimental import pallas as pl
from jax.experimental.pallas import tpu as pltpu
from jax.sharding import PartitionSpec as P

HEADS = 16
HD = 128
DOMAINS = 7
BLOCK = 128
D = 2048
SHARD = 896
DOCS = 32
TILE = 256
NX, NY, NZ = 4, 4, 8
MESH = pl.DeviceIdType.MESH


class Place:
    def __init__(self):
        seq, doc = lax.axis_index("seq"), lax.axis_index("doc")
        self.y, self.c = lax.div(seq, 2), lax.rem(seq, 2)
        self.x, self.z = lax.div(doc, NZ), lax.rem(doc, NZ)
        self.pos = self.x * NY + self.y

    def at(self, x=None, y=None, z=None, c=None):
        x = self.x if x is None else x
        y = self.y if y is None else y
        z = self.z if z is None else z
        c = self.c if c is None else c
        return {"seq": y * 2 + c, "doc": x * NZ + z}

    def step(self, axis, by):
        if axis == "x":
            return self.at(x=lax.rem(self.x + by + NX, NX))
        if axis == "y":
            return self.at(y=lax.rem(self.y + by + NY, NY))
        return self.at(z=lax.rem(self.z + by + NZ, NZ))

    def slot(self, dx, dy):
        return lax.rem(self.x + dx + NX, NX) * NY + lax.rem(self.y + dy + NY, NY)

    def plane_peer(self, i):
        other = lax.rem(self.pos + i, NX * NY)
        return other, self.at(x=lax.div(other, NY), y=lax.rem(other, NY))

    def column_peer(self, i):
        mine = self.z * 2 + self.c
        other = lax.rem(mine + i, NZ * 2)
        return other, self.at(z=lax.div(other, 2), c=lax.rem(other, 2))


def remote(src, dst, send, recv, to):
    return pltpu.make_async_remote_copy(
        src_ref=src, dst_ref=dst, send_sem=send, recv_sem=recv, device_id=to, device_id_type=MESH
    )


def greet_all(here):
    barrier = pltpu.get_barrier_semaphore()

    def greet(i, _):
        pl.semaphore_signal(barrier, 1, device_id=here.plane_peer(i)[1], device_id_type=MESH)
        pl.semaphore_signal(barrier, 1, device_id=here.column_peer(i)[1], device_id_type=MESH)
        return 0

    lax.fori_loop(1, 16, greet, 0)


def await_all():
    pl.semaphore_wait(pltpu.get_barrier_semaphore(), 30)


class VocabRing:
    def __init__(self, here, w_hbm, wv, near, send, recv, psend, precv):
        self.here, self.w, self.wv, self.near = here, w_hbm, wv, near
        self.send, self.recv, self.psend, self.precv = send, recv, psend, precv
        self.first = pl.multiple_of(here.c * (D // 2), D // 2)
        self.column = pl.multiple_of(jnp.minimum(here.y * TILE, SHARD - TILE), 128)

    def rows(self, part):
        if part == "lo":
            return pl.ds(self.first, D // 4)
        if part == "hi":
            return pl.ds(self.first + D // 4, D // 4)
        return pl.ds(self.first, D // 2)

    def slot(self, off):
        return lax.rem(self.here.z + off + NZ, NZ)

    def hop(self, k, by, at_receiver):
        part = "all" if k < 4 else ("lo" if by > 0 else "hi")
        off = -by * (k if at_receiver else k - 1)
        dst = self.wv.at[self.slot(off), self.rows(part)]
        src = self.w.at[self.rows(part), pl.ds(self.column, TILE)] if (k == 1 and not at_receiver) else dst
        n = 0 if by > 0 else 1
        return remote(src, dst, self.send.at[n, k - 1], self.recv.at[n, k - 1], self.here.step("z", by))

    def share(self, k, by, at_receiver):
        part = "all" if k < 4 else ("lo" if by > 0 else "hi")
        off = -by * k
        rows = self.rows(part)
        if at_receiver:
            start = pl.multiple_of((1 - self.here.c) * (D // 2), D // 2)
            rows = {"all": pl.ds(start, D // 2), "lo": pl.ds(start, D // 4), "hi": pl.ds(start + D // 4, D // 4)}[part]
        ref = self.wv.at[self.slot(off), rows]
        n = 0 if by > 0 else 1
        return remote(ref, ref, self.psend.at[n, k - 1], self.precv.at[n, k - 1], self.here.at(c=1 - self.here.c))

    def own(self):
        return pltpu.make_async_copy(self.w.at[:, pl.ds(self.column, TILE)], self.wv.at[self.here.z], self.near)

    def begin(self):
        for by in (1, -1):
            self.hop(1, by, False).start()
        self.own().start()

    def advance(self, k):
        for by in (1, -1):
            self.hop(k, by, True).wait_recv()
            if k < 4:
                self.hop(k + 1, by, False).start()
            self.share(k, by, False).start()

    def finish_recv(self):
        self.own().wait()
        for k in range(1, 5):
            for by in (1, -1):
                self.share(k, by, True).wait_recv()

    def finish_send(self):
        for k in range(1, 5):
            for by in (1, -1):
                self.hop(k, by, False).wait_send()
                self.share(k, by, False).wait_send()


HALF = {
    "A1+": (0, 0, "all", "A", 1),
    "A1-": (0, 0, "all", "A", -1),
    "B1+o": (0, 0, "all", "B", 1),
    "B1-o": (0, 0, "all", "B", -1),
    "A2+": (-1, 0, "lo", "A", 1),
    "A2-": (1, 0, "hi", "A", -1),
    "B1+m": (-1, 0, "all", "B", 1),
    "B1-m": (-1, 0, "all", "B", -1),
    "B1+p": (1, 0, "all", "B", 1),
    "B1-p": (1, 0, "all", "B", -1),
    "B1+l": (-2, 0, "lo", "B", 1),
    "B1-l": (-2, 0, "lo", "B", -1),
    "B1+h": (2, 0, "hi", "B", 1),
    "B1-h": (2, 0, "hi", "B", -1),
    "B2+o": (0, -1, "lo", "B", 1),
    "B2-o": (0, 1, "hi", "B", -1),
    "B2+p": (1, -1, "all", "B", 1),
    "B2-m": (-1, 1, "all", "B", -1),
    "B2+l": (-2, -1, "lo", "B", 1),
    "B2-h": (2, 1, "hi", "B", -1),
}
ORDER = list(HALF)


class PlaneGather:
    def __init__(self, here, view, send, recv):
        self.here, self.view, self.send_sem, self.recv_sem = here, view, send, recv

    def copy(self, half, name, at_receiver):
        a, b, part, axis, by = HALF[name]
        if at_receiver:
            a, b = (a - by, b) if axis == "A" else (a, b - by)
        first, second = ("x", "y") if half == 0 else ("y", "x")
        dx, dy = (a, b) if half == 0 else (b, a)
        start, count = {"all": (0, 2), "lo": (0, 1), "hi": (1, 1)}[part]
        column, row = lax.rem(self.here.x + dx + NX, NX), lax.rem(self.here.y + dy + NY, NY)
        ref = self.view(column, row, half * 2 + start, count)
        n = half * len(ORDER) + ORDER.index(name)
        return remote(
            ref, ref, self.send_sem.at[n], self.recv_sem.at[n], self.here.step(first if axis == "A" else second, by)
        )

    def begin_along(self, axis):
        half = 0 if axis == "x" else 1
        for name in ("A1+", "A1-"):
            self.copy(half, name, False).start()
        for name in ("B1+o", "B1-o"):
            self.copy(1 - half, name, False).start()

    def send(self, *names):
        for name in names:
            for half in (0, 1):
                self.copy(half, name, False).start()

    def take(self, *names):
        for name in names:
            for half in (0, 1):
                self.copy(half, name, True).wait_recv()

    def begin(self):
        self.send("A1+", "A1-", "B1+o", "B1-o")

    def event(self, e):
        if e == 1:
            self.take("A1+", "A1-")
            self.send("A2+", "A2-", "B1+m", "B1-m", "B1+p", "B1-p")
        elif e == 2:
            self.take("B1+o", "B1-o")
            self.send("B2+o", "B2-o")
        elif e == 3:
            self.take("A2+", "A2-")
            self.send("B1+l", "B1-l", "B1+h", "B1-h")
        elif e == 4:
            self.take("B1+p", "B1-p", "B1+m", "B1-m")
            self.send("B2+p", "B2-m")
        elif e == 5:
            self.take("B2+o", "B2-o")
        elif e == 6:
            self.take("B1+l", "B1-l", "B1+h", "B1-h")
            self.send("B2+l", "B2-h")
        elif e == 7:
            self.take("B2+p", "B2-m")
        else:
            self.take("B2+l", "B2-h")

    def finish_send(self):
        for name in ORDER:
            for half in (0, 1):
                self.copy(half, name, False).wait_send()


SOURCES = (
    ((0, 0), (-1, 0)),
    ((1, 0), (0, -1)),
    ((0, 1), (-1, -1)),
    ((-1, 1), (1, -1)),
    ((1, 1), (2, 0)),
    ((0, 2), (2, -1)),
    ((2, 1), (-1, 2)),
    ((1, 2), (2, 2)),
)
EVENTS = ((), (3,), (4,), (), (5,), (6, 7), (), (8,))


def pick(table, i):
    value = table[0]
    for n in range(1, len(table)):
        value = jnp.where(i == n, table[n], value)
    return value


def stats_of(here, acts, wv, tcol, p1, p2):
    rows = 2 * BLOCK
    lane = lax.broadcasted_iota(jnp.int32, (rows, 128), 1)
    whole = here.y < NY - 1
    column = jnp.minimum(here.y * TILE, SHARD - TILE)
    wanted = jnp.concatenate([tcol[p1], tcol[p2]], axis=0) - lane.astype(jnp.float32)

    def tile(n, carry):
        top, total, hit = carry
        left = jnp.concatenate([acts[p1], acts[p2]], axis=0)
        logits = jnp.dot(left, wv[n], preferred_element_type=jnp.float32)
        base = ((here.x * NZ + n) * SHARD + column).astype(jnp.float32)
        one, two = logits[:, :128], logits[:, 128:]
        now = jnp.maximum(top, jnp.maximum(jnp.where(whole, one, two), two))
        add = jnp.exp(one - now)
        total = total * jnp.exp(top - now) + jnp.exp(two - now) + jnp.where(whole, add, 0.0)
        hit = hit + jnp.where(wanted == jnp.where(whole, base, -1e6), one, 0.0)
        hit = hit + jnp.where(wanted == base + 128.0, two, 0.0)
        return now, total, hit

    start = (
        jnp.full((rows, 128), -jnp.inf, jnp.float32),
        jnp.zeros((rows, 128), jnp.float32),
        jnp.zeros((rows, 128), jnp.float32),
    )
    top, total, hit = lax.fori_loop(0, NZ, tile, start)
    peak = jnp.max(top, axis=1, keepdims=True)
    total = jnp.sum(total * jnp.exp(top - peak), axis=1, keepdims=True)
    hit = jnp.sum(hit, axis=1, keepdims=True)
    return jnp.where(lane == 0, peak, jnp.where(lane == 1, total, jnp.where(lane == 2, hit, 0.0)))


def vocab_part(here, gather, acts, wv, tg, tcol, out_stats, in_stats, ssend, srecv, tsend, trecv):
    def columns(slot):
        wide = jnp.broadcast_to(tg[slot].astype(jnp.float32), (BLOCK, BLOCK))
        tcol[slot] = wide.T

    def take_targets(i, _):
        slot, peer = here.plane_peer(i)
        remote(tg.at[slot], tg.at[slot], tsend.at[i], trecv.at[slot], peer).wait_recv()
        columns(slot)
        return 0

    columns(here.pos)
    lax.fori_loop(1, 16, take_targets, 0)

    def batch(i, _):
        for n, events in enumerate(EVENTS):
            if events:

                @pl.when(i == n)
                def _():
                    for e in events:
                        gather.event(e)

        slots = []
        for half in (0, 1):
            dx = pick([pair[half][0] for pair in SOURCES], i)
            dy = pick([pair[half][1] for pair in SOURCES], i)
            slots.append(here.slot(dx, dy))
        table = stats_of(here, acts, wv, tcol, *slots)
        for half in (0, 1):
            slot = slots[half]
            out_stats[slot] = table[half * BLOCK : (half + 1) * BLOCK].T[:8]

        def give(half):
            slot = slots[half]
            to = here.at(x=lax.div(slot, NY), y=lax.rem(slot, NY))
            remote(out_stats.at[slot], in_stats.at[here.pos], ssend.at[slot], srecv.at[here.pos], to).start()

        @pl.when(i > 0)
        def _():
            give(0)

        give(1)
        return 0

    lax.fori_loop(0, len(SOURCES), batch, 0)


def losses_of(here, out_stats, in_stats, ssend, srecv):
    in_stats[here.pos] = out_stats[here.pos]

    def take(i, _):
        slot, peer = here.plane_peer(i)
        remote(out_stats.at[slot], in_stats.at[slot], ssend.at[slot], srecv.at[slot], peer).wait_recv()
        return 0

    lax.fori_loop(1, 16, take, 0)
    stats = [in_stats[n] for n in range(16)]
    top = functools.reduce(jnp.maximum, [s[0:1] for s in stats])
    total = sum(s[1:2] * jnp.exp(s[0:1] - top) for s in stats)
    hit = sum(s[2:3] for s in stats)
    return top + jnp.log(total) - hit


def domain_part(here, losses, domains, dom, dsend, drecv):
    lane = lax.broadcasted_iota(jnp.int32, (8, 128), 1)
    mine = domains[here.x * NZ + here.z]
    value = jnp.broadcast_to(jnp.sum(losses, axis=1, keepdims=True), (8, 128))
    value = jnp.where(lane == mine, value, 0.0)
    for stage in (0, 1):
        peers = here.plane_peer if stage == 0 else here.column_peer
        own = here.pos if stage == 0 else here.z * 2 + here.c
        dom[stage, own] = value

        def give(i, _):
            slot, peer = peers(i)
            remote(dom.at[stage, own], dom.at[stage, own], dsend.at[stage, i], drecv.at[stage, own], peer).start()
            return 0

        def take(i, _):
            slot, peer = peers(i)
            remote(dom.at[stage, slot], dom.at[stage, slot], dsend.at[stage, i], drecv.at[stage, slot], peer).wait_recv()
            return 0

        lax.fori_loop(1, 16, give, 0)
        lax.fori_loop(1, 16, take, 0)
        value = sum(dom[stage, n] for n in range(16))
    counts = jnp.zeros((8, 128), jnp.float32)
    for n in range(DOCS):
        counts = counts + jnp.where(lane == domains[n], 1.0, 0.0)
    return value / jnp.maximum(counts * (NY * 2 * BLOCK), 1.0)


def finish_sends(here, out_stats, in_stats, ssend, srecv, tg, tsend, trecv, dom, dsend, drecv):
    def one(i, _):
        slot, peer = here.plane_peer(i)
        remote(out_stats.at[slot], in_stats.at[slot], ssend.at[slot], srecv.at[slot], peer).wait_send()
        remote(tg.at[slot], tg.at[slot], tsend.at[i], trecv.at[slot], peer).wait_send()
        for stage in (0, 1):
            remote(dom.at[stage, slot], dom.at[stage, slot], dsend.at[stage, i], drecv.at[stage, slot], peer).wait_send()
        return 0

    lax.fori_loop(1, 16, one, 0)


HALF_HEADS = HEADS // 2
CHUNKS = 4
PER = HALF_HEADS // CHUNKS


def feature(inputs):
    wide = inputs.astype(jnp.float32)
    return jnp.where(wide > 0.0, wide + 1.0, jnp.exp(jnp.minimum(wide, 0.0))).astype(jnp.bfloat16)


def head_slice(h):
    return pl.ds(pl.multiple_of(h * HD, HD), HD)


def local_states(keys, values, kf, state, sums):
    def one(h, _):
        cols = head_slice(h)
        feat = feature(keys[:, cols])
        kf[:, cols] = feat
        group, n = lax.div(h, HALF_HEADS), lax.rem(h, HALF_HEADS)
        state[group, n] = lax.dot_general(
            feat, values[:, cols], (((0,), (0,)), ((), ())), preferred_element_type=jnp.float32
        )
        sums[group, n] = jnp.sum(feat.astype(jnp.float32), axis=0, keepdims=True)
        return 0

    lax.fori_loop(0, HEADS, one, 0)


def inner_blocks(queries, kf, values, qf, probs, numer):
    row = lax.broadcasted_iota(jnp.int32, (BLOCK, BLOCK), 0)
    causal = row >= lax.broadcasted_iota(jnp.int32, (BLOCK, BLOCK), 1)

    def one(h, _):
        cols = head_slice(h)
        feat = feature(queries[:, cols])
        qf[:, cols] = feat
        scores = lax.dot_general(feat, kf[:, cols], (((1,), (1,)), ((), ())), preferred_element_type=jnp.float32)
        prob = jnp.where(causal, scores, 0.0).astype(jnp.bfloat16)
        probs[h] = prob
        numer[:, cols] = jnp.dot(prob, values[:, cols], preferred_element_type=jnp.float32)
        return 0

    lax.fori_loop(0, HEADS, one, 0)


def outer_blocks(first, qf, probs, numer, state_in, sum_in, out):
    def one(n, _):
        h = first + n
        cols = head_slice(h)
        group, n = lax.div(h, HALF_HEADS), lax.rem(h, HALF_HEADS)
        feat = qf[:, cols]
        top = numer[:, cols] + jnp.dot(feat, state_in[group, n], preferred_element_type=jnp.float32)
        below = probs[h].astype(jnp.float32) + feat.astype(jnp.float32) * sum_in[group, n]
        out[:, cols] = (top / jnp.sum(below, axis=1, keepdims=True)).astype(jnp.bfloat16)
        return 0

    lax.fori_loop(0, HALF_HEADS, one, 0)


class Prefix:
    def __init__(self, here, refs, sems):
        self.here = here
        (self.state, self.sums, self.part, self.ksum, self.cin, self.kin, self.cout, self.kout,
         self.stage, self.kstage, self.state_in, self.sum_in) = refs
        (self.xsend, self.xrecv, self.csend, self.crecv, self.fsend, self.frecv) = sems
        self.partner = here.at(c=1 - here.c)
        self.up = here.step("y", 1)

    def exchange(self):
        other = 1 - self.here.c
        return (
            remote(self.state.at[other], self.part, self.xsend.at[0], self.xrecv.at[0], self.partner),
            remote(self.sums.at[other], self.ksum, self.xsend.at[1], self.xrecv.at[1], self.partner),
        )

    def climb(self, j):
        heads = pl.ds(j * PER, PER)
        copies = [remote(self.cout.at[heads], self.cin.at[heads], self.csend.at[j], self.crecv.at[j], self.up)]
        if j == 0:
            copies.append(remote(self.kout, self.kin, self.csend.at[CHUNKS], self.crecv.at[CHUNKS], self.up))
        return copies

    def give(self, j):
        heads = pl.ds(j * PER, PER)
        there = self.state_in.at[self.here.c, heads]
        copies = [remote(self.stage.at[heads], there, self.fsend.at[j], self.frecv.at[j], self.partner)]
        if j == 0:
            copies.append(
                remote(self.kstage, self.sum_in.at[self.here.c], self.fsend.at[CHUNKS], self.frecv.at[CHUNKS], self.partner)
            )
        return copies

    def chunk(self, j):
        here = self.here

        @pl.when(here.y > 0)
        def _():
            for copy in self.climb(j):
                copy.wait_recv()

        second = (here.c == 1).astype(jnp.float32)
        heads = pl.ds(j * PER, PER)
        before = self.cin[heads].astype(jnp.float32)
        own, other = self.state[here.c, heads], self.part[heads]
        self.cout[heads] = (before + (own + other)).astype(jnp.bfloat16)
        if j == 0:
            kbefore, kown, kother = self.kin[...], self.sums[here.c], self.ksum[...]
            self.kout[...] = kbefore + (kown + kother)

        @pl.when(here.y < NY - 1)
        def _():
            for copy in self.climb(j):
                copy.start()

        self.stage[heads] = (before + own * (1.0 - second)).astype(jnp.bfloat16)
        self.state_in[here.c, heads] = (before + other * second).astype(jnp.bfloat16)
        if j == 0:
            self.kstage[...] = kbefore + kown * (1.0 - second)
            self.sum_in[here.c] = kbefore + kother * second
        for copy in self.give(j):
            copy.start()

    def take(self):
        for j in range(CHUNKS):
            heads = pl.ds(j * PER, PER)
            other = 1 - self.here.c
            remote(
                self.stage.at[heads], self.state_in.at[other, heads], self.fsend.at[j], self.frecv.at[j], self.partner
            ).wait_recv()
        remote(
            self.kstage, self.sum_in.at[other], self.fsend.at[CHUNKS], self.frecv.at[CHUNKS], self.partner
        ).wait_recv()

    def finish_send(self):
        for copy in self.exchange():
            copy.wait_send()
        for j in range(CHUNKS):
            for copy in self.give(j):
                copy.wait_send()

            @pl.when(self.here.y < NY - 1)
            def _():
                for copy in self.climb(j):
                    copy.wait_send()


def normalise(projected, gain, out):
    def rows(r, _):
        some = pl.ds(pl.multiple_of(r * 16, 16), 16)
        wide = projected[some].astype(jnp.float32)
        scale = lax.rsqrt(jnp.mean(wide * wide, axis=1, keepdims=True) + 1e-05)
        out[some] = (wide * scale * gain[...]).astype(jnp.bfloat16)
        return 0

    lax.fori_loop(0, BLOCK // 16, rows, 0)


def whole_kernel(
    queries, keys, values, gain, targets, domains, wo_hbm, w_hbm, projected, loss_ref, mean_ref,
    qf, kf, probs, numer, state, sums, part, ksum, cin, kin, cout, kout, stage, kstage, state_in, sum_in,
    attended, wo, halves, given, acts, wv, tg, tcol, out_stats, in_stats, dom,
    near, xsend, xrecv, csend, crecv, fsend, frecv, zsend, zrecv, hsend, hrecv, psend, precv,
    gsend, grecv, rsend, rrecv, rpsend, rprecv, tsend, trecv, ssend, srecv, dsend, drecv,
):
    here = Place()
    cin[...] = jnp.zeros_like(cin)
    kin[...] = jnp.zeros_like(kin)
    greet_all(here)
    partner = here.at(c=1 - here.c)
    half = D // 2
    wo_rows = pl.ds(pl.multiple_of(here.y * 16, 16), 16)
    wo_own = wo_hbm.at[wo_rows, pl.ds(pl.multiple_of(here.c * half, half), half)]
    wo_place = wo.at[here.x, here.z, here.y]
    own_wo = pltpu.make_async_copy(wo_own, wo_place, near.at[1])
    own_wo.start()
    tg[here.pos] = targets[...]
    local_states(keys, values, kf, state, sums)
    await_all()

    def wo_peer(i):
        z = lax.rem(here.z + i, NZ)
        return z, here.at(z=z)

    def wo_give(i, _):
        z, to = wo_peer(i)
        remote(wo_own, wo_place, zsend.at[i], zrecv.at[here.z], to).start()
        return 0

    def wo_take(i, _):
        z, to = wo_peer(i)
        place = wo.at[here.x, z, here.y]
        remote(place, place, zsend.at[i], zrecv.at[z], to).wait_recv()
        return 0

    def wo_sent(i, _):
        z, to = wo_peer(i)
        remote(wo_own, wo_place, zsend.at[i], zrecv.at[here.z], to).wait_send()
        return 0

    lax.fori_loop(1, NZ, wo_give, 0)
    prefix = Prefix(
        here,
        (state, sums, part, ksum, cin, kin, cout, kout, stage, kstage, state_in, sum_in),
        (xsend, xrecv, csend, crecv, fsend, frecv),
    )
    for copy in prefix.exchange():
        copy.start()
    ring = VocabRing(here, w_hbm, wv, near.at[0], rsend, rrecv, rpsend, rprecv)
    ring.begin()

    def give_targets(i, _):
        slot, peer = here.plane_peer(i)
        mine = tg.at[here.pos]
        remote(mine, mine, tsend.at[i], trecv.at[here.pos], peer).start()
        return 0

    lax.fori_loop(1, 16, give_targets, 0)
    for copy in prefix.exchange():
        copy.wait_recv()

    @pl.when(here.y == 0)
    def _():
        for j in range(CHUNKS):
            prefix.chunk(j)

    inner_blocks(queries, kf, values, qf, probs, numer)
    own_wo.wait()
    lax.fori_loop(1, NZ, wo_take, 0)
    weights = PlaneGather(here, lambda x, y, start, count: wo.at[x, pl.ds(start * 2, count * 2), y], psend, precv)
    weights.begin_along("x")

    @pl.when(here.y > 0)
    def _():
        for j in range(CHUNKS):
            prefix.chunk(j)

    weights.begin_along("y")
    weights.event(1)
    prefix.take()
    mine = attended.at[here.c]
    outer_blocks(0, qf, probs, numer, state_in, sum_in, mine)
    weights.event(2)
    weights.event(3)
    outer_blocks(HALF_HEADS, qf, probs, numer, state_in, sum_in, mine)
    rows_over = remote(mine, mine, hsend.at[0], hrecv.at[0], partner)
    rows_over.start()
    ring.advance(1)
    weights.event(4)
    weights.event(5)
    weights.event(6)
    weights.event(7)
    theirs = attended.at[1 - here.c]
    remote(theirs, theirs, hsend.at[0], hrecv.at[0], partner).wait_recv()
    weights.event(8)

    def project(n, _):
        cols = pl.ds(pl.multiple_of(n * TILE, TILE), TILE)
        rows = jnp.concatenate([attended[0], attended[1]], axis=0)
        w = wo[:, :, :, :, cols].reshape(D, TILE)
        both = jnp.dot(rows, w, preferred_element_type=jnp.float32).astype(jnp.bfloat16)
        low = here.c == 0
        halves[here.c, :, cols] = jnp.where(low, both[:BLOCK], both[BLOCK:])
        given[:, cols] = jnp.where(low, both[BLOCK:], both[:BLOCK])
        return 0

    lax.fori_loop(0, half // TILE, project, 0)
    back = remote(given, halves.at[here.c], hsend.at[1], hrecv.at[1], partner)
    back.start()
    other = halves.at[1 - here.c]
    remote(given, other, hsend.at[1], hrecv.at[1], partner).wait_recv()
    projected[:, :half] = halves[0]
    projected[:, half:] = halves[1]
    normalise(projected, gain, acts.at[here.pos])
    unit = BLOCK // 4
    gather = PlaneGather(
        here, lambda x, y, start, count: acts.at[x * NY + y, pl.ds(start * unit, count * unit)], gsend, grecv
    )
    gather.begin()
    ring.advance(2)
    gather.event(1)
    gather.event(2)
    ring.advance(3)
    ring.advance(4)
    ring.finish_recv()
    vocab_part(here, gather, acts, wv, tg, tcol, out_stats, in_stats, ssend, srecv, tsend, trecv)
    losses = losses_of(here, out_stats, in_stats, ssend, srecv)
    loss_ref[...] = losses
    mean_ref[...] = domain_part(here, losses, domains, dom, dsend, drecv)
    lax.fori_loop(1, NZ, wo_sent, 0)
    prefix.finish_send()
    weights.finish_send()
    rows_over.wait_send()
    back.wait_send()
    gather.finish_send()
    ring.finish_send()
    finish_sends(here, out_stats, in_stats, ssend, srecv, tg, tsend, trecv, dom, dsend, drecv)


def on_device(queries, keys, values, w_out, norm_gain, w_vocab, targets, domains):
    vmem = pl.BlockSpec(memory_space=pltpu.VMEM)
    dma = pltpu.SemaphoreType.DMA
    low, wide = jnp.bfloat16, jnp.float32
    projected, losses, means = pl.pallas_call(
        whole_kernel,
        out_shape=(
            jax.ShapeDtypeStruct((BLOCK, D), low),
            jax.ShapeDtypeStruct((1, BLOCK), wide),
            jax.ShapeDtypeStruct((8, 128), wide),
        ),
        in_specs=[vmem] * 5
        + [pl.BlockSpec(memory_space=pltpu.SMEM), pl.BlockSpec(memory_space=pl.ANY), pl.BlockSpec(memory_space=pl.ANY)],
        out_specs=(vmem, vmem, vmem),
        scratch_shapes=[
            pltpu.VMEM((BLOCK, D), low),
            pltpu.VMEM((BLOCK, D), low),
            pltpu.VMEM((HEADS, BLOCK, BLOCK), low),
            pltpu.VMEM((BLOCK, D), wide),
            pltpu.VMEM((2, HALF_HEADS, HD, HD), wide),
            pltpu.VMEM((2, HALF_HEADS, 1, HD), wide),
            pltpu.VMEM((HALF_HEADS, HD, HD), wide),
            pltpu.VMEM((HALF_HEADS, 1, HD), wide),
            pltpu.VMEM((HALF_HEADS, HD, HD), low),
            pltpu.VMEM((HALF_HEADS, 1, HD), wide),
            pltpu.VMEM((HALF_HEADS, HD, HD), low),
            pltpu.VMEM((HALF_HEADS, 1, HD), wide),
            pltpu.VMEM((HALF_HEADS, HD, HD), low),
            pltpu.VMEM((HALF_HEADS, 1, HD), wide),
            pltpu.VMEM((2, HALF_HEADS, HD, HD), low),
            pltpu.VMEM((2, HALF_HEADS, 1, HD), wide),
            pltpu.VMEM((2, BLOCK, D), low),
            pltpu.VMEM((NX, NZ, NY, 16, D // 2), low),
            pltpu.VMEM((2, BLOCK, D // 2), low),
            pltpu.VMEM((BLOCK, D // 2), low),
            pltpu.VMEM((16, BLOCK, D), low),
            pltpu.VMEM((NZ, D, TILE), low),
            pltpu.VMEM((16, 1, BLOCK), jnp.int32),
            pltpu.VMEM((16, BLOCK, BLOCK), wide),
            pltpu.VMEM((16, 8, 128), wide),
            pltpu.VMEM((16, 8, 128), wide),
            pltpu.VMEM((2, 16, 8, 128), wide),
            dma((2,)),
            dma((2,)),
            dma((2,)),
            dma((CHUNKS + 1,)),
            dma((CHUNKS + 1,)),
            dma((CHUNKS + 1,)),
            dma((CHUNKS + 1,)),
            dma((NZ,)),
            dma((NZ,)),
            dma((2,)),
            dma((2,)),
            dma((40,)),
            dma((40,)),
            dma((40,)),
            dma((40,)),
            dma((2, 4)),
            dma((2, 4)),
            dma((2, 4)),
            dma((2, 4)),
            dma((16,)),
            dma((16,)),
            dma((16,)),
            dma((16,)),
            dma((2, 16)),
            dma((2, 16)),
        ],
        compiler_params=pltpu.CompilerParams(
            collective_id=0, has_side_effects=True, vmem_limit_bytes=60 * 1024 * 1024
        ),
    )(queries[0], keys[0], values[0], norm_gain[None], targets, domains, w_out, w_vocab)
    return (projected[None], losses, means[0, :DOMAINS])


def solution(mesh):
    return jax.shard_map(
        on_device,
        mesh=mesh,
        in_specs=(
            P("doc", "seq", None),
            P("doc", "seq", None),
            P("doc", "seq", None),
            P("doc", None),
            P(),
            P(None, "doc"),
            P("doc", "seq"),
            P(),
        ),
        out_specs=(P("doc", "seq", None), P("doc", "seq"), P()),
        check_vma=False,
    )
```

```python
import functools

import jax
import jax.numpy as jnp
from jax import lax
from jax.experimental import pallas as pl
from jax.experimental.pallas import tpu as pltpu
from jax.sharding import PartitionSpec as P

HEADS = 16
HD = 128
DOMAINS = 7
BLOCK = 128
D = 2048
SHARD = 896
DOCS = 32
TILE = 256
NX, NY, NZ = 4, 4, 8
MESH = pl.DeviceIdType.MESH


class Place:
    def __init__(self):
        seq, doc = lax.axis_index("seq"), lax.axis_index("doc")
        self.y, self.c = lax.div(seq, 2), lax.rem(seq, 2)
        self.x, self.z = lax.div(doc, NZ), lax.rem(doc, NZ)
        self.pos = self.x * NY + self.y

    def at(self, x=None, y=None, z=None, c=None):
        x = self.x if x is None else x
        y = self.y if y is None else y
        z = self.z if z is None else z
        c = self.c if c is None else c
        return {"seq": y * 2 + c, "doc": x * NZ + z}

    def step(self, axis, by):
        if axis == "x":
            return self.at(x=lax.rem(self.x + by + NX, NX))
        if axis == "y":
            return self.at(y=lax.rem(self.y + by + NY, NY))
        return self.at(z=lax.rem(self.z + by + NZ, NZ))

    def slot(self, dx, dy):
        return lax.rem(self.x + dx + NX, NX) * NY + lax.rem(self.y + dy + NY, NY)

    def plane_peer(self, i):
        other = lax.rem(self.pos + i, NX * NY)
        return other, self.at(x=lax.div(other, NY), y=lax.rem(other, NY))

    def column_peer(self, i):
        mine = self.z * 2 + self.c
        other = lax.rem(mine + i, NZ * 2)
        return other, self.at(z=lax.div(other, 2), c=lax.rem(other, 2))


def remote(src, dst, send, recv, to):
    return pltpu.make_async_remote_copy(
        src_ref=src, dst_ref=dst, send_sem=send, recv_sem=recv, device_id=to, device_id_type=MESH
    )


def greet_all(here):
    barrier = pltpu.get_barrier_semaphore()

    def greet(i, _):
        pl.semaphore_signal(barrier, 1, device_id=here.plane_peer(i)[1], device_id_type=MESH)
        pl.semaphore_signal(barrier, 1, device_id=here.column_peer(i)[1], device_id_type=MESH)
        return 0

    lax.fori_loop(1, 16, greet, 0)


def await_all():
    pl.semaphore_wait(pltpu.get_barrier_semaphore(), 30)


class VocabRing:
    def __init__(self, here, w_hbm, wv, near, send, recv, psend, precv):
        self.here, self.w, self.wv, self.near = here, w_hbm, wv, near
        self.send, self.recv, self.psend, self.precv = send, recv, psend, precv
        self.first = pl.multiple_of(here.c * (D // 2), D // 2)
        self.column = pl.multiple_of(jnp.minimum(here.y * TILE, SHARD - TILE), 128)

    def rows(self, part):
        if part == "lo":
            return pl.ds(self.first, D // 4)
        if part == "hi":
            return pl.ds(self.first + D // 4, D // 4)
        return pl.ds(self.first, D // 2)

    def slot(self, off):
        return lax.rem(self.here.z + off + NZ, NZ)

    def hop(self, k, by, at_receiver):
        part = "all" if k < 4 else ("lo" if by > 0 else "hi")
        off = -by * (k if at_receiver else k - 1)
        dst = self.wv.at[self.slot(off), self.rows(part)]
        src = self.w.at[self.rows(part), pl.ds(self.column, TILE)] if (k == 1 and not at_receiver) else dst
        n = 0 if by > 0 else 1
        return remote(src, dst, self.send.at[n, k - 1], self.recv.at[n, k - 1], self.here.step("z", by))

    def share(self, k, by, at_receiver):
        part = "all" if k < 4 else ("lo" if by > 0 else "hi")
        off = -by * k
        rows = self.rows(part)
        if at_receiver:
            start = pl.multiple_of((1 - self.here.c) * (D // 2), D // 2)
            rows = {"all": pl.ds(start, D // 2), "lo": pl.ds(start, D // 4), "hi": pl.ds(start + D // 4, D // 4)}[part]
        ref = self.wv.at[self.slot(off), rows]
        n = 0 if by > 0 else 1
        return remote(ref, ref, self.psend.at[n, k - 1], self.precv.at[n, k - 1], self.here.at(c=1 - self.here.c))

    def own(self):
        return pltpu.make_async_copy(self.w.at[:, pl.ds(self.column, TILE)], self.wv.at[self.here.z], self.near)

    def begin(self):
        for by in (1, -1):
            self.hop(1, by, False).start()
        self.own().start()

    def advance(self, k):
        for by in (1, -1):
            self.hop(k, by, True).wait_recv()
            if k < 4:
                self.hop(k + 1, by, False).start()
            self.share(k, by, False).start()

    def finish_recv(self):
        self.own().wait()
        for k in range(1, 5):
            for by in (1, -1):
                self.share(k, by, True).wait_recv()

    def finish_send(self):
        for k in range(1, 5):
            for by in (1, -1):
                self.hop(k, by, False).wait_send()
                self.share(k, by, False).wait_send()


HALF = {
    "A1+": (0, 0, "all", "A", 1),
    "A1-": (0, 0, "all", "A", -1),
    "B1+o": (0, 0, "all", "B", 1),
    "B1-o": (0, 0, "all", "B", -1),
    "A2+": (-1, 0, "lo", "A", 1),
    "A2-": (1, 0, "hi", "A", -1),
    "B1+m": (-1, 0, "all", "B", 1),
    "B1-m": (-1, 0, "all", "B", -1),
    "B1+p": (1, 0, "all", "B", 1),
    "B1-p": (1, 0, "all", "B", -1),
    "B1+l": (-2, 0, "lo", "B", 1),
    "B1-l": (-2, 0, "lo", "B", -1),
    "B1+h": (2, 0, "hi", "B", 1),
    "B1-h": (2, 0, "hi", "B", -1),
    "B2+o": (0, -1, "lo", "B", 1),
    "B2-o": (0, 1, "hi", "B", -1),
    "B2+p": (1, -1, "all", "B", 1),
    "B2-m": (-1, 1, "all", "B", -1),
    "B2+l": (-2, -1, "lo", "B", 1),
    "B2-h": (2, 1, "hi", "B", -1),
}
ORDER = list(HALF)
WO_CUTS = ((0, 1, 3), (3, 5, 8))
ROW_CUTS = ((0, 32, 64), (64, 96, 128))


class PlaneGather:
    def __init__(self, here, view, cuts, send, recv):
        self.here, self.view, self.cuts, self.send_sem, self.recv_sem = here, view, cuts, send, recv

    def copy(self, half, name, at_receiver):
        a, b, part, axis, by = HALF[name]
        if at_receiver:
            a, b = (a - by, b) if axis == "A" else (a, b - by)
        first, second = ("x", "y") if half == 0 else ("y", "x")
        dx, dy = (a, b) if half == 0 else (b, a)
        first_row, middle, last_row = self.cuts[half]
        start, stop = {"all": (first_row, last_row), "lo": (first_row, middle), "hi": (middle, last_row)}[part]
        column, row = lax.rem(self.here.x + dx + NX, NX), lax.rem(self.here.y + dy + NY, NY)
        ref = self.view(column, row, start, stop - start)
        n = half * len(ORDER) + ORDER.index(name)
        return remote(
            ref, ref, self.send_sem.at[n], self.recv_sem.at[n], self.here.step(first if axis == "A" else second, by)
        )

    def begin_along(self, axis):
        half = 0 if axis == "x" else 1
        for name in ("A1+", "A1-"):
            self.copy(half, name, False).start()
        for name in ("B1+o", "B1-o"):
            self.copy(1 - half, name, False).start()

    def send(self, halves, *names):
        for name in names:
            for half in halves:
                self.copy(half, name, False).start()

    def take(self, halves, *names):
        for name in names:
            for half in halves:
                self.copy(half, name, True).wait_recv()

    def begin(self):
        self.send((0, 1), "A1+", "A1-", "B1+o", "B1-o")

    def event(self, e, halves=(0, 1)):
        if e == 1:
            self.take(halves, "A1+", "A1-")
            self.send(halves, "A2+", "A2-", "B1+m", "B1-m", "B1+p", "B1-p")
        elif e == 2:
            self.take(halves, "B1+o", "B1-o")
            self.send(halves, "B2+o", "B2-o")
        elif e == 3:
            self.take(halves, "A2+", "A2-")
            self.send(halves, "B1+l", "B1-l", "B1+h", "B1-h")
        elif e == 4:
            self.take(halves, "B1+p", "B1-p", "B1+m", "B1-m")
            self.send(halves, "B2+p", "B2-m")
        elif e == 5:
            self.take(halves, "B2+o", "B2-o")
        elif e == 6:
            self.take(halves, "B1+l", "B1-l", "B1+h", "B1-h")
            self.send(halves, "B2+l", "B2-h")
        elif e == 7:
            self.take(halves, "B2+p", "B2-m")
        else:
            self.take(halves, "B2+l", "B2-h")

    def finish_send(self):
        for name in ORDER:
            for half in (0, 1):
                self.copy(half, name, False).wait_send()


SOURCES = (
    ((0, 0), (-1, 0)),
    ((1, 0), (0, -1)),
    ((0, 1), (-1, -1)),
    ((-1, 1), (1, -1)),
    ((1, 1), (2, 0)),
    ((0, 2), (2, -1)),
    ((2, 1), (-1, 2)),
    ((1, 2), (2, 2)),
)
EVENTS = ((), (3,), (4,), (), (5,), (6, 7), (), (8,))


def pick(table, i):
    value = table[0]
    for n in range(1, len(table)):
        value = jnp.where(i == n, table[n], value)
    return value


def stats_of(here, acts, wv, tcol, p1, p2):
    rows = 2 * BLOCK
    lane = lax.broadcasted_iota(jnp.int32, (rows, 128), 1)
    whole = here.y < NY - 1
    column = jnp.minimum(here.y * TILE, SHARD - TILE)
    wanted = jnp.concatenate([tcol[p1], tcol[p2]], axis=0) - lane.astype(jnp.float32)

    def tile(n, carry):
        top, total, hit = carry
        left = jnp.concatenate([acts[p1], acts[p2]], axis=0)
        logits = jnp.dot(left, wv[n], preferred_element_type=jnp.float32)
        base = ((here.x * NZ + n) * SHARD + column).astype(jnp.float32)
        one, two = logits[:, :128], logits[:, 128:]
        now = jnp.maximum(top, jnp.maximum(jnp.where(whole, one, two), two))
        add = jnp.exp(one - now)
        total = total * jnp.exp(top - now) + jnp.exp(two - now) + jnp.where(whole, add, 0.0)
        hit = hit + jnp.where(wanted == jnp.where(whole, base, -1e6), one, 0.0)
        hit = hit + jnp.where(wanted == base + 128.0, two, 0.0)
        return now, total, hit

    start = (
        jnp.full((rows, 128), -jnp.inf, jnp.float32),
        jnp.zeros((rows, 128), jnp.float32),
        jnp.zeros((rows, 128), jnp.float32),
    )
    top, total, hit = lax.fori_loop(0, NZ, tile, start)
    peak = jnp.max(top, axis=1, keepdims=True)
    total = jnp.sum(total * jnp.exp(top - peak), axis=1, keepdims=True)
    hit = jnp.sum(hit, axis=1, keepdims=True)
    return jnp.where(lane == 0, peak, jnp.where(lane == 1, total, jnp.where(lane == 2, hit, 0.0)))


def target_columns(here, tg, tcol, tsend, trecv):
    def columns(slot):
        wide = jnp.broadcast_to(tg[slot].astype(jnp.float32), (BLOCK, BLOCK))
        tcol[slot] = wide.T

    def take_targets(i, _):
        slot, peer = here.plane_peer(i)
        remote(tg.at[slot], tg.at[slot], tsend.at[i], trecv.at[slot], peer).wait_recv()
        columns(slot)
        return 0

    columns(here.pos)
    lax.fori_loop(1, 16, take_targets, 0)


def vocab_part(here, gather, acts, wv, tcol, out_stats, in_stats, ssend, srecv):
    def batch(i, _):
        for n, events in enumerate(EVENTS):
            if events:

                @pl.when(i == n)
                def _():
                    for e in events:
                        gather.event(e)

        slots = []
        for half in (0, 1):
            dx = pick([pair[half][0] for pair in SOURCES], i)
            dy = pick([pair[half][1] for pair in SOURCES], i)
            slots.append(here.slot(dx, dy))
        table = stats_of(here, acts, wv, tcol, *slots)
        for half in (0, 1):
            slot = slots[half]
            out_stats[slot] = table[half * BLOCK : (half + 1) * BLOCK].T[:8]

        def give(half):
            slot = slots[half]
            to = here.at(x=lax.div(slot, NY), y=lax.rem(slot, NY))
            remote(out_stats.at[slot], in_stats.at[here.pos], ssend.at[slot], srecv.at[here.pos], to).start()

        @pl.when(i > 0)
        def _():
            give(0)

        give(1)
        return 0

    lax.fori_loop(0, len(SOURCES), batch, 0)


def losses_of(here, out_stats, in_stats, ssend, srecv):
    in_stats[here.pos] = out_stats[here.pos]

    def take(i, _):
        slot, peer = here.plane_peer(i)
        remote(out_stats.at[slot], in_stats.at[slot], ssend.at[slot], srecv.at[slot], peer).wait_recv()
        return 0

    lax.fori_loop(1, 16, take, 0)
    stats = [in_stats[n] for n in range(16)]
    top = functools.reduce(jnp.maximum, [s[0:1] for s in stats])
    total = sum(s[1:2] * jnp.exp(s[0:1] - top) for s in stats)
    hit = sum(s[2:3] for s in stats)
    return top + jnp.log(total) - hit


def domain_part(here, losses, domains, dom, dsend, drecv):
    lane = lax.broadcasted_iota(jnp.int32, (8, 128), 1)
    mine = domains[here.x * NZ + here.z]
    value = jnp.broadcast_to(jnp.sum(losses, axis=1, keepdims=True), (8, 128))
    value = jnp.where(lane == mine, value, 0.0)
    for stage in (0, 1):
        peers = here.plane_peer if stage == 0 else here.column_peer
        own = here.pos if stage == 0 else here.z * 2 + here.c
        dom[stage, own] = value

        def give(i, _):
            slot, peer = peers(i)
            remote(dom.at[stage, own], dom.at[stage, own], dsend.at[stage, i], drecv.at[stage, own], peer).start()
            return 0

        def take(i, _):
            slot, peer = peers(i)
            remote(dom.at[stage, slot], dom.at[stage, slot], dsend.at[stage, i], drecv.at[stage, slot], peer).wait_recv()
            return 0

        lax.fori_loop(1, 16, give, 0)
        lax.fori_loop(1, 16, take, 0)
        value = sum(dom[stage, n] for n in range(16))
    counts = jnp.zeros((8, 128), jnp.float32)
    for n in range(DOCS):
        counts = counts + jnp.where(lane == domains[n], 1.0, 0.0)
    return value / jnp.maximum(counts * (NY * 2 * BLOCK), 1.0)


def finish_sends(here, out_stats, in_stats, ssend, srecv, tg, tsend, trecv, dom, dsend, drecv):
    def one(i, _):
        slot, peer = here.plane_peer(i)
        remote(out_stats.at[slot], in_stats.at[slot], ssend.at[slot], srecv.at[slot], peer).wait_send()
        remote(tg.at[slot], tg.at[slot], tsend.at[i], trecv.at[slot], peer).wait_send()
        for stage in (0, 1):
            remote(dom.at[stage, slot], dom.at[stage, slot], dsend.at[stage, i], drecv.at[stage, slot], peer).wait_send()
        return 0

    lax.fori_loop(1, 16, one, 0)


HALF_HEADS = HEADS // 2
CHUNKS = 4
PER = HALF_HEADS // CHUNKS


def feature(inputs):
    wide = inputs.astype(jnp.float32)
    return jnp.where(wide > 0.0, wide + 1.0, jnp.exp(jnp.minimum(wide, 0.0))).astype(jnp.bfloat16)


def head_slice(h):
    return pl.ds(pl.multiple_of(h * HD, HD), HD)


def local_states(keys, values, kf, state, sums):
    def one(h, _):
        cols = head_slice(h)
        feat = feature(keys[:, cols])
        kf[:, cols] = feat
        group, n = lax.div(h, HALF_HEADS), lax.rem(h, HALF_HEADS)
        state[group, n] = lax.dot_general(
            feat, values[:, cols], (((0,), (0,)), ((), ())), preferred_element_type=jnp.float32
        )
        sums[group, n] = jnp.sum(feat.astype(jnp.float32), axis=0, keepdims=True)
        return 0

    lax.fori_loop(0, HEADS, one, 0)


def inner_blocks(first, queries, kf, values, qf, probs, numer):
    row = lax.broadcasted_iota(jnp.int32, (BLOCK, BLOCK), 0)
    causal = row >= lax.broadcasted_iota(jnp.int32, (BLOCK, BLOCK), 1)

    def one(n, _):
        h = first + n
        cols = head_slice(h)
        feat = feature(queries[:, cols])
        qf[:, cols] = feat
        scores = lax.dot_general(feat, kf[:, cols], (((1,), (1,)), ((), ())), preferred_element_type=jnp.float32)
        prob = jnp.where(causal, scores, 0.0).astype(jnp.bfloat16)
        probs[h] = prob
        numer[:, cols] = jnp.dot(prob, values[:, cols], preferred_element_type=jnp.float32)
        return 0

    lax.fori_loop(0, HALF_HEADS, one, 0)


def outer_blocks(first, qf, probs, numer, state_in, sum_in, out):
    def one(n, _):
        h = first + n
        cols = head_slice(h)
        group, n = lax.div(h, HALF_HEADS), lax.rem(h, HALF_HEADS)
        feat = qf[:, cols]
        top = numer[:, cols] + jnp.dot(feat, state_in[group, n], preferred_element_type=jnp.float32)
        below = probs[h].astype(jnp.float32) + feat.astype(jnp.float32) * sum_in[group, n]
        out[:, cols] = (top / jnp.sum(below, axis=1, keepdims=True)).astype(jnp.bfloat16)
        return 0

    lax.fori_loop(0, HALF_HEADS, one, 0)


class Prefix:
    def __init__(self, here, refs, sems):
        self.here = here
        (self.state, self.sums, self.part, self.ksum, self.below, self.kbelow, self.above, self.kabove, self.cout, self.kout,
         self.stage, self.kstage, self.state_in, self.sum_in) = refs
        (self.xsend, self.xrecv, self.usend, self.urecv, self.dsend, self.drecv, self.fsend, self.frecv) = sems
        self.partner = here.at(c=1 - here.c)

    def exchange(self):
        other = 1 - self.here.c
        return (
            remote(self.state.at[other], self.part, self.xsend.at[0], self.xrecv.at[0], self.partner),
            remote(self.sums.at[other], self.ksum, self.xsend.at[1], self.xrecv.at[1], self.partner),
        )

    def heads(self, j):
        return pl.ds(j * PER, PER)

    def move(self, j, src, ksrc, dst, kdst, send, recv, to):
        heads = self.heads(j)
        copies = [remote(src.at[heads], dst.at[heads], send.at[j], recv.at[j], to)]
        if j == 0:
            copies.append(remote(ksrc, kdst, send.at[CHUNKS], recv.at[CHUNKS], to))
        return copies

    def up(self, j):
        return self.move(
            j, self.cout, self.kout, self.below, self.kbelow, self.usend, self.urecv, self.here.step("y", 1)
        )

    def down(self, j, relay):
        src, ksrc = (self.above, self.kabove) if relay else (self.cout, self.kout)
        return self.move(j, src, ksrc, self.above, self.kabove, self.dsend, self.drecv, self.here.step("y", -1))

    def total(self, j, add):
        heads = self.heads(j)
        value = self.state[self.here.c, heads] + self.part[heads]
        if add:
            value = value + self.below[heads].astype(jnp.float32)
        self.cout[heads] = value.astype(jnp.bfloat16)
        if j == 0:
            value = self.sums[self.here.c] + self.ksum[...]
            self.kout[...] = value + self.kbelow[...] if add else value

    def start(self):
        @pl.when(self.here.y < 2)
        def _():
            for j in range(CHUNKS):
                self.total(j, False)
                for copy in self.up(j):
                    copy.start()

                @pl.when(self.here.y == 0)
                def _():
                    for copy in self.down(j, False):
                        copy.start()

    def relay(self):
        @pl.when(self.here.y == 2)
        def _():
            for j in range(CHUNKS):
                for copy in self.up(j):
                    copy.wait_recv()
                self.total(j, True)
                for copy in self.up(j):
                    copy.start()

        @pl.when(self.here.y == 3)
        def _():
            for j in range(CHUNKS):
                for copy in self.down(j, False):
                    copy.wait_recv()
                for copy in self.down(j, True):
                    copy.start()

    def give(self, j):
        heads = self.heads(j)
        there = self.state_in.at[self.here.c, heads]
        copies = [remote(self.stage.at[heads], there, self.fsend.at[j], self.frecv.at[j], self.partner)]
        if j == 0:
            copies.append(
                remote(self.kstage, self.sum_in.at[self.here.c], self.fsend.at[CHUNKS], self.frecv.at[CHUNKS], self.partner)
            )
        return copies

    def finish(self):
        here = self.here
        second = (here.c == 1).astype(jnp.float32)
        for j in range(CHUNKS):

            @pl.when(jnp.logical_or(here.y == 1, here.y == 3))
            def _():
                for copy in self.up(j):
                    copy.wait_recv()

            @pl.when(here.y == 2)
            def _():
                for copy in self.down(j, False):
                    copy.wait_recv()

            heads = self.heads(j)
            before = self.below[heads].astype(jnp.float32) + self.above[heads].astype(jnp.float32)
            own, other = self.state[here.c, heads], self.part[heads]
            self.stage[heads] = (before + own * (1.0 - second)).astype(jnp.bfloat16)
            self.state_in[here.c, heads] = (before + other * second).astype(jnp.bfloat16)
            if j == 0:
                kbefore = self.kbelow[...] + self.kabove[...]
                self.kstage[...] = kbefore + self.sums[here.c] * (1.0 - second)
                self.sum_in[here.c] = kbefore + self.ksum[...] * second
            for copy in self.give(j):
                copy.start()

    def take(self):
        other = 1 - self.here.c
        for j in range(CHUNKS):
            heads = self.heads(j)
            remote(
                self.stage.at[heads], self.state_in.at[other, heads], self.fsend.at[j], self.frecv.at[j], self.partner
            ).wait_recv()
        remote(
            self.kstage, self.sum_in.at[other], self.fsend.at[CHUNKS], self.frecv.at[CHUNKS], self.partner
        ).wait_recv()

    def finish_send(self):
        for copy in self.exchange():
            copy.wait_send()
        for j in range(CHUNKS):
            for copy in self.give(j):
                copy.wait_send()

            @pl.when(self.here.y < NY - 1)
            def _():
                for copy in self.up(j):
                    copy.wait_send()

            @pl.when(jnp.logical_or(self.here.y == 0, self.here.y == 3))
            def _():
                for copy in self.down(j, False):
                    copy.wait_send()


def normalise(projected, gain, out):
    def rows(r, _):
        some = pl.ds(pl.multiple_of(r * 16, 16), 16)
        wide = projected[some].astype(jnp.float32)
        scale = lax.rsqrt(jnp.mean(wide * wide, axis=1, keepdims=True) + 1e-05)
        out[some] = (wide * scale * gain[...]).astype(jnp.bfloat16)
        return 0

    lax.fori_loop(0, BLOCK // 16, rows, 0)


def whole_kernel(
    q_hbm, k_hbm, v_hbm, gain_hbm, targets, domains, wo_hbm, w_hbm, projected, small,
    queries, keys, values, gain, qf, kf, probs, numer, state, sums, part, ksum, below, kbelow, above, kabove, cout, kout,
    stage, kstage, state_in, sum_in, attended, wo, halves, given, acts, wv, tg, tcol, out_stats, in_stats, dom,
    near, xsend, xrecv, usend, urecv, downsend, downrecv, fsend, frecv, zsend, zrecv, hsend, hrecv, psend, precv,
    gsend, grecv, rsend, rrecv, rpsend, rprecv, tsend, trecv, ssend, srecv, dsend, drecv,
):
    here = Place()
    for ref in (below, kbelow, above, kabove):
        ref[...] = jnp.zeros_like(ref)
    greet_all(here)
    moves = ((k_hbm, keys), (v_hbm, values), (q_hbm, queries), (gain_hbm, gain), (targets, tg.at[here.pos]))
    loads = [pltpu.make_async_copy(src, dst, near.at[2 + n]) for n, (src, dst) in enumerate(moves)]
    for load in loads:
        load.start()
    partner = here.at(c=1 - here.c)
    half = D // 2
    wo_rows = pl.ds(pl.multiple_of(here.y * 16, 16), 16)
    wo_own = wo_hbm.at[wo_rows, pl.ds(pl.multiple_of(here.c * half, half), half)]
    wo_place = wo.at[here.x, here.z, here.y]
    own_wo = pltpu.make_async_copy(wo_own, wo_place, near.at[1])
    own_wo.start()
    loads[0].wait()
    loads[1].wait()
    local_states(keys, values, kf, state, sums)
    for load in loads[2:]:
        load.wait()
    await_all()

    def wo_peer(i):
        z = lax.rem(here.z + i, NZ)
        return z, here.at(z=z)

    def wo_give(i, _):
        z, to = wo_peer(i)
        remote(wo_own, wo_place, zsend.at[i], zrecv.at[here.z], to).start()
        return 0

    def wo_take(i, _):
        z, to = wo_peer(i)
        place = wo.at[here.x, z, here.y]
        remote(place, place, zsend.at[i], zrecv.at[z], to).wait_recv()
        return 0

    def wo_sent(i, _):
        z, to = wo_peer(i)
        remote(wo_own, wo_place, zsend.at[i], zrecv.at[here.z], to).wait_send()
        return 0

    for i in (4, 3, 5, 2, 6, 1, 7):
        wo_give(i, 0)
    prefix = Prefix(
        here,
        (state, sums, part, ksum, below, kbelow, above, kabove, cout, kout, stage, kstage, state_in, sum_in),
        (xsend, xrecv, usend, urecv, downsend, downrecv, fsend, frecv),
    )
    ring = VocabRing(here, w_hbm, wv, near.at[0], rsend, rrecv, rpsend, rprecv)
    weights = PlaneGather(here, lambda x, y, start, count: wo.at[x, pl.ds(start, count), y], WO_CUTS, psend, precv)
    mine, theirs = attended.at[here.c], attended.at[1 - here.c]
    rows_over = remote(mine, mine, hsend.at[0], hrecv.at[0], partner)

    def give_targets(i, _):
        slot, peer = here.plane_peer(i)
        own = tg.at[here.pos]
        remote(own, own, tsend.at[i], trecv.at[here.pos], peer).start()
        return 0

    for copy in prefix.exchange():
        copy.start()
    ring.begin()
    inner_blocks(0, queries, kf, values, qf, probs, numer)
    for copy in prefix.exchange():
        copy.wait_recv()
    prefix.start()
    inner_blocks(HALF_HEADS, queries, kf, values, qf, probs, numer)
    own_wo.wait()
    lax.fori_loop(1, NZ, wo_take, 0)
    weights.begin_along("x")
    prefix.relay()
    weights.begin_along("y")
    lax.fori_loop(1, 16, give_targets, 0)
    weights.event(1, (0,))
    prefix.finish()
    weights.event(1, (1,))
    weights.event(2)
    prefix.take()
    outer_blocks(0, qf, probs, numer, state_in, sum_in, mine)
    ring.advance(1)
    weights.event(3)
    outer_blocks(HALF_HEADS, qf, probs, numer, state_in, sum_in, mine)
    rows_over.start()
    weights.event(4)
    target_columns(here, tg, tcol, tsend, trecv)
    weights.event(5)
    weights.event(6)
    ring.advance(2)
    weights.event(7)
    remote(theirs, theirs, hsend.at[0], hrecv.at[0], partner).wait_recv()
    weights.event(8)

    def project(n, _):
        cols = pl.ds(pl.multiple_of(n * TILE, TILE), TILE)
        rows = jnp.concatenate([attended[0], attended[1]], axis=0)
        w = wo[:, :, :, :, cols].reshape(D, TILE)
        both = jnp.dot(rows, w, preferred_element_type=jnp.float32).astype(jnp.bfloat16)
        low = here.c == 0
        halves[here.c, :, cols] = jnp.where(low, both[:BLOCK], both[BLOCK:])
        given[:, cols] = jnp.where(low, both[BLOCK:], both[:BLOCK])
        return 0

    lax.fori_loop(0, half // TILE, project, 0)
    back = remote(given, halves.at[here.c], hsend.at[1], hrecv.at[1], partner)
    back.start()
    other = halves.at[1 - here.c]
    remote(given, other, hsend.at[1], hrecv.at[1], partner).wait_recv()
    projected[:, :half] = halves[0]
    projected[:, half:] = halves[1]
    normalise(projected, gain, acts.at[here.pos])
    gather = PlaneGather(
        here, lambda x, y, start, count: acts.at[x * NY + y, pl.ds(start, count)], ROW_CUTS, gsend, grecv
    )
    gather.begin()
    gather.event(1)
    ring.advance(3)
    gather.event(2)
    ring.advance(4)
    ring.finish_recv()
    vocab_part(here, gather, acts, wv, tcol, out_stats, in_stats, ssend, srecv)
    losses = losses_of(here, out_stats, in_stats, ssend, srecv)
    means = domain_part(here, losses, domains, dom, dsend, drecv)
    first = lax.broadcasted_iota(jnp.int32, (8, 128), 0) == 0
    small[...] = jnp.where(first, losses, means)
    lax.fori_loop(1, NZ, wo_sent, 0)
    prefix.finish_send()
    weights.finish_send()
    rows_over.wait_send()
    back.wait_send()
    gather.finish_send()
    ring.finish_send()
    finish_sends(here, out_stats, in_stats, ssend, srecv, tg, tsend, trecv, dom, dsend, drecv)


def on_device(queries, keys, values, w_out, norm_gain, w_vocab, targets, domains):
    vmem = pl.BlockSpec(memory_space=pltpu.VMEM)
    dma = pltpu.SemaphoreType.DMA
    low, wide = jnp.bfloat16, jnp.float32
    anywhere = pl.BlockSpec(memory_space=pl.ANY)
    projected, small = pl.pallas_call(
        whole_kernel,
        out_shape=(
            jax.ShapeDtypeStruct((BLOCK, D), low),
            jax.ShapeDtypeStruct((8, BLOCK), wide),
        ),
        in_specs=[anywhere] * 5 + [pl.BlockSpec(memory_space=pltpu.SMEM), anywhere, anywhere],
        out_specs=(vmem, vmem),
        scratch_shapes=[
            pltpu.VMEM((BLOCK, D), low),
            pltpu.VMEM((BLOCK, D), low),
            pltpu.VMEM((BLOCK, D), low),
            pltpu.VMEM((1, D), wide),
            pltpu.VMEM((BLOCK, D), low),
            pltpu.VMEM((BLOCK, D), low),
            pltpu.VMEM((HEADS, BLOCK, BLOCK), low),
            pltpu.VMEM((BLOCK, D), wide),
            pltpu.VMEM((2, HALF_HEADS, HD, HD), wide),
            pltpu.VMEM((2, HALF_HEADS, 1, HD), wide),
            pltpu.VMEM((HALF_HEADS, HD, HD), wide),
            pltpu.VMEM((HALF_HEADS, 1, HD), wide),
            pltpu.VMEM((HALF_HEADS, HD, HD), low),
            pltpu.VMEM((HALF_HEADS, 1, HD), wide),
            pltpu.VMEM((HALF_HEADS, HD, HD), low),
            pltpu.VMEM((HALF_HEADS, 1, HD), wide),
            pltpu.VMEM((HALF_HEADS, HD, HD), low),
            pltpu.VMEM((HALF_HEADS, 1, HD), wide),
            pltpu.VMEM((HALF_HEADS, HD, HD), low),
            pltpu.VMEM((HALF_HEADS, 1, HD), wide),
            pltpu.VMEM((2, HALF_HEADS, HD, HD), low),
            pltpu.VMEM((2, HALF_HEADS, 1, HD), wide),
            pltpu.VMEM((2, BLOCK, D), low),
            pltpu.VMEM((NX, NZ, NY, 16, D // 2), low),
            pltpu.VMEM((2, BLOCK, D // 2), low),
            pltpu.VMEM((BLOCK, D // 2), low),
            pltpu.VMEM((16, BLOCK, D), low),
            pltpu.VMEM((NZ, D, TILE), low),
            pltpu.VMEM((16, 1, BLOCK), jnp.int32),
            pltpu.VMEM((16, BLOCK, BLOCK), wide),
            pltpu.VMEM((16, 8, 128), wide),
            pltpu.VMEM((16, 8, 128), wide),
            pltpu.VMEM((2, 16, 8, 128), wide),
            dma((7,)),
            dma((2,)),
            dma((2,)),
            dma((CHUNKS + 1,)),
            dma((CHUNKS + 1,)),
            dma((CHUNKS + 1,)),
            dma((CHUNKS + 1,)),
            dma((CHUNKS + 1,)),
            dma((CHUNKS + 1,)),
            dma((NZ,)),
            dma((NZ,)),
            dma((2,)),
            dma((2,)),
            dma((40,)),
            dma((40,)),
            dma((40,)),
            dma((40,)),
            dma((2, 4)),
            dma((2, 4)),
            dma((2, 4)),
            dma((2, 4)),
            dma((16,)),
            dma((16,)),
            dma((16,)),
            dma((16,)),
            dma((2, 16)),
            dma((2, 16)),
        ],
        compiler_params=pltpu.CompilerParams(
            collective_id=0, has_side_effects=True, vmem_limit_bytes=60 * 1024 * 1024
        ),
    )(queries[0], keys[0], values[0], norm_gain[None], targets, domains, w_out, w_vocab)
    return (projected[None], small[:1], small[1, :DOMAINS])


def solution(mesh):
    return jax.shard_map(
        on_device,
        mesh=mesh,
        in_specs=(
            P("doc", "seq", None),
            P("doc", "seq", None),
            P("doc", "seq", None),
            P("doc", None),
            P(),
            P(None, "doc"),
            P("doc", "seq"),
            P(),
        ),
        out_specs=(P("doc", "seq", None), P("doc", "seq"), P()),
        check_vma=False,
    )
```

```python
import functools

import jax
import jax.numpy as jnp
from jax import lax
from jax.experimental import pallas as pl
from jax.experimental.pallas import tpu as pltpu
from jax.sharding import PartitionSpec as P

HEADS = 16
HD = 128
DOMAINS = 7
BLOCK = 128
D = 2048
SHARD = 896
DOCS = 32
TILE = 256
NX, NY, NZ = 4, 4, 8
MESH = pl.DeviceIdType.MESH


class Place:
    def __init__(self):
        seq, doc = lax.axis_index("seq"), lax.axis_index("doc")
        self.y, self.c = lax.div(seq, 2), lax.rem(seq, 2)
        self.x, self.z = lax.div(doc, NZ), lax.rem(doc, NZ)
        self.pos = self.x * NY + self.y

    def at(self, x=None, y=None, z=None, c=None):
        x = self.x if x is None else x
        y = self.y if y is None else y
        z = self.z if z is None else z
        c = self.c if c is None else c
        return {"seq": y * 2 + c, "doc": x * NZ + z}

    def step(self, axis, by):
        if axis == "x":
            return self.at(x=lax.rem(self.x + by + NX, NX))
        if axis == "y":
            return self.at(y=lax.rem(self.y + by + NY, NY))
        return self.at(z=lax.rem(self.z + by + NZ, NZ))

    def slot(self, dx, dy):
        return lax.rem(self.x + dx + NX, NX) * NY + lax.rem(self.y + dy + NY, NY)

    def plane_peer(self, i):
        other = lax.rem(self.pos + i, NX * NY)
        return other, self.at(x=lax.div(other, NY), y=lax.rem(other, NY))

    def column_peer(self, i):
        mine = self.z * 2 + self.c
        other = lax.rem(mine + i, NZ * 2)
        return other, self.at(z=lax.div(other, 2), c=lax.rem(other, 2))


def remote(src, dst, send, recv, to):
    return pltpu.make_async_remote_copy(
        src_ref=src, dst_ref=dst, send_sem=send, recv_sem=recv, device_id=to, device_id_type=MESH
    )


def greet_all(here):
    barrier = pltpu.get_barrier_semaphore()

    def greet(i, _):
        pl.semaphore_signal(barrier, 1, device_id=here.plane_peer(i)[1], device_id_type=MESH)
        pl.semaphore_signal(barrier, 1, device_id=here.column_peer(i)[1], device_id_type=MESH)
        return 0

    lax.fori_loop(1, 16, greet, 0)


def await_all():
    pl.semaphore_wait(pltpu.get_barrier_semaphore(), 30)


class VocabRing:
    def __init__(self, here, w_hbm, wv, near, send, recv, psend, precv):
        self.here, self.w, self.wv, self.near = here, w_hbm, wv, near
        self.send, self.recv, self.psend, self.precv = send, recv, psend, precv
        self.first = pl.multiple_of(here.c * (D // 2), D // 2)
        self.column = pl.multiple_of(jnp.minimum(here.y * TILE, SHARD - TILE), 128)

    def rows(self, part):
        if part == "lo":
            return pl.ds(self.first, D // 4)
        if part == "hi":
            return pl.ds(self.first + D // 4, D // 4)
        return pl.ds(self.first, D // 2)

    def slot(self, off):
        return lax.rem(self.here.z + off + NZ, NZ)

    def hop(self, k, by, at_receiver):
        part = "all" if k < 4 else ("lo" if by > 0 else "hi")
        off = -by * (k if at_receiver else k - 1)
        dst = self.wv.at[self.slot(off), self.rows(part)]
        src = self.w.at[self.rows(part), pl.ds(self.column, TILE)] if (k == 1 and not at_receiver) else dst
        n = 0 if by > 0 else 1
        return remote(src, dst, self.send.at[n, k - 1], self.recv.at[n, k - 1], self.here.step("z", by))

    def share(self, k, by, at_receiver):
        part = "all" if k < 4 else ("lo" if by > 0 else "hi")
        off = -by * k
        rows = self.rows(part)
        if at_receiver:
            start = pl.multiple_of((1 - self.here.c) * (D // 2), D // 2)
            rows = {"all": pl.ds(start, D // 2), "lo": pl.ds(start, D // 4), "hi": pl.ds(start + D // 4, D // 4)}[part]
        ref = self.wv.at[self.slot(off), rows]
        n = 0 if by > 0 else 1
        return remote(ref, ref, self.psend.at[n, k - 1], self.precv.at[n, k - 1], self.here.at(c=1 - self.here.c))

    def own(self):
        return pltpu.make_async_copy(self.w.at[:, pl.ds(self.column, TILE)], self.wv.at[self.here.z], self.near)

    def begin(self):
        for by in (1, -1):
            self.hop(1, by, False).start()
        self.own().start()

    def advance(self, k):
        for by in (1, -1):
            self.hop(k, by, True).wait_recv()
            if k < 4:
                self.hop(k + 1, by, False).start()
            self.share(k, by, False).start()

    def finish_recv(self, *steps):
        for k in steps:
            for by in (1, -1):
                self.share(k, by, True).wait_recv()

    def finish_send(self):
        for k in range(1, 5):
            for by in (1, -1):
                self.hop(k, by, False).wait_send()
                self.share(k, by, False).wait_send()


HALF = {
    "A1+": (0, 0, "all", "A", 1),
    "A1-": (0, 0, "all", "A", -1),
    "B1+o": (0, 0, "all", "B", 1),
    "B1-o": (0, 0, "all", "B", -1),
    "A2+": (-1, 0, "lo", "A", 1),
    "A2-": (1, 0, "hi", "A", -1),
    "B1+m": (-1, 0, "all", "B", 1),
    "B1-m": (-1, 0, "all", "B", -1),
    "B1+p": (1, 0, "all", "B", 1),
    "B1-p": (1, 0, "all", "B", -1),
    "B1+l": (-2, 0, "lo", "B", 1),
    "B1-l": (-2, 0, "lo", "B", -1),
    "B1+h": (2, 0, "hi", "B", 1),
    "B1-h": (2, 0, "hi", "B", -1),
    "B2+o": (0, -1, "lo", "B", 1),
    "B2-o": (0, 1, "hi", "B", -1),
    "B2+p": (1, -1, "all", "B", 1),
    "B2-m": (-1, 1, "all", "B", -1),
    "B2+l": (-2, -1, "lo", "B", 1),
    "B2-h": (2, 1, "hi", "B", -1),
}
ORDER = list(HALF)
WO_CUTS = ((0, 1, 3), (3, 5, 8))
ROW_CUTS = ((0, 32, 64), (64, 96, 128))


class PlaneGather:
    def __init__(self, here, view, cuts, send, recv):
        self.here, self.view, self.cuts, self.send_sem, self.recv_sem = here, view, cuts, send, recv

    def copy(self, half, name, at_receiver):
        a, b, part, axis, by = HALF[name]
        if at_receiver:
            a, b = (a - by, b) if axis == "A" else (a, b - by)
        first, second = ("x", "y") if half == 0 else ("y", "x")
        dx, dy = (a, b) if half == 0 else (b, a)
        first_row, middle, last_row = self.cuts[half]
        start, stop = {"all": (first_row, last_row), "lo": (first_row, middle), "hi": (middle, last_row)}[part]
        column, row = lax.rem(self.here.x + dx + NX, NX), lax.rem(self.here.y + dy + NY, NY)
        ref = self.view(column, row, start, stop - start)
        n = half * len(ORDER) + ORDER.index(name)
        return remote(
            ref, ref, self.send_sem.at[n], self.recv_sem.at[n], self.here.step(first if axis == "A" else second, by)
        )

    def begin_along(self, axis):
        half = 0 if axis == "x" else 1
        for name in ("A1+", "A1-"):
            self.copy(half, name, False).start()
        for name in ("B1+o", "B1-o"):
            self.copy(1 - half, name, False).start()

    def send(self, halves, *names):
        for name in names:
            for half in halves:
                self.copy(half, name, False).start()

    def take(self, halves, *names):
        for name in names:
            for half in halves:
                self.copy(half, name, True).wait_recv()

    def begin(self):
        self.send((0, 1), "A1+", "A1-", "B1+o", "B1-o")

    def event(self, e, halves=(0, 1)):
        if e == 1:
            self.take(halves, "A1+", "A1-")
            self.send(halves, "A2+", "A2-", "B1+m", "B1-m", "B1+p", "B1-p")
        elif e == 2:
            self.take(halves, "B1+o", "B1-o")
            self.send(halves, "B2+o", "B2-o")
        elif e == 3:
            self.take(halves, "A2+", "A2-")
            self.send(halves, "B1+l", "B1-l", "B1+h", "B1-h")
        elif e == 4:
            self.take(halves, "B1+p", "B1-p", "B1+m", "B1-m")
            self.send(halves, "B2+p", "B2-m")
        elif e == 5:
            self.take(halves, "B2+o", "B2-o")
        elif e == 6:
            self.take(halves, "B1+l", "B1-l", "B1+h", "B1-h")
            self.send(halves, "B2+l", "B2-h")
        elif e == 7:
            self.take(halves, "B2+p", "B2-m")
        else:
            self.take(halves, "B2+l", "B2-h")

    def finish_send(self):
        for name in ORDER:
            for half in (0, 1):
                self.copy(half, name, False).wait_send()


PIECES = (
    ((0, 0), (0, 0), (-1, 0), (0, -1)),
    ((1, 0), (0, 1), (0, -1), (-1, 0)),
    ((0, 1), (1, 0), (2, 0), (0, 2)),
    ((-1, -1), (-1, -1), (1, 1), (1, 1)),
    ((-1, 1), (-1, 1), (1, -1), (1, -1)),
    ((0, 2), (2, 0), (2, -1), (-1, 2)),
    ((2, 1), (1, 2), (-1, 2), (2, -1)),
    ((1, 2), (2, 1), (2, 2), (2, 2)),
)
EVENTS = ((1,), (2,), (3,), (4,), (), (5, 6), (7,), (8,))
NEAR = (0, -1, 1, -2, 2, -3, 3, 4)


def pick(table, i):
    value = table[0]
    for n in range(1, len(table)):
        value = jnp.where(i == n, table[n], value)
    return value


def stats_of(here, acts, wv, tcol, slots, before):
    rows = 2 * BLOCK
    lane = lax.broadcasted_iota(jnp.int32, (rows, 128), 1)
    whole = here.y < NY - 1
    column = jnp.minimum(here.y * TILE, SHARD - TILE)
    middle = BLOCK // 2

    def joined(ref):
        return jnp.concatenate(
            [ref[slot, (n % 2) * middle : (n % 2 + 1) * middle] for n, slot in enumerate(slots)], axis=0
        )

    wanted = joined(tcol) - lane.astype(jnp.float32)

    def tile(n, carry):
        before(n)
        top, total, hit = carry
        shard = lax.rem(here.z + pick(NEAR, n) + NZ, NZ)
        logits = jnp.dot(joined(acts), wv[shard], preferred_element_type=jnp.float32)
        base = ((here.x * NZ + shard) * SHARD + column).astype(jnp.float32)
        one, two = logits[:, :128], logits[:, 128:]
        now = jnp.maximum(top, jnp.maximum(jnp.where(whole, one, two), two))
        add = jnp.exp(one - now)
        total = total * jnp.exp(top - now) + jnp.exp(two - now) + jnp.where(whole, add, 0.0)
        hit = hit + jnp.where(wanted == jnp.where(whole, base, -1e6), one, 0.0)
        hit = hit + jnp.where(wanted == base + 128.0, two, 0.0)
        return now, total, hit

    start = (
        jnp.full((rows, 128), -jnp.inf, jnp.float32),
        jnp.zeros((rows, 128), jnp.float32),
        jnp.zeros((rows, 128), jnp.float32),
    )
    top, total, hit = lax.fori_loop(0, NZ, tile, start)
    peak = jnp.max(top, axis=1, keepdims=True)
    total = jnp.sum(total * jnp.exp(top - peak), axis=1, keepdims=True)
    hit = jnp.sum(hit, axis=1, keepdims=True)
    return jnp.where(lane == 0, peak, jnp.where(lane == 1, total, jnp.where(lane == 2, hit, 0.0)))


def target_columns(here, tg, tcol, tsend, trecv):
    def columns(slot):
        wide = jnp.broadcast_to(tg[slot].astype(jnp.float32), (BLOCK, BLOCK))
        tcol[slot] = wide.T

    def take_targets(i, _):
        slot, peer = here.plane_peer(i)
        remote(tg.at[slot], tg.at[slot], tsend.at[i], trecv.at[slot], peer).wait_recv()
        columns(slot)
        return 0

    columns(here.pos)
    lax.fori_loop(1, 16, take_targets, 0)


def stat_copies(here, i, pair, slots, out_stats, in_stats, ssend, srecv):
    for half in (0, 1):
        slot = slots[2 * pair + half]
        to = here.at(x=lax.div(slot, NY), y=lax.rem(slot, NY))
        yield remote(
            out_stats.at[i, pair], in_stats.at[half, here.pos], ssend.at[i, pair, half], srecv.at[half, here.pos], to
        )


def slots_of(here, i):
    return [
        here.slot(pick([four[n][0] for four in PIECES], i), pick([four[n][1] for four in PIECES], i)) for n in range(4)
    ]


def vocab_part(here, gather, ring, acts, wv, tcol, out_stats, in_stats, ssend, srecv):
    def batch(i, _):
        for n, events in enumerate(EVENTS):
            if events:

                @pl.when(i == n)
                def _():
                    for e in events:
                        gather.event(e)

        def before(n):
            @pl.when(jnp.logical_and(i == 0, n == NZ - 1))
            def _():
                ring.advance(4)
                ring.finish_recv(4)

        slots = slots_of(here, i)
        table = stats_of(here, acts, wv, tcol, slots, before)
        for pair in (0, 1):
            out_stats[i, pair] = table[pair * BLOCK : (pair + 1) * BLOCK].T[:8]

        @pl.when(i > 0)
        def _():
            for copy in stat_copies(here, i, 0, slots, out_stats, in_stats, ssend, srecv):
                copy.start()

        for copy in stat_copies(here, i, 1, slots, out_stats, in_stats, ssend, srecv):
            copy.start()
        return 0

    lax.fori_loop(0, len(PIECES), batch, 0)


def losses_of(here, out_stats, in_stats, ssend, srecv):
    for half in (0, 1):
        in_stats[half, here.pos] = out_stats[0, 0]

    def take(i, _):
        slot, peer = here.plane_peer(i)
        for half in (0, 1):
            place = in_stats.at[half, slot]
            remote(place, place, ssend.at[0, 0, 0], srecv.at[half, slot], peer).wait_recv()
        return 0

    lax.fori_loop(1, 16, take, 0)
    early = lax.broadcasted_iota(jnp.int32, (8, BLOCK), 1) < BLOCK // 2
    stats = [jnp.where(early, in_stats[0, n], in_stats[1, n]) for n in range(16)]
    top = functools.reduce(jnp.maximum, [s[0:1] for s in stats])
    total = sum(s[1:2] * jnp.exp(s[0:1] - top) for s in stats)
    hit = sum(s[2:3] for s in stats)
    return top + jnp.log(total) - hit


def domain_part(here, losses, domains, dom, dsend, drecv):
    lane = lax.broadcasted_iota(jnp.int32, (8, 128), 1)
    mine = domains[here.x * NZ + here.z]
    value = jnp.broadcast_to(jnp.sum(losses, axis=1, keepdims=True), (8, 128))
    value = jnp.where(lane == mine, value, 0.0)
    for stage in (0, 1):
        peers = here.plane_peer if stage == 0 else here.column_peer
        own = here.pos if stage == 0 else here.z * 2 + here.c
        dom[stage, own] = value

        def give(i, _):
            slot, peer = peers(i)
            remote(dom.at[stage, own], dom.at[stage, own], dsend.at[stage, i], drecv.at[stage, own], peer).start()
            return 0

        def take(i, _):
            slot, peer = peers(i)
            remote(dom.at[stage, slot], dom.at[stage, slot], dsend.at[stage, i], drecv.at[stage, slot], peer).wait_recv()
            return 0

        lax.fori_loop(1, 16, give, 0)
        lax.fori_loop(1, 16, take, 0)
        value = sum(dom[stage, n] for n in range(16))
    counts = jnp.zeros((8, 128), jnp.float32)
    for n in range(DOCS):
        counts = counts + jnp.where(lane == domains[n], 1.0, 0.0)
    return value / jnp.maximum(counts * (NY * 2 * BLOCK), 1.0)


def finish_sends(here, out_stats, in_stats, ssend, srecv, tg, tsend, trecv, dom, dsend, drecv):
    def one(i, _):
        slot, peer = here.plane_peer(i)
        remote(tg.at[slot], tg.at[slot], tsend.at[i], trecv.at[slot], peer).wait_send()
        for stage in (0, 1):
            remote(dom.at[stage, slot], dom.at[stage, slot], dsend.at[stage, i], drecv.at[stage, slot], peer).wait_send()
        return 0

    lax.fori_loop(1, 16, one, 0)

    def batch(i, _):
        slots = slots_of(here, i)

        @pl.when(i > 0)
        def _():
            for copy in stat_copies(here, i, 0, slots, out_stats, in_stats, ssend, srecv):
                copy.wait_send()

        for copy in stat_copies(here, i, 1, slots, out_stats, in_stats, ssend, srecv):
            copy.wait_send()
        return 0

    lax.fori_loop(0, len(PIECES), batch, 0)


HALF_HEADS = HEADS // 2
CHUNKS = 4
PER = HALF_HEADS // CHUNKS


def feature(inputs):
    wide = inputs.astype(jnp.float32)
    return jnp.where(wide > 0.0, wide + 1.0, jnp.exp(jnp.minimum(wide, 0.0))).astype(jnp.bfloat16)


def head_slice(h):
    return pl.ds(pl.multiple_of(h * HD, HD), HD)


def local_states(keys, values, kf, state, sums):
    def one(h, _):
        cols = head_slice(h)
        feat = feature(keys[:, cols])
        kf[:, cols] = feat
        group, n = lax.div(h, HALF_HEADS), lax.rem(h, HALF_HEADS)
        state[group, n] = lax.dot_general(
            feat, values[:, cols], (((0,), (0,)), ((), ())), preferred_element_type=jnp.float32
        )
        sums[group, n] = jnp.sum(feat.astype(jnp.float32), axis=0, keepdims=True)
        return 0

    lax.fori_loop(0, HEADS, one, 0)


def inner_blocks(first, queries, kf, values, qf, probs, numer):
    row = lax.broadcasted_iota(jnp.int32, (BLOCK, BLOCK), 0)
    causal = row >= lax.broadcasted_iota(jnp.int32, (BLOCK, BLOCK), 1)

    def one(n, _):
        h = first + n
        cols = head_slice(h)
        feat = feature(queries[:, cols])
        qf[:, cols] = feat
        scores = lax.dot_general(feat, kf[:, cols], (((1,), (1,)), ((), ())), preferred_element_type=jnp.float32)
        prob = jnp.where(causal, scores, 0.0).astype(jnp.bfloat16)
        probs[h] = prob
        numer[:, cols] = jnp.dot(prob, values[:, cols], preferred_element_type=jnp.float32)
        return 0

    lax.fori_loop(0, HALF_HEADS, one, 0)


def outer_blocks(first, qf, probs, numer, state_in, sum_in, out):
    def one(n, _):
        h = first + n
        cols = head_slice(h)
        group, n = lax.div(h, HALF_HEADS), lax.rem(h, HALF_HEADS)
        feat = qf[:, cols]
        top = numer[:, cols] + jnp.dot(feat, state_in[group, n], preferred_element_type=jnp.float32)
        below = probs[h].astype(jnp.float32) + feat.astype(jnp.float32) * sum_in[group, n]
        out[:, cols] = (top / jnp.sum(below, axis=1, keepdims=True)).astype(jnp.bfloat16)
        return 0

    lax.fori_loop(0, HALF_HEADS, one, 0)


class Prefix:
    def __init__(self, here, refs, sems):
        self.here = here
        (self.state, self.sums, self.part, self.ksum, self.below, self.kbelow, self.above, self.kabove, self.cout, self.kout,
         self.stage, self.kstage, self.state_in, self.sum_in) = refs
        (self.xsend, self.xrecv, self.usend, self.urecv, self.dsend, self.drecv, self.fsend, self.frecv) = sems
        self.partner = here.at(c=1 - here.c)

    def exchange(self):
        other = 1 - self.here.c
        return (
            remote(self.state.at[other], self.part, self.xsend.at[0], self.xrecv.at[0], self.partner),
            remote(self.sums.at[other], self.ksum, self.xsend.at[1], self.xrecv.at[1], self.partner),
        )

    def heads(self, j):
        return pl.ds(j * PER, PER)

    def move(self, j, src, ksrc, dst, kdst, send, recv, to):
        heads = self.heads(j)
        copies = [remote(src.at[heads], dst.at[heads], send.at[j], recv.at[j], to)]
        if j == 0:
            copies.append(remote(ksrc, kdst, send.at[CHUNKS], recv.at[CHUNKS], to))
        return copies

    def up(self, j):
        return self.move(
            j, self.cout, self.kout, self.below, self.kbelow, self.usend, self.urecv, self.here.step("y", 1)
        )

    def down(self, j, relay):
        src, ksrc = (self.above, self.kabove) if relay else (self.cout, self.kout)
        return self.move(j, src, ksrc, self.above, self.kabove, self.dsend, self.drecv, self.here.step("y", -1))

    def total(self, j, add):
        heads = self.heads(j)
        value = self.state[self.here.c, heads] + self.part[heads]
        if add:
            value = value + self.below[heads].astype(jnp.float32)
        self.cout[heads] = value.astype(jnp.bfloat16)
        if j == 0:
            value = self.sums[self.here.c] + self.ksum[...]
            self.kout[...] = value + self.kbelow[...] if add else value

    def start(self):
        @pl.when(self.here.y < 2)
        def _():
            for j in range(CHUNKS):
                self.total(j, False)
                for copy in self.up(j):
                    copy.start()

                @pl.when(self.here.y == 0)
                def _():
                    for copy in self.down(j, False):
                        copy.start()

    def relay(self):
        @pl.when(self.here.y == 2)
        def _():
            for j in range(CHUNKS):
                for copy in self.up(j):
                    copy.wait_recv()
                self.total(j, True)
                for copy in self.up(j):
                    copy.start()

        @pl.when(self.here.y == 3)
        def _():
            for j in range(CHUNKS):
                for copy in self.down(j, False):
                    copy.wait_recv()
                for copy in self.down(j, True):
                    copy.start()

    def give(self, j):
        heads = self.heads(j)
        there = self.state_in.at[self.here.c, heads]
        copies = [remote(self.stage.at[heads], there, self.fsend.at[j], self.frecv.at[j], self.partner)]
        if j == 0:
            copies.append(
                remote(self.kstage, self.sum_in.at[self.here.c], self.fsend.at[CHUNKS], self.frecv.at[CHUNKS], self.partner)
            )
        return copies

    def finish(self):
        here = self.here
        second = (here.c == 1).astype(jnp.float32)
        for j in range(CHUNKS):

            @pl.when(jnp.logical_or(here.y == 1, here.y == 3))
            def _():
                for copy in self.up(j):
                    copy.wait_recv()

            @pl.when(here.y == 2)
            def _():
                for copy in self.down(j, False):
                    copy.wait_recv()

            heads = self.heads(j)
            before = self.below[heads].astype(jnp.float32) + self.above[heads].astype(jnp.float32)
            own, other = self.state[here.c, heads], self.part[heads]
            self.stage[heads] = (before + own * (1.0 - second)).astype(jnp.bfloat16)
            self.state_in[here.c, heads] = (before + other * second).astype(jnp.bfloat16)
            if j == 0:
                kbefore = self.kbelow[...] + self.kabove[...]
                self.kstage[...] = kbefore + self.sums[here.c] * (1.0 - second)
                self.sum_in[here.c] = kbefore + self.ksum[...] * second
            for copy in self.give(j):
                copy.start()

    def take(self):
        other = 1 - self.here.c
        for j in range(CHUNKS):
            heads = self.heads(j)
            remote(
                self.stage.at[heads], self.state_in.at[other, heads], self.fsend.at[j], self.frecv.at[j], self.partner
            ).wait_recv()
        remote(
            self.kstage, self.sum_in.at[other], self.fsend.at[CHUNKS], self.frecv.at[CHUNKS], self.partner
        ).wait_recv()

    def finish_send(self):
        for copy in self.exchange():
            copy.wait_send()
        for j in range(CHUNKS):
            for copy in self.give(j):
                copy.wait_send()

            @pl.when(self.here.y < NY - 1)
            def _():
                for copy in self.up(j):
                    copy.wait_send()

            @pl.when(jnp.logical_or(self.here.y == 0, self.here.y == 3))
            def _():
                for copy in self.down(j, False):
                    copy.wait_send()


def normalise(projected, gain, out):
    def rows(r, _):
        some = pl.ds(pl.multiple_of(r * 16, 16), 16)
        wide = projected[some].astype(jnp.float32)
        scale = lax.rsqrt(jnp.mean(wide * wide, axis=1, keepdims=True) + 1e-05)
        out[some] = (wide * scale * gain[...]).astype(jnp.bfloat16)
        return 0

    lax.fori_loop(0, BLOCK // 16, rows, 0)


def whole_kernel(
    q_hbm, k_hbm, v_hbm, gain_hbm, targets, domains, wo_hbm, w_hbm, projected, small,
    queries, keys, values, gain, qf, kf, probs, numer, state, sums, part, ksum, below, kbelow, above, kabove, cout, kout,
    stage, kstage, state_in, sum_in, attended, wo, halves, given, acts, wv, tg, tcol, out_stats, in_stats, dom,
    near, xsend, xrecv, usend, urecv, downsend, downrecv, fsend, frecv, zsend, zrecv, hsend, hrecv, psend, precv,
    gsend, grecv, rsend, rrecv, rpsend, rprecv, tsend, trecv, ssend, srecv, dsend, drecv,
):
    here = Place()
    for ref in (below, kbelow, above, kabove):
        ref[...] = jnp.zeros_like(ref)
    greet_all(here)
    moves = ((k_hbm, keys), (v_hbm, values), (q_hbm, queries), (gain_hbm, gain), (targets, tg.at[here.pos]))
    loads = [pltpu.make_async_copy(src, dst, near.at[2 + n]) for n, (src, dst) in enumerate(moves)]
    for load in loads:
        load.start()
    partner = here.at(c=1 - here.c)
    half = D // 2
    wo_rows = pl.ds(pl.multiple_of(here.y * 16, 16), 16)
    wo_own = wo_hbm.at[wo_rows, pl.ds(pl.multiple_of(here.c * half, half), half)]
    wo_place = wo.at[here.x, here.z, here.y]
    own_wo = pltpu.make_async_copy(wo_own, wo_place, near.at[1])
    own_wo.start()
    loads[0].wait()
    loads[1].wait()
    local_states(keys, values, kf, state, sums)
    for load in loads[2:]:
        load.wait()
    await_all()

    def wo_peer(i):
        z = lax.rem(here.z + i, NZ)
        return z, here.at(z=z)

    def wo_give(i, _):
        z, to = wo_peer(i)
        remote(wo_own, wo_place, zsend.at[i], zrecv.at[here.z], to).start()
        return 0

    def wo_take(i, _):
        z, to = wo_peer(i)
        place = wo.at[here.x, z, here.y]
        remote(place, place, zsend.at[i], zrecv.at[z], to).wait_recv()
        return 0

    def wo_sent(i, _):
        z, to = wo_peer(i)
        remote(wo_own, wo_place, zsend.at[i], zrecv.at[here.z], to).wait_send()
        return 0

    for i in (4, 3, 5, 2, 6, 1, 7):
        wo_give(i, 0)
    prefix = Prefix(
        here,
        (state, sums, part, ksum, below, kbelow, above, kabove, cout, kout, stage, kstage, state_in, sum_in),
        (xsend, xrecv, usend, urecv, downsend, downrecv, fsend, frecv),
    )
    ring = VocabRing(here, w_hbm, wv, near.at[0], rsend, rrecv, rpsend, rprecv)
    weights = PlaneGather(here, lambda x, y, start, count: wo.at[x, pl.ds(start, count), y], WO_CUTS, psend, precv)
    mine, theirs = attended.at[here.c], attended.at[1 - here.c]
    rows_over = remote(mine, mine, hsend.at[0], hrecv.at[0], partner)

    def give_targets(i, _):
        slot, peer = here.plane_peer(i)
        own = tg.at[here.pos]
        remote(own, own, tsend.at[i], trecv.at[here.pos], peer).start()
        return 0

    for copy in prefix.exchange():
        copy.start()
    ring.begin()
    inner_blocks(0, queries, kf, values, qf, probs, numer)
    for copy in prefix.exchange():
        copy.wait_recv()
    prefix.start()
    inner_blocks(HALF_HEADS, queries, kf, values, qf, probs, numer)
    own_wo.wait()
    lax.fori_loop(1, NZ, wo_take, 0)
    weights.begin_along("x")
    prefix.relay()
    weights.begin_along("y")
    lax.fori_loop(1, 16, give_targets, 0)
    weights.event(1, (0,))
    prefix.finish()
    weights.event(1, (1,))
    weights.event(2)
    prefix.take()
    outer_blocks(0, qf, probs, numer, state_in, sum_in, mine)
    ring.advance(1)
    weights.event(3)
    outer_blocks(HALF_HEADS, qf, probs, numer, state_in, sum_in, mine)
    rows_over.start()
    weights.event(4)
    target_columns(here, tg, tcol, tsend, trecv)
    weights.event(5)
    weights.event(6)
    ring.advance(2)
    weights.event(7)
    remote(theirs, theirs, hsend.at[0], hrecv.at[0], partner).wait_recv()
    weights.event(8)

    def project(n, _):
        cols = pl.ds(pl.multiple_of(n * TILE, TILE), TILE)
        rows = jnp.concatenate([attended[0], attended[1]], axis=0)
        w = wo[:, :, :, :, cols].reshape(D, TILE)
        both = jnp.dot(rows, w, preferred_element_type=jnp.float32).astype(jnp.bfloat16)
        low = here.c == 0
        halves[here.c, :, cols] = jnp.where(low, both[:BLOCK], both[BLOCK:])
        given[:, cols] = jnp.where(low, both[BLOCK:], both[:BLOCK])
        return 0

    lax.fori_loop(0, half // TILE, project, 0)
    back = remote(given, halves.at[here.c], hsend.at[1], hrecv.at[1], partner)
    back.start()
    other = halves.at[1 - here.c]
    remote(given, other, hsend.at[1], hrecv.at[1], partner).wait_recv()
    projected[:, :half] = halves[0]
    projected[:, half:] = halves[1]
    normalise(projected, gain, acts.at[here.pos])
    gather = PlaneGather(
        here, lambda x, y, start, count: acts.at[x * NY + y, pl.ds(start, count)], ROW_CUTS, gsend, grecv
    )
    gather.begin()
    ring.own().wait()
    ring.advance(3)
    ring.finish_recv(1, 2, 3)
    vocab_part(here, gather, ring, acts, wv, tcol, out_stats, in_stats, ssend, srecv)
    losses = losses_of(here, out_stats, in_stats, ssend, srecv)
    means = domain_part(here, losses, domains, dom, dsend, drecv)
    first = lax.broadcasted_iota(jnp.int32, (8, 128), 0) == 0
    small[...] = jnp.where(first, losses, means)
    lax.fori_loop(1, NZ, wo_sent, 0)
    prefix.finish_send()
    weights.finish_send()
    rows_over.wait_send()
    back.wait_send()
    gather.finish_send()
    ring.finish_send()
    finish_sends(here, out_stats, in_stats, ssend, srecv, tg, tsend, trecv, dom, dsend, drecv)


def outputs_kernel(projected, small, projected_out, loss_out, mean_out):
    projected_out[...] = projected[...]
    loss_out[...] = small[0:1]
    mean_out[...] = small[1, :DOMAINS]


def on_device(queries, keys, values, w_out, norm_gain, w_vocab, targets, domains):
    vmem = pl.BlockSpec(memory_space=pltpu.VMEM)
    dma = pltpu.SemaphoreType.DMA
    low, wide = jnp.bfloat16, jnp.float32
    anywhere = pl.BlockSpec(memory_space=pl.ANY)
    projected, small = pl.pallas_call(
        whole_kernel,
        out_shape=(
            jax.ShapeDtypeStruct((BLOCK, D), low),
            jax.ShapeDtypeStruct((8, BLOCK), wide),
        ),
        in_specs=[anywhere] * 5 + [pl.BlockSpec(memory_space=pltpu.SMEM), anywhere, anywhere],
        out_specs=(vmem, vmem),
        scratch_shapes=[
            pltpu.VMEM((BLOCK, D), low),
            pltpu.VMEM((BLOCK, D), low),
            pltpu.VMEM((BLOCK, D), low),
            pltpu.VMEM((1, D), wide),
            pltpu.VMEM((BLOCK, D), low),
            pltpu.VMEM((BLOCK, D), low),
            pltpu.VMEM((HEADS, BLOCK, BLOCK), low),
            pltpu.VMEM((BLOCK, D), wide),
            pltpu.VMEM((2, HALF_HEADS, HD, HD), wide),
            pltpu.VMEM((2, HALF_HEADS, 1, HD), wide),
            pltpu.VMEM((HALF_HEADS, HD, HD), wide),
            pltpu.VMEM((HALF_HEADS, 1, HD), wide),
            pltpu.VMEM((HALF_HEADS, HD, HD), low),
            pltpu.VMEM((HALF_HEADS, 1, HD), wide),
            pltpu.VMEM((HALF_HEADS, HD, HD), low),
            pltpu.VMEM((HALF_HEADS, 1, HD), wide),
            pltpu.VMEM((HALF_HEADS, HD, HD), low),
            pltpu.VMEM((HALF_HEADS, 1, HD), wide),
            pltpu.VMEM((HALF_HEADS, HD, HD), low),
            pltpu.VMEM((HALF_HEADS, 1, HD), wide),
            pltpu.VMEM((2, HALF_HEADS, HD, HD), low),
            pltpu.VMEM((2, HALF_HEADS, 1, HD), wide),
            pltpu.VMEM((2, BLOCK, D), low),
            pltpu.VMEM((NX, NZ, NY, 16, D // 2), low),
            pltpu.VMEM((2, BLOCK, D // 2), low),
            pltpu.VMEM((BLOCK, D // 2), low),
            pltpu.VMEM((16, BLOCK, D), low),
            pltpu.VMEM((NZ, D, TILE), low),
            pltpu.VMEM((16, 1, BLOCK), jnp.int32),
            pltpu.VMEM((16, BLOCK, BLOCK), wide),
            pltpu.VMEM((8, 2, 8, 128), wide),
            pltpu.VMEM((2, 16, 8, 128), wide),
            pltpu.VMEM((2, 16, 8, 128), wide),
            dma((7,)),
            dma((2,)),
            dma((2,)),
            dma((CHUNKS + 1,)),
            dma((CHUNKS + 1,)),
            dma((CHUNKS + 1,)),
            dma((CHUNKS + 1,)),
            dma((CHUNKS + 1,)),
            dma((CHUNKS + 1,)),
            dma((NZ,)),
            dma((NZ,)),
            dma((2,)),
            dma((2,)),
            dma((40,)),
            dma((40,)),
            dma((40,)),
            dma((40,)),
            dma((2, 4)),
            dma((2, 4)),
            dma((2, 4)),
            dma((2, 4)),
            dma((16,)),
            dma((16,)),
            dma((8, 2, 2)),
            dma((2, 16)),
            dma((2, 16)),
            dma((2, 16)),
        ],
        compiler_params=pltpu.CompilerParams(
            collective_id=0, has_side_effects=True, vmem_limit_bytes=60 * 1024 * 1024
        ),
    )(queries[0], keys[0], values[0], norm_gain[None], targets, domains, w_out, w_vocab)
    projected, losses, means = pl.pallas_call(
        outputs_kernel,
        out_shape=(
            jax.ShapeDtypeStruct((BLOCK, D), low),
            jax.ShapeDtypeStruct((1, BLOCK), wide),
            jax.ShapeDtypeStruct((DOMAINS,), wide),
        ),
        in_specs=[vmem, vmem],
        out_specs=(vmem, vmem, vmem),
    )(projected, small)
    return (projected[None], losses, means)


def solution(mesh):
    return jax.shard_map(
        on_device,
        mesh=mesh,
        in_specs=(
            P("doc", "seq", None),
            P("doc", "seq", None),
            P("doc", "seq", None),
            P("doc", None),
            P(),
            P(None, "doc"),
            P("doc", "seq"),
            P(),
        ),
        out_specs=(P("doc", "seq", None), P("doc", "seq"), P()),
        check_vma=False,
    )
```

```python
import functools

import jax
import jax.numpy as jnp
from jax import lax
from jax.experimental import pallas as pl
from jax.experimental.pallas import tpu as pltpu
from jax.sharding import PartitionSpec as P

HEADS = 16
HD = 128
DOMAINS = 7
BLOCK = 128
D = 2048
SHARD = 896
DOCS = 32
TILE = 256
NX, NY, NZ = 4, 4, 8
MESH = pl.DeviceIdType.MESH


class Place:
    def __init__(self):
        seq, doc = lax.axis_index("seq"), lax.axis_index("doc")
        self.y, self.c = lax.div(seq, 2), lax.rem(seq, 2)
        self.x, self.z = lax.div(doc, NZ), lax.rem(doc, NZ)
        self.pos = self.x * NY + self.y

    def at(self, x=None, y=None, z=None, c=None):
        x = self.x if x is None else x
        y = self.y if y is None else y
        z = self.z if z is None else z
        c = self.c if c is None else c
        return {"seq": y * 2 + c, "doc": x * NZ + z}

    def step(self, axis, by):
        if axis == "x":
            return self.at(x=lax.rem(self.x + by + NX, NX))
        if axis == "y":
            return self.at(y=lax.rem(self.y + by + NY, NY))
        return self.at(z=lax.rem(self.z + by + NZ, NZ))

    def slot(self, dx, dy):
        return lax.rem(self.x + dx + NX, NX) * NY + lax.rem(self.y + dy + NY, NY)

    def plane_peer(self, i):
        other = lax.rem(self.pos + i, NX * NY)
        return other, self.at(x=lax.div(other, NY), y=lax.rem(other, NY))

    def column_peer(self, i):
        mine = self.z * 2 + self.c
        other = lax.rem(mine + i, NZ * 2)
        return other, self.at(z=lax.div(other, 2), c=lax.rem(other, 2))


def remote(src, dst, send, recv, to):
    return pltpu.make_async_remote_copy(
        src_ref=src, dst_ref=dst, send_sem=send, recv_sem=recv, device_id=to, device_id_type=MESH
    )


def all_sent(ref, sem, here):
    remote(ref, ref, sem, sem, here.at(c=1 - here.c)).wait_send()


def all_here(ref, sem, here):
    remote(ref, ref, sem, sem, here.at(c=1 - here.c)).wait_recv()


def greet_all(here):
    barrier = pltpu.get_barrier_semaphore()

    def greet(i, _):
        pl.semaphore_signal(barrier, 1, device_id=here.plane_peer(i)[1], device_id_type=MESH)
        pl.semaphore_signal(barrier, 1, device_id=here.column_peer(i)[1], device_id_type=MESH)
        return 0

    lax.fori_loop(1, 16, greet, 0)


def await_all():
    pl.semaphore_wait(pltpu.get_barrier_semaphore(), 30)


class VocabRing:
    def __init__(self, here, w_hbm, wv, near, send, recv, precv):
        self.here, self.w, self.wv, self.near = here, w_hbm, wv, near
        self.send, self.recv, self.precv = send, recv, precv
        self.first = pl.multiple_of(here.c * (D // 2), D // 2)
        self.column = pl.multiple_of(jnp.minimum(here.y * TILE, SHARD - TILE), 128)

    def rows(self, part):
        if part == "lo":
            return pl.ds(self.first, D // 4)
        if part == "hi":
            return pl.ds(self.first + D // 4, D // 4)
        return pl.ds(self.first, D // 2)

    def slot(self, off):
        return lax.rem(self.here.z + off + NZ, NZ)

    def hop(self, k, by):
        part = "all" if k < 4 else ("lo" if by > 0 else "hi")
        dst = self.wv.at[self.slot(-by * (k - 1)), self.rows(part)]
        src = self.w.at[self.rows(part), pl.ds(self.column, TILE)] if k == 1 else dst
        return remote(src, dst, self.send, self.recv.at[k - 1], self.here.step("z", by))

    def share(self, k, by):
        part = "all" if k < 4 else ("lo" if by > 0 else "hi")
        ref = self.wv.at[self.slot(-by * k), self.rows(part)]
        return remote(ref, ref, self.send, self.precv.at[k // 4], self.here.at(c=1 - self.here.c))

    def own(self):
        return pltpu.make_async_copy(self.w.at[:, pl.ds(self.column, TILE)], self.wv.at[self.here.z], self.near)

    def begin(self):
        for by in (1, -1):
            self.hop(1, by).start()
        self.own().start()

    def advance(self, k):
        all_here(self.wv.at[0] if k < 4 else self.wv.at[0, : D // 2], self.recv.at[k - 1], self.here)
        for by in (1, -1):
            if k < 4:
                self.hop(k + 1, by).start()
            self.share(k, by).start()

    def shared(self, last):
        if last:
            all_here(self.wv.at[0, : D // 2], self.precv.at[1], self.here)
        else:
            all_here(self.wv.at[0:3], self.precv.at[0], self.here)

    def finish_send(self):
        all_sent(self.wv.at[0:7], self.send, self.here)


HALF = {
    "A1+": (0, 0, "all", "A", 1),
    "A1-": (0, 0, "all", "A", -1),
    "B1+o": (0, 0, "all", "B", 1),
    "B1-o": (0, 0, "all", "B", -1),
    "A2+": (-1, 0, "lo", "A", 1),
    "A2-": (1, 0, "hi", "A", -1),
    "B1+m": (-1, 0, "all", "B", 1),
    "B1-m": (-1, 0, "all", "B", -1),
    "B1+p": (1, 0, "all", "B", 1),
    "B1-p": (1, 0, "all", "B", -1),
    "B1+l": (-2, 0, "lo", "B", 1),
    "B1-l": (-2, 0, "lo", "B", -1),
    "B1+h": (2, 0, "hi", "B", 1),
    "B1-h": (2, 0, "hi", "B", -1),
    "B2+o": (0, -1, "lo", "B", 1),
    "B2-o": (0, 1, "hi", "B", -1),
    "B2+p": (1, -1, "all", "B", 1),
    "B2-m": (-1, 1, "all", "B", -1),
    "B2+l": (-2, -1, "lo", "B", 1),
    "B2-h": (2, 1, "hi", "B", -1),
}
EVENT = {
    1: (("A1+", "A1-"), ("A2+", "A2-", "B1+m", "B1-m", "B1+p", "B1-p")),
    2: (("B1+o", "B1-o"), ("B2+o", "B2-o")),
    3: (("A2+", "A2-"), ("B1+l", "B1-l", "B1+h", "B1-h")),
    4: (("B1+m", "B1-m"), ("B2-m",)),
    5: (("B1+p", "B1-p"), ("B2+p",)),
    6: (("B2+o", "B2-o"), ()),
    7: (("B1+l", "B1-l", "B1+h", "B1-h"), ("B2+l", "B2-h")),
    8: (("B2+p", "B2-m"), ()),
    9: (("B2+l", "B2-h"), ()),
}
EVENT_OF = {name: e for e, (names, _) in EVENT.items() for name in names}
WO_CUTS = ((0, 1, 3), (3, 5, 8))
ROW_CUTS = ((0, 32, 64), (64, 96, 128))


class PlaneGather:
    def __init__(self, here, view, cuts, amount, apart, send, recv):
        self.here, self.view, self.cuts, self.amount, self.apart = here, view, cuts, amount, apart
        self.send_sem, self.recv_sem = send, recv

    def start(self, half, name):
        a, b, part, axis, by = HALF[name]
        first, second = ("x", "y") if half == 0 else ("y", "x")
        dx, dy = (a, b) if half == 0 else (b, a)
        first_row, middle, last_row = self.cuts[half]
        begin, end = {"all": (first_row, last_row), "lo": (first_row, middle), "hi": (middle, last_row)}[part]
        column, row = lax.rem(self.here.x + dx + NX, NX), lax.rem(self.here.y + dy + NY, NY)
        ref = self.view(column, row, begin, end - begin)
        to = self.here.step(first if axis == "A" else second, by)
        remote(ref, ref, self.send_sem, self.recv_sem.at[self.index(EVENT_OF[name], half)], to).start()

    def index(self, e, half):
        return len(EVENT) if e == 1 and half == 1 and self.apart else e - 1

    def begin_along(self, axis):
        half = 0 if axis == "x" else 1
        for name in ("A1+", "A1-"):
            self.start(half, name)
        for name in ("B1+o", "B1-o"):
            self.start(1 - half, name)

    def begin(self):
        self.begin_along("x")
        self.begin_along("y")

    def event(self, e, halves=(0, 1)):
        apart = len(halves) == 1
        all_here(self.amount(e, halves[0] if apart else None), self.recv_sem.at[self.index(e, halves[0])], self.here)
        for name in EVENT[e][1]:
            for half in halves:
                self.start(half, name)


def rows_of_event(acts, e, half):
    blocks = {1: 2, 2: 2, 3: 1, 4: 2, 5: 2, 6: 1, 7: 2, 8: 2, 9: 1}[e]
    return acts.at[0:blocks]


def places_of_event(wo, e, half):
    if half is not None:
        return wo.at[0, 0:6, 0] if half == 0 else wo.at[0, 0:5, 0:2]
    places = {2: 4, 3: 2, 4: 4, 5: 4, 6: 2, 7: 4, 8: 4, 9: 2}[e]
    return wo.at[0, 0:places]


PIECES = (
    ((0, 0), (0, 0), (-1, 0), (0, -1)),
    ((1, 0), (0, 1), (0, -1), (-1, 0)),
    ((0, 1), (1, 0), (2, 0), (0, 2)),
    ((-1, -1), (-1, -1), (-1, 1), (1, -1)),
    ((1, -1), (-1, 1), (1, 1), (1, 1)),
    ((0, 2), (2, 0), (2, -1), (-1, 2)),
    ((2, 1), (1, 2), (-1, 2), (2, -1)),
    ((1, 2), (2, 1), (2, 2), (2, 2)),
)
EVENTS = ((1,), (2,), (3,), (4,), (5,), (6, 7), (8,), (9,))
NEAR = (0, -1, 1, -2, 2, -3, 3, 4)


def pick(table, i):
    value = table[0]
    for n in range(1, len(table)):
        value = jnp.where(i == n, table[n], value)
    return value


def stats_of(here, acts, wv, tcol, slots, before):
    rows = 2 * BLOCK
    lane = lax.broadcasted_iota(jnp.int32, (rows, 128), 1)
    whole = here.y < NY - 1
    column = jnp.minimum(here.y * TILE, SHARD - TILE)
    middle = BLOCK // 2

    def joined(ref):
        return jnp.concatenate(
            [ref[slot, (n % 2) * middle : (n % 2 + 1) * middle] for n, slot in enumerate(slots)], axis=0
        )

    wanted = joined(tcol) - lane.astype(jnp.float32)

    def tile(n, carry):
        before(n)
        top, total, hit = carry
        shard = lax.rem(here.z + pick(NEAR, n) + NZ, NZ)
        logits = jnp.dot(joined(acts), wv[shard], preferred_element_type=jnp.float32)
        base = ((here.x * NZ + shard) * SHARD + column).astype(jnp.float32)
        one, two = logits[:, :128], logits[:, 128:]
        now = jnp.maximum(top, jnp.maximum(jnp.where(whole, one, two), two))
        add = jnp.exp(one - now)
        total = total * jnp.exp(top - now) + jnp.exp(two - now) + jnp.where(whole, add, 0.0)
        hit = hit + jnp.where(wanted == jnp.where(whole, base, -1e6), one, 0.0)
        hit = hit + jnp.where(wanted == base + 128.0, two, 0.0)
        return now, total, hit

    start = (
        jnp.full((rows, 128), -jnp.inf, jnp.float32),
        jnp.zeros((rows, 128), jnp.float32),
        jnp.zeros((rows, 128), jnp.float32),
    )
    top, total, hit = lax.fori_loop(0, NZ, tile, start)
    peak = jnp.max(top, axis=1, keepdims=True)
    total = jnp.sum(total * jnp.exp(top - peak), axis=1, keepdims=True)
    hit = jnp.sum(hit, axis=1, keepdims=True)
    return jnp.where(lane == 0, peak, jnp.where(lane == 1, total, jnp.where(lane == 2, hit, 0.0)))


def target_columns(here, tg, tcol, tsend, trecv):
    def columns(slot):
        wide = jnp.broadcast_to(tg[slot].astype(jnp.float32), (BLOCK, BLOCK))
        tcol[slot] = wide.T

    def take_targets(i, _):
        columns(i)
        return 0

    all_here(tg.at[0:15], trecv, here)
    lax.fori_loop(0, 16, take_targets, 0)


def stat_copies(here, i, pair, slots, out_stats, in_stats, ssend, srecv):
    for half in (0, 1):
        slot = slots[2 * pair + half]
        to = here.at(x=lax.div(slot, NY), y=lax.rem(slot, NY))
        yield remote(
            out_stats.at[i, pair], in_stats.at[half, here.pos], ssend, srecv, to
        )


def slots_of(here, i):
    return [
        here.slot(pick([four[n][0] for four in PIECES], i), pick([four[n][1] for four in PIECES], i)) for n in range(4)
    ]


def vocab_part(here, gather, ring, acts, wv, tcol, out_stats, in_stats, ssend, srecv):
    def batch(i, _):
        for n, events in enumerate(EVENTS):
            if events:

                @pl.when(i == n)
                def _():
                    for e in events:
                        gather.event(e)

        def before(n):
            @pl.when(jnp.logical_and(i == 0, n == NZ - 1))
            def _():
                ring.advance(4)
                ring.shared(True)

        slots = slots_of(here, i)
        table = stats_of(here, acts, wv, tcol, slots, before)
        for pair in (0, 1):
            out_stats[i, pair] = table[pair * BLOCK : (pair + 1) * BLOCK].T[:8]

        @pl.when(i > 0)
        def _():
            for copy in stat_copies(here, i, 0, slots, out_stats, in_stats, ssend, srecv):
                copy.start()

        for copy in stat_copies(here, i, 1, slots, out_stats, in_stats, ssend, srecv):
            copy.start()
        return 0

    lax.fori_loop(0, len(PIECES), batch, 0)


def losses_of(here, out_stats, in_stats, ssend, srecv):
    for half in (0, 1):
        in_stats[half, here.pos] = out_stats[0, 0]

    all_here(in_stats.at[:, 0:15], srecv, here)
    early = lax.broadcasted_iota(jnp.int32, (8, BLOCK), 1) < BLOCK // 2
    stats = [jnp.where(early, in_stats[0, n], in_stats[1, n]) for n in range(16)]
    top = functools.reduce(jnp.maximum, [s[0:1] for s in stats])
    total = sum(s[1:2] * jnp.exp(s[0:1] - top) for s in stats)
    hit = sum(s[2:3] for s in stats)
    return top + jnp.log(total) - hit


def domain_part(here, losses, domains, dom, dsend, drecv):
    lane = lax.broadcasted_iota(jnp.int32, (8, 128), 1)
    mine = domains[here.x * NZ + here.z]
    value = jnp.broadcast_to(jnp.sum(losses, axis=1, keepdims=True), (8, 128))
    value = jnp.where(lane == mine, value, 0.0)
    for stage in (0, 1):
        peers = here.plane_peer if stage == 0 else here.column_peer
        own = here.pos if stage == 0 else here.z * 2 + here.c
        dom[stage, own] = value

        def give(i, _):
            slot, peer = peers(i)
            remote(dom.at[stage, own], dom.at[stage, own], dsend.at[stage], drecv.at[stage], peer).start()
            return 0

        lax.fori_loop(1, 16, give, 0)
        all_here(dom.at[stage, 0:15], drecv.at[stage], here)
        value = sum(dom[stage, n] for n in range(16))
    counts = jnp.zeros((8, 128), jnp.float32)
    for n in range(DOCS):
        counts = counts + jnp.where(lane == domains[n], 1.0, 0.0)
    return value / jnp.maximum(counts * (NY * 2 * BLOCK), 1.0)


def finish_sends(here, in_stats, ssend, tg, tsend, dom, dsend):
    all_sent(in_stats.at[:, 0:15], ssend, here)
    all_sent(tg.at[0:15], tsend, here)
    for stage in (0, 1):
        all_sent(dom.at[stage, 0:15], dsend.at[stage], here)


HALF_HEADS = HEADS // 2
CHUNKS = 4
PER = HALF_HEADS // CHUNKS


def feature(inputs):
    wide = inputs.astype(jnp.float32)
    return jnp.where(wide > 0.0, wide + 1.0, jnp.exp(jnp.minimum(wide, 0.0))).astype(jnp.bfloat16)


def head_slice(h):
    return pl.ds(pl.multiple_of(h * HD, HD), HD)


def local_states(keys, values, kf, state, sums):
    def one(h, _):
        cols = head_slice(h)
        feat = feature(keys[:, cols])
        kf[:, cols] = feat
        group, n = lax.div(h, HALF_HEADS), lax.rem(h, HALF_HEADS)
        state[group, n] = lax.dot_general(
            feat, values[:, cols], (((0,), (0,)), ((), ())), preferred_element_type=jnp.float32
        )
        sums[group, n] = jnp.sum(feat.astype(jnp.float32), axis=0, keepdims=True)
        return 0

    lax.fori_loop(0, HEADS, one, 0)


def inner_blocks(first, queries, kf, values, qf, probs, numer):
    row = lax.broadcasted_iota(jnp.int32, (BLOCK, BLOCK), 0)
    causal = row >= lax.broadcasted_iota(jnp.int32, (BLOCK, BLOCK), 1)

    def one(n, _):
        h = first + n
        cols = head_slice(h)
        feat = feature(queries[:, cols])
        qf[:, cols] = feat
        scores = lax.dot_general(feat, kf[:, cols], (((1,), (1,)), ((), ())), preferred_element_type=jnp.float32)
        prob = jnp.where(causal, scores, 0.0).astype(jnp.bfloat16)
        probs[h] = prob
        numer[:, cols] = jnp.dot(prob, values[:, cols], preferred_element_type=jnp.float32)
        return 0

    lax.fori_loop(0, HALF_HEADS, one, 0)


def outer_blocks(first, qf, probs, numer, state_in, sum_in, out):
    def one(n, _):
        h = first + n
        cols = head_slice(h)
        group, n = lax.div(h, HALF_HEADS), lax.rem(h, HALF_HEADS)
        feat = qf[:, cols]
        top = numer[:, cols] + jnp.dot(feat, state_in[group, n], preferred_element_type=jnp.float32)
        below = probs[h].astype(jnp.float32) + feat.astype(jnp.float32) * sum_in[group, n]
        out[:, cols] = (top / jnp.sum(below, axis=1, keepdims=True)).astype(jnp.bfloat16)
        return 0

    lax.fori_loop(0, HALF_HEADS, one, 0)


class Prefix:
    def __init__(self, here, refs, sems):
        self.here = here
        (self.state, self.sums, self.part, self.ksum, self.below, self.kbelow, self.above, self.kabove, self.cout, self.kout,
         self.stage, self.kstage, self.state_in, self.sum_in) = refs
        (self.xsend, self.xrecv, self.usend, self.urecv, self.dsend, self.drecv, self.fsend, self.frecv) = sems
        self.partner = here.at(c=1 - here.c)

    def exchange(self):
        other = 1 - self.here.c
        return (
            remote(self.state.at[other], self.part, self.xsend.at[0], self.xrecv.at[0], self.partner),
            remote(self.sums.at[other], self.ksum, self.xsend.at[1], self.xrecv.at[1], self.partner),
        )

    def heads(self, j):
        return pl.ds(j * PER, PER)

    def move(self, j, src, ksrc, dst, kdst, send, recv, to):
        heads = self.heads(j)
        copies = [remote(src.at[heads], dst.at[heads], send.at[0], recv.at[j], to)]
        if j == 0:
            copies.append(remote(ksrc, kdst, send.at[1], recv.at[CHUNKS], to))
        return copies

    def up(self, j):
        return self.move(
            j, self.cout, self.kout, self.below, self.kbelow, self.usend, self.urecv, self.here.step("y", 1)
        )

    def down(self, j, relay):
        src, ksrc = (self.above, self.kabove) if relay else (self.cout, self.kout)
        return self.move(j, src, ksrc, self.above, self.kabove, self.dsend, self.drecv, self.here.step("y", -1))

    def total(self, j, add):
        heads = self.heads(j)
        value = self.state[self.here.c, heads] + self.part[heads]
        if add:
            value = value + self.below[heads].astype(jnp.float32)
        self.cout[heads] = value.astype(jnp.bfloat16)
        if j == 0:
            value = self.sums[self.here.c] + self.ksum[...]
            self.kout[...] = value + self.kbelow[...] if add else value

    def start(self):
        @pl.when(self.here.y < 2)
        def _():
            for j in range(CHUNKS):
                self.total(j, False)
                for copy in self.up(j):
                    copy.start()

                @pl.when(self.here.y == 0)
                def _():
                    for copy in self.down(j, False):
                        copy.start()

    def relay(self):
        @pl.when(self.here.y == 2)
        def _():
            for j in range(CHUNKS):
                for copy in self.up(j):
                    copy.wait_recv()
                self.total(j, True)
                for copy in self.up(j):
                    copy.start()

        @pl.when(self.here.y == 3)
        def _():
            for j in range(CHUNKS):
                for copy in self.down(j, False):
                    copy.wait_recv()
                for copy in self.down(j, True):
                    copy.start()

    def give(self, j):
        heads = self.heads(j)
        there = self.state_in.at[self.here.c, heads]
        copies = [remote(self.stage.at[heads], there, self.fsend.at[0], self.frecv.at[0], self.partner)]
        if j == 0:
            copies.append(
                remote(self.kstage, self.sum_in.at[self.here.c], self.fsend.at[1], self.frecv.at[1], self.partner)
            )
        return copies

    def finish(self):
        here = self.here
        second = (here.c == 1).astype(jnp.float32)
        for j in range(CHUNKS):

            @pl.when(jnp.logical_or(here.y == 1, here.y == 3))
            def _():
                for copy in self.up(j):
                    copy.wait_recv()

            @pl.when(here.y == 2)
            def _():
                for copy in self.down(j, False):
                    copy.wait_recv()

            heads = self.heads(j)
            before = self.below[heads].astype(jnp.float32) + self.above[heads].astype(jnp.float32)
            own, other = self.state[here.c, heads], self.part[heads]
            self.stage[heads] = (before + own * (1.0 - second)).astype(jnp.bfloat16)
            self.state_in[here.c, heads] = (before + other * second).astype(jnp.bfloat16)
            if j == 0:
                kbefore = self.kbelow[...] + self.kabove[...]
                self.kstage[...] = kbefore + self.sums[here.c] * (1.0 - second)
                self.sum_in[here.c] = kbefore + self.ksum[...] * second
            for copy in self.give(j):
                copy.start()

    def take(self):
        all_here(self.stage, self.frecv.at[0], self.here)
        all_here(self.kstage, self.frecv.at[1], self.here)

    def finish_send(self):
        for copy in self.exchange():
            copy.wait_send()
        all_sent(self.stage, self.fsend.at[0], self.here)
        all_sent(self.kstage, self.fsend.at[1], self.here)

        @pl.when(self.here.y < NY - 1)
        def _():
            all_sent(self.cout, self.usend.at[0], self.here)
            all_sent(self.kout, self.usend.at[1], self.here)

        @pl.when(jnp.logical_or(self.here.y == 0, self.here.y == 3))
        def _():
            all_sent(self.above, self.dsend.at[0], self.here)
            all_sent(self.kabove, self.dsend.at[1], self.here)


def normalise(projected, gain, out):
    def rows(r, _):
        some = pl.ds(pl.multiple_of(r * 16, 16), 16)
        wide = projected[some].astype(jnp.float32)
        scale = lax.rsqrt(jnp.mean(wide * wide, axis=1, keepdims=True) + 1e-05)
        out[some] = (wide * scale * gain[...]).astype(jnp.bfloat16)
        return 0

    lax.fori_loop(0, BLOCK // 16, rows, 0)


def whole_kernel(
    q_hbm, k_hbm, v_hbm, gain_hbm, targets, domains, wo_hbm, w_hbm, projected, small,
    queries, keys, values, gain, qf, kf, probs, numer, state, sums, part, ksum, below, kbelow, above, kabove, cout, kout,
    stage, kstage, state_in, sum_in, attended, wo, halves, given, acts, wv, tg, tcol, out_stats, in_stats, dom,
    near, xsend, xrecv, usend, urecv, downsend, downrecv, fsend, frecv, zsend, zrecv, hsend, hrecv, psend, precv,
    gsend, grecv, rsend, rrecv, rprecv, tsend, trecv, ssend, srecv, dsend, drecv,
):
    here = Place()
    for ref in (below, kbelow, above, kabove):
        ref[...] = jnp.zeros_like(ref)
    greet_all(here)
    moves = ((k_hbm, keys), (v_hbm, values), (q_hbm, queries), (gain_hbm, gain), (targets, tg.at[here.pos]))
    loads = [pltpu.make_async_copy(src, dst, near.at[2 + n]) for n, (src, dst) in enumerate(moves)]
    for load in loads:
        load.start()
    partner = here.at(c=1 - here.c)
    half = D // 2
    wo_rows = pl.ds(pl.multiple_of(here.y * 16, 16), 16)
    wo_own = wo_hbm.at[wo_rows, pl.ds(pl.multiple_of(here.c * half, half), half)]
    wo_place = wo.at[here.x, here.z, here.y]
    own_wo = pltpu.make_async_copy(wo_own, wo_place, near.at[1])
    own_wo.start()
    loads[0].wait()
    loads[1].wait()
    local_states(keys, values, kf, state, sums)
    for load in loads[2:]:
        load.wait()
    await_all()

    def wo_peer(i):
        z = lax.rem(here.z + i, NZ)
        return z, here.at(z=z)

    def wo_give(i, _):
        z, to = wo_peer(i)
        remote(wo_own, wo_place, zsend, zrecv, to).start()
        return 0

    for i in (4, 3, 5, 2, 6, 1, 7):
        wo_give(i, 0)
    prefix = Prefix(
        here,
        (state, sums, part, ksum, below, kbelow, above, kabove, cout, kout, stage, kstage, state_in, sum_in),
        (xsend, xrecv, usend, urecv, downsend, downrecv, fsend, frecv),
    )
    ring = VocabRing(here, w_hbm, wv, near.at[0], rsend, rrecv, rprecv)
    weights = PlaneGather(
        here, lambda x, y, start, count: wo.at[x, pl.ds(start, count), y],
        WO_CUTS, functools.partial(places_of_event, wo), True, psend, precv,
    )
    mine, theirs = attended.at[here.c], attended.at[1 - here.c]
    rows_over = remote(mine, mine, hsend.at[0], hrecv.at[0], partner)

    def give_targets(i, _):
        slot, peer = here.plane_peer(i)
        own = tg.at[here.pos]
        remote(own, own, tsend, trecv, peer).start()
        return 0

    for copy in prefix.exchange():
        copy.start()
    ring.begin()
    inner_blocks(0, queries, kf, values, qf, probs, numer)
    for copy in prefix.exchange():
        copy.wait_recv()
    prefix.start()
    inner_blocks(HALF_HEADS, queries, kf, values, qf, probs, numer)
    own_wo.wait()
    all_here(wo.at[0, 0:7, 0], zrecv, here)
    weights.begin_along("x")
    prefix.relay()
    weights.begin_along("y")
    lax.fori_loop(1, 16, give_targets, 0)
    weights.event(1, (0,))
    prefix.finish()
    weights.event(1, (1,))
    weights.event(2)
    prefix.take()
    outer_blocks(0, qf, probs, numer, state_in, sum_in, mine)
    ring.advance(1)
    weights.event(3)
    outer_blocks(HALF_HEADS, qf, probs, numer, state_in, sum_in, mine)
    rows_over.start()
    weights.event(4)
    target_columns(here, tg, tcol, tsend, trecv)
    weights.event(5)
    weights.event(6)
    weights.event(7)
    ring.advance(2)
    weights.event(8)
    remote(theirs, theirs, hsend.at[0], hrecv.at[0], partner).wait_recv()
    weights.event(9)

    def project(n, _):
        cols = pl.ds(pl.multiple_of(n * TILE, TILE), TILE)
        rows = jnp.concatenate([attended[0], attended[1]], axis=0)
        w = wo[:, :, :, :, cols].reshape(D, TILE)
        both = jnp.dot(rows, w, preferred_element_type=jnp.float32).astype(jnp.bfloat16)
        low = here.c == 0
        halves[here.c, :, cols] = jnp.where(low, both[:BLOCK], both[BLOCK:])
        given[:, cols] = jnp.where(low, both[BLOCK:], both[:BLOCK])
        return 0

    lax.fori_loop(0, half // TILE, project, 0)
    back = remote(given, halves.at[here.c], hsend.at[1], hrecv.at[1], partner)
    back.start()
    other = halves.at[1 - here.c]
    remote(given, other, hsend.at[1], hrecv.at[1], partner).wait_recv()
    projected[:, :half] = halves[0]
    projected[:, half:] = halves[1]
    normalise(projected, gain, acts.at[here.pos])
    gather = PlaneGather(
        here, lambda x, y, start, count: acts.at[x * NY + y, pl.ds(start, count)],
        ROW_CUTS, functools.partial(rows_of_event, acts), False, gsend, grecv,
    )
    gather.begin()
    ring.own().wait()
    ring.advance(3)
    ring.shared(False)
    vocab_part(here, gather, ring, acts, wv, tcol, out_stats, in_stats, ssend, srecv)
    losses = losses_of(here, out_stats, in_stats, ssend, srecv)
    means = domain_part(here, losses, domains, dom, dsend, drecv)
    first = lax.broadcasted_iota(jnp.int32, (8, 128), 0) == 0
    small[...] = jnp.where(first, losses, means)
    all_sent(wo.at[0, 0:7, 0], zsend, here)
    prefix.finish_send()
    all_sent(acts.at[0:15, 0:64], psend, here)
    rows_over.wait_send()
    back.wait_send()
    all_sent(acts.at[0:15], gsend, here)
    ring.finish_send()
    finish_sends(here, in_stats, ssend, tg, tsend, dom, dsend)


def outputs_kernel(projected, small, projected_out, loss_out, mean_out):
    projected_out[...] = projected[...]
    loss_out[...] = small[0:1]
    mean_out[...] = small[1, :DOMAINS]


def on_device(queries, keys, values, w_out, norm_gain, w_vocab, targets, domains):
    vmem = pl.BlockSpec(memory_space=pltpu.VMEM)
    dma = pltpu.SemaphoreType.DMA
    low, wide = jnp.bfloat16, jnp.float32
    anywhere = pl.BlockSpec(memory_space=pl.ANY)
    projected, small = pl.pallas_call(
        whole_kernel,
        out_shape=(
            jax.ShapeDtypeStruct((BLOCK, D), low),
            jax.ShapeDtypeStruct((8, BLOCK), wide),
        ),
        in_specs=[anywhere] * 5 + [pl.BlockSpec(memory_space=pltpu.SMEM), anywhere, anywhere],
        out_specs=(vmem, vmem),
        scratch_shapes=[
            pltpu.VMEM((BLOCK, D), low),
            pltpu.VMEM((BLOCK, D), low),
            pltpu.VMEM((BLOCK, D), low),
            pltpu.VMEM((1, D), wide),
            pltpu.VMEM((BLOCK, D), low),
            pltpu.VMEM((BLOCK, D), low),
            pltpu.VMEM((HEADS, BLOCK, BLOCK), low),
            pltpu.VMEM((BLOCK, D), wide),
            pltpu.VMEM((2, HALF_HEADS, HD, HD), wide),
            pltpu.VMEM((2, HALF_HEADS, 1, HD), wide),
            pltpu.VMEM((HALF_HEADS, HD, HD), wide),
            pltpu.VMEM((HALF_HEADS, 1, HD), wide),
            pltpu.VMEM((HALF_HEADS, HD, HD), low),
            pltpu.VMEM((HALF_HEADS, 1, HD), wide),
            pltpu.VMEM((HALF_HEADS, HD, HD), low),
            pltpu.VMEM((HALF_HEADS, 1, HD), wide),
            pltpu.VMEM((HALF_HEADS, HD, HD), low),
            pltpu.VMEM((HALF_HEADS, 1, HD), wide),
            pltpu.VMEM((HALF_HEADS, HD, HD), low),
            pltpu.VMEM((HALF_HEADS, 1, HD), wide),
            pltpu.VMEM((2, HALF_HEADS, HD, HD), low),
            pltpu.VMEM((2, HALF_HEADS, 1, HD), wide),
            pltpu.VMEM((2, BLOCK, D), low),
            pltpu.VMEM((NX, NZ, NY, 16, D // 2), low),
            pltpu.VMEM((2, BLOCK, D // 2), low),
            pltpu.VMEM((BLOCK, D // 2), low),
            pltpu.VMEM((16, BLOCK, D), low),
            pltpu.VMEM((NZ, D, TILE), low),
            pltpu.VMEM((16, 1, BLOCK), jnp.int32),
            pltpu.VMEM((16, BLOCK, BLOCK), wide),
            pltpu.VMEM((8, 2, 8, 128), wide),
            pltpu.VMEM((2, 16, 8, 128), wide),
            pltpu.VMEM((2, 16, 8, 128), wide),
            dma((7,)),
            dma((2,)),
            dma((2,)),
            dma((2,)),
            dma((CHUNKS + 1,)),
            dma((2,)),
            dma((CHUNKS + 1,)),
            dma((2,)),
            dma((2,)),
            dma(()),
            dma(()),
            dma((2,)),
            dma((2,)),
            dma(()),
            dma((len(EVENT) + 1,)),
            dma(()),
            dma((len(EVENT),)),
            dma(()),
            dma((4,)),
            dma((2,)),
            dma(()),
            dma(()),
            dma(()),
            dma(()),
            dma((2,)),
            dma((2,)),
        ],
        compiler_params=pltpu.CompilerParams(
            collective_id=0, has_side_effects=True, vmem_limit_bytes=60 * 1024 * 1024
        ),
    )(queries[0], keys[0], values[0], norm_gain[None], targets, domains, w_out, w_vocab)
    projected, losses, means = pl.pallas_call(
        outputs_kernel,
        out_shape=(
            jax.ShapeDtypeStruct((BLOCK, D), low),
            jax.ShapeDtypeStruct((1, BLOCK), wide),
            jax.ShapeDtypeStruct((DOMAINS,), wide),
        ),
        in_specs=[vmem, vmem],
        out_specs=(vmem, vmem, vmem),
    )(projected, small)
    return (projected[None], losses, means)


def solution(mesh):
    return jax.shard_map(
        on_device,
        mesh=mesh,
        in_specs=(
            P("doc", "seq", None),
            P("doc", "seq", None),
            P("doc", "seq", None),
            P("doc", None),
            P(),
            P(None, "doc"),
            P("doc", "seq"),
            P(),
        ),
        out_specs=(P("doc", "seq", None), P("doc", "seq"), P()),
        check_vma=False,
    )
```

```python
import functools

import jax
import jax.numpy as jnp
from jax import lax
from jax.experimental import pallas as pl
from jax.experimental.pallas import tpu as pltpu
from jax.sharding import PartitionSpec as P

HEADS = 16
HD = 128
DOMAINS = 7
BLOCK = 128
D = 2048
SHARD = 896
DOCS = 32
TILE = 256
NX, NY, NZ = 4, 4, 8
MESH = pl.DeviceIdType.MESH


class Place:
    def __init__(self):
        seq, doc = lax.axis_index("seq"), lax.axis_index("doc")
        self.y, self.c = lax.div(seq, 2), lax.rem(seq, 2)
        self.x, self.z = lax.div(doc, NZ), lax.rem(doc, NZ)
        self.pos = self.x * NY + self.y

    def at(self, x=None, y=None, z=None, c=None):
        x = self.x if x is None else x
        y = self.y if y is None else y
        z = self.z if z is None else z
        c = self.c if c is None else c
        return {"seq": y * 2 + c, "doc": x * NZ + z}

    def step(self, axis, by):
        if axis == "x":
            return self.at(x=lax.rem(self.x + by + NX, NX))
        if axis == "y":
            return self.at(y=lax.rem(self.y + by + NY, NY))
        return self.at(z=lax.rem(self.z + by + NZ, NZ))

    def slot(self, dx, dy):
        return lax.rem(self.x + dx + NX, NX) * NY + lax.rem(self.y + dy + NY, NY)

    def plane_peer(self, i):
        other = lax.rem(self.pos + i, NX * NY)
        return other, self.at(x=lax.div(other, NY), y=lax.rem(other, NY))

    def column_peer(self, i):
        mine = self.z * 2 + self.c
        other = lax.rem(mine + i, NZ * 2)
        return other, self.at(z=lax.div(other, 2), c=lax.rem(other, 2))


def remote(src, dst, send, recv, to):
    return pltpu.make_async_remote_copy(
        src_ref=src, dst_ref=dst, send_sem=send, recv_sem=recv, device_id=to, device_id_type=MESH
    )


def all_sent(ref, sem, here):
    remote(ref, ref, sem, sem, here.at(c=1 - here.c)).wait_send()


def all_here(ref, sem, here):
    remote(ref, ref, sem, sem, here.at(c=1 - here.c)).wait_recv()


def greet_all(here):
    barrier = pltpu.get_barrier_semaphore()

    def greet(i, _):
        pl.semaphore_signal(barrier, 1, device_id=here.plane_peer(i)[1], device_id_type=MESH)
        pl.semaphore_signal(barrier, 1, device_id=here.column_peer(i)[1], device_id_type=MESH)
        return 0

    lax.fori_loop(1, 16, greet, 0)


def await_all():
    pl.semaphore_wait(pltpu.get_barrier_semaphore(), 30)


class VocabRing:
    def __init__(self, here, w_hbm, wv, near, send, recv, precv):
        self.here, self.w, self.wv, self.near = here, w_hbm, wv, near
        self.send, self.recv, self.precv = send, recv, precv
        self.first = pl.multiple_of(here.c * (D // 2), D // 2)
        self.column = pl.multiple_of(jnp.minimum(here.y * TILE, SHARD - TILE), 128)

    def rows(self, part):
        if part == "lo":
            return pl.ds(self.first, D // 4)
        if part == "hi":
            return pl.ds(self.first + D // 4, D // 4)
        return pl.ds(self.first, D // 2)

    def slot(self, off):
        return lax.rem(self.here.z + off + NZ, NZ)

    def hop(self, k, by):
        part = "all" if k < 4 else ("lo" if by > 0 else "hi")
        dst = self.wv.at[self.slot(-by * (k - 1)), self.rows(part)]
        src = self.w.at[self.rows(part), pl.ds(self.column, TILE)] if k == 1 else dst
        return remote(src, dst, self.send, self.recv.at[k - 1], self.here.step("z", by))

    def share(self, k, by):
        part = "all" if k < 4 else ("lo" if by > 0 else "hi")
        ref = self.wv.at[self.slot(-by * k), self.rows(part)]
        return remote(ref, ref, self.send, self.precv.at[k // 4], self.here.at(c=1 - self.here.c))

    def own(self):
        return pltpu.make_async_copy(self.w.at[:, pl.ds(self.column, TILE)], self.wv.at[self.here.z], self.near)

    def begin(self):
        for by in (1, -1):
            self.hop(1, by).start()
        self.own().start()

    def advance(self, k):
        all_here(self.wv.at[0] if k < 4 else self.wv.at[0, : D // 2], self.recv.at[k - 1], self.here)
        for by in (1, -1):
            if k < 4:
                self.hop(k + 1, by).start()
            self.share(k, by).start()

    def shared(self, last):
        if last:
            all_here(self.wv.at[0, : D // 2], self.precv.at[1], self.here)
        else:
            all_here(self.wv.at[0:3], self.precv.at[0], self.here)

    def finish_send(self):
        all_sent(self.wv.at[0:7], self.send, self.here)


HALF = {
    "A1+": (0, 0, "all", "A", 1),
    "A1-": (0, 0, "all", "A", -1),
    "B1+o": (0, 0, "all", "B", 1),
    "B1-o": (0, 0, "all", "B", -1),
    "A2+": (-1, 0, "lo", "A", 1),
    "A2-": (1, 0, "hi", "A", -1),
    "B1+m": (-1, 0, "all", "B", 1),
    "B1-m": (-1, 0, "all", "B", -1),
    "B1+p": (1, 0, "all", "B", 1),
    "B1-p": (1, 0, "all", "B", -1),
    "B1+l": (-2, 0, "lo", "B", 1),
    "B1-l": (-2, 0, "lo", "B", -1),
    "B1+h": (2, 0, "hi", "B", 1),
    "B1-h": (2, 0, "hi", "B", -1),
    "B2+o": (0, -1, "lo", "B", 1),
    "B2-o": (0, 1, "hi", "B", -1),
    "B2+p": (1, -1, "all", "B", 1),
    "B2-m": (-1, 1, "all", "B", -1),
    "B2+l": (-2, -1, "lo", "B", 1),
    "B2-h": (2, 1, "hi", "B", -1),
}
EVENT = {
    1: (("A1+", "A1-"), ("A2+", "A2-", "B1+m", "B1-m", "B1+p", "B1-p")),
    2: (("B1+o", "B1-o"), ("B2+o", "B2-o")),
    3: (("A2+", "A2-"), ("B1+l", "B1-l", "B1+h", "B1-h")),
    4: (("B1+m", "B1-m"), ("B2-m",)),
    5: (("B1+p", "B1-p"), ("B2+p",)),
    6: (("B2+o", "B2-o"), ()),
    7: (("B1+l", "B1-l", "B1+h", "B1-h"), ("B2+l", "B2-h")),
    8: (("B2+p", "B2-m"), ()),
    9: (("B2+l", "B2-h"), ()),
}
EVENT_OF = {name: e for e, (names, _) in EVENT.items() for name in names}
WO_CUTS = ((5, 6, 8), (0, 2, 5))
ROW_CUTS = ((0, 32, 64), (64, 96, 128))


class PlaneGather:
    def __init__(self, here, view, cuts, amount, apart, send, recv):
        self.here, self.view, self.cuts, self.amount, self.apart = here, view, cuts, amount, apart
        self.send_sem, self.recv_sem = send, recv

    def start(self, half, name):
        a, b, part, axis, by = HALF[name]
        first, second = ("x", "y") if half == 0 else ("y", "x")
        dx, dy = (a, b) if half == 0 else (b, a)
        first_row, middle, last_row = self.cuts[half]
        begin, end = {"all": (first_row, last_row), "lo": (first_row, middle), "hi": (middle, last_row)}[part]
        column, row = lax.rem(self.here.x + dx + NX, NX), lax.rem(self.here.y + dy + NY, NY)
        ref = self.view(column, row, begin, end - begin)
        to = self.here.step(first if axis == "A" else second, by)
        remote(ref, ref, self.send_sem, self.recv_sem.at[self.index(EVENT_OF[name], half)], to).start()

    def index(self, e, half):
        return len(EVENT) if e == 1 and half == 1 and self.apart else e - 1

    def begin_along(self, axis):
        half = 0 if axis == "x" else 1
        for name in ("A1+", "A1-"):
            self.start(half, name)
        for name in ("B1+o", "B1-o"):
            self.start(1 - half, name)

    def begin(self):
        self.begin_along("x")
        self.begin_along("y")

    def event(self, e, halves=(0, 1)):
        apart = len(halves) == 1
        all_here(self.amount(e, halves[0] if apart else None), self.recv_sem.at[self.index(e, halves[0])], self.here)
        for name in EVENT[e][1]:
            for half in halves:
                self.start(half, name)


def rows_of_event(acts, e, half):
    blocks = {1: 2, 2: 2, 3: 1, 4: 2, 5: 2, 6: 1, 7: 2, 8: 2, 9: 1}[e]
    return acts.at[0:blocks]


def places_of_event(wo, e, half):
    if half is not None:
        return wo.at[0, 0:6, 0] if half == 0 else wo.at[0, 0:5, 0:2]
    places = {2: 4, 3: 2, 4: 4, 5: 4, 6: 2, 7: 4, 8: 4, 9: 2}[e]
    return wo.at[0, 0:places]


PIECES = (
    ((0, 0), (0, 0), (-1, 0), (0, -1)),
    ((1, 0), (0, 1), (0, -1), (-1, 0)),
    ((0, 1), (1, 0), (2, 0), (0, 2)),
    ((-1, -1), (-1, -1), (-1, 1), (1, -1)),
    ((1, -1), (-1, 1), (1, 1), (1, 1)),
    ((0, 2), (2, 0), (2, -1), (-1, 2)),
    ((2, 1), (1, 2), (-1, 2), (2, -1)),
    ((1, 2), (2, 1), (2, 2), (2, 2)),
)
EVENTS = ((1, 2), (3,), (), (4,), (5,), (6, 7), (8,), (9,))
NEAR = (0, -1, 1, -2, 2, -3, 3, 4)


def pick(table, i):
    value = table[0]
    for n in range(1, len(table)):
        value = jnp.where(i == n, table[n], value)
    return value


def stats_of(here, acts, wv, tcol, slots):
    rows = 2 * BLOCK
    lane = lax.broadcasted_iota(jnp.int32, (rows, 128), 1)
    whole = here.y < NY - 1
    column = jnp.minimum(here.y * TILE, SHARD - TILE)
    middle = BLOCK // 2

    def joined(ref):
        return jnp.concatenate(
            [ref[slot, (n % 2) * middle : (n % 2 + 1) * middle] for n, slot in enumerate(slots)], axis=0
        )

    wanted = joined(tcol) - lane.astype(jnp.float32)

    def tile(n, carry):
        top, total, hit = carry
        shard = lax.rem(here.z + NEAR[n] + NZ, NZ)
        logits = jnp.dot(joined(acts), wv[shard], preferred_element_type=jnp.float32)
        base = ((here.x * NZ + shard) * SHARD + column).astype(jnp.float32)
        one, two = logits[:, :128], logits[:, 128:]
        now = jnp.maximum(top, jnp.maximum(jnp.where(whole, one, two), two))
        add = jnp.exp(one - now)
        total = total * jnp.exp(top - now) + jnp.exp(two - now) + jnp.where(whole, add, 0.0)
        hit = hit + jnp.where(wanted == jnp.where(whole, base, -1e6), one, 0.0)
        hit = hit + jnp.where(wanted == base + 128.0, two, 0.0)
        return now, total, hit

    carry = (
        jnp.full((rows, 128), -jnp.inf, jnp.float32),
        jnp.zeros((rows, 128), jnp.float32),
        jnp.zeros((rows, 128), jnp.float32),
    )
    for n in range(NZ):
        carry = tile(n, carry)
    top, total, hit = carry
    peak = jnp.max(top, axis=1, keepdims=True)
    total = jnp.sum(total * jnp.exp(top - peak), axis=1, keepdims=True)
    hit = jnp.sum(hit, axis=1, keepdims=True)
    return jnp.where(lane == 0, peak, jnp.where(lane == 1, total, jnp.where(lane == 2, hit, 0.0)))


def target_columns(here, tg, tcol, tsend, trecv):
    def columns(slot):
        wide = jnp.broadcast_to(tg[slot].astype(jnp.float32), (BLOCK, BLOCK))
        tcol[slot] = wide.T

    def take_targets(i, _):
        columns(i)
        return 0

    all_here(tg.at[0:15], trecv, here)
    lax.fori_loop(0, 16, take_targets, 0)


def stat_copies(here, i, pair, slots, out_stats, in_stats, ssend, srecv):
    for half in (0, 1):
        slot = slots[2 * pair + half]
        to = here.at(x=lax.div(slot, NY), y=lax.rem(slot, NY))
        yield remote(
            out_stats.at[i, pair], in_stats.at[half, here.pos], ssend, srecv, to
        )


def slots_of(here, i):
    return [
        here.slot(pick([four[n][0] for four in PIECES], i), pick([four[n][1] for four in PIECES], i)) for n in range(4)
    ]


def vocab_part(here, gather, ring, acts, wv, tcol, out_stats, in_stats, ssend, srecv):
    def batch(i, _):
        for n, events in enumerate(EVENTS):
            if events:

                @pl.when(i == n)
                def _():
                    for e in events:
                        gather.event(e)
                    if n == 0:
                        ring.advance(4)
                        ring.shared(True)

        slots = slots_of(here, i)
        table = stats_of(here, acts, wv, tcol, slots)
        for pair in (0, 1):
            out_stats[i, pair] = table[pair * BLOCK : (pair + 1) * BLOCK].T[:8]

        @pl.when(i > 0)
        def _():
            for copy in stat_copies(here, i, 0, slots, out_stats, in_stats, ssend, srecv):
                copy.start()

        for copy in stat_copies(here, i, 1, slots, out_stats, in_stats, ssend, srecv):
            copy.start()
        return 0

    lax.fori_loop(0, len(PIECES), batch, 0)


def losses_of(here, out_stats, in_stats, ssend, srecv):
    for half in (0, 1):
        in_stats[half, here.pos] = out_stats[0, 0]

    all_here(in_stats.at[:, 0:15], srecv, here)
    early = lax.broadcasted_iota(jnp.int32, (8, BLOCK), 1) < BLOCK // 2
    stats = [jnp.where(early, in_stats[0, n], in_stats[1, n]) for n in range(16)]
    top = functools.reduce(jnp.maximum, [s[0:1] for s in stats])
    total = sum(s[1:2] * jnp.exp(s[0:1] - top) for s in stats)
    hit = sum(s[2:3] for s in stats)
    return top + jnp.log(total) - hit


def domain_part(here, losses, domains, dom, dsend, drecv):
    lane = lax.broadcasted_iota(jnp.int32, (8, 128), 1)
    mine = domains[here.x * NZ + here.z]
    value = jnp.broadcast_to(jnp.sum(losses, axis=1, keepdims=True), (8, 128))
    value = jnp.where(lane == mine, value, 0.0)
    for stage in (0, 1):
        peers = here.plane_peer if stage == 0 else here.column_peer
        own = here.pos if stage == 0 else here.z * 2 + here.c
        dom[stage, own] = value

        def give(i, _):
            slot, peer = peers(i)
            remote(dom.at[stage, own], dom.at[stage, own], dsend.at[stage], drecv.at[stage], peer).start()
            return 0

        lax.fori_loop(1, 16, give, 0)
        all_here(dom.at[stage, 0:15], drecv.at[stage], here)
        value = sum(dom[stage, n] for n in range(16))
    counts = jnp.zeros((8, 128), jnp.float32)
    for n in range(DOCS):
        counts = counts + jnp.where(lane == domains[n], 1.0, 0.0)
    return value / jnp.maximum(counts * (NY * 2 * BLOCK), 1.0)


def finish_sends(here, in_stats, ssend, tg, tsend, dom, dsend):
    all_sent(in_stats.at[:, 0:15], ssend, here)
    all_sent(tg.at[0:15], tsend, here)
    for stage in (0, 1):
        all_sent(dom.at[stage, 0:15], dsend.at[stage], here)


HALF_HEADS = HEADS // 2
CHUNKS = 4
PER = HALF_HEADS // CHUNKS


def feature(inputs):
    wide = inputs.astype(jnp.float32)
    return jnp.where(wide > 0.0, wide + 1.0, jnp.exp(jnp.minimum(wide, 0.0))).astype(jnp.bfloat16)


def head_slice(h):
    return pl.ds(pl.multiple_of(h * HD, HD), HD)


def by_four(one, count):
    def turn(t, _):
        for n in range(4):
            one(t * 4 + n, 0)
        return 0

    lax.fori_loop(0, count // 4, turn, 0)


def local_states(keys, values, kf, state, sums):
    def one(h, _):
        cols = head_slice(h)
        feat = feature(keys[:, cols])
        kf[:, cols] = feat
        group, n = lax.div(h, HALF_HEADS), lax.rem(h, HALF_HEADS)
        state[group, n] = lax.dot_general(
            feat, values[:, cols], (((0,), (0,)), ((), ())), preferred_element_type=jnp.float32
        )
        sums[group, n] = jnp.sum(feat.astype(jnp.float32), axis=0, keepdims=True)
        return 0

    by_four(one, HEADS)


def inner_blocks(first, queries, kf, values, qf, probs, numer):
    row = lax.broadcasted_iota(jnp.int32, (BLOCK, BLOCK), 0)
    causal = row >= lax.broadcasted_iota(jnp.int32, (BLOCK, BLOCK), 1)

    def one(n, _):
        h = first + n
        cols = head_slice(h)
        feat = feature(queries[:, cols])
        qf[:, cols] = feat
        scores = lax.dot_general(feat, kf[:, cols], (((1,), (1,)), ((), ())), preferred_element_type=jnp.float32)
        prob = jnp.where(causal, scores, 0.0).astype(jnp.bfloat16)
        probs[h] = prob
        numer[:, cols] = jnp.dot(prob, values[:, cols], preferred_element_type=jnp.float32)
        return 0

    by_four(one, HALF_HEADS)


def outer_blocks(first, qf, probs, numer, state_in, sum_in, out):
    def one(n, _):
        h = first + n
        cols = head_slice(h)
        group, n = lax.div(h, HALF_HEADS), lax.rem(h, HALF_HEADS)
        feat = qf[:, cols]
        top = numer[:, cols] + jnp.dot(feat, state_in[group, n], preferred_element_type=jnp.float32)
        below = probs[h].astype(jnp.float32) + feat.astype(jnp.float32) * sum_in[group, n]
        out[:, cols] = (top / jnp.sum(below, axis=1, keepdims=True)).astype(jnp.bfloat16)
        return 0

    by_four(one, HALF_HEADS)


class Prefix:
    def __init__(self, here, refs, sems):
        self.here = here
        (self.state, self.sums, self.part, self.ksum, self.below, self.kbelow, self.above, self.kabove, self.cout, self.kout,
         self.stage, self.kstage, self.state_in, self.sum_in) = refs
        (self.xsend, self.xrecv, self.usend, self.urecv, self.dsend, self.drecv, self.fsend, self.frecv) = sems
        self.partner = here.at(c=1 - here.c)

    def exchange(self):
        other = 1 - self.here.c
        return (
            remote(self.state.at[other], self.part, self.xsend.at[0], self.xrecv.at[0], self.partner),
            remote(self.sums.at[other], self.ksum, self.xsend.at[1], self.xrecv.at[1], self.partner),
        )

    def heads(self, j):
        return pl.ds(j * PER, PER)

    def move(self, j, src, ksrc, dst, kdst, send, recv, to):
        heads = self.heads(j)
        copies = [remote(src.at[heads], dst.at[heads], send.at[0], recv.at[j], to)]
        if j == 0:
            copies.append(remote(ksrc, kdst, send.at[1], recv.at[CHUNKS], to))
        return copies

    def up(self, j):
        return self.move(
            j, self.cout, self.kout, self.below, self.kbelow, self.usend, self.urecv, self.here.step("y", 1)
        )

    def down(self, j, relay):
        src, ksrc = (self.above, self.kabove) if relay else (self.cout, self.kout)
        return self.move(j, src, ksrc, self.above, self.kabove, self.dsend, self.drecv, self.here.step("y", -1))

    def total(self, j, add):
        heads = self.heads(j)
        value = self.state[self.here.c, heads] + self.part[heads]
        if add:
            value = value + self.below[heads].astype(jnp.float32)
        self.cout[heads] = value.astype(jnp.bfloat16)
        if j == 0:
            value = self.sums[self.here.c] + self.ksum[...]
            self.kout[...] = value + self.kbelow[...] if add else value

    def start(self):
        @pl.when(self.here.y < 2)
        def _():
            for j in range(CHUNKS):
                self.total(j, False)
                for copy in self.up(j):
                    copy.start()

                @pl.when(self.here.y == 0)
                def _():
                    for copy in self.down(j, False):
                        copy.start()

    def relay(self):
        @pl.when(self.here.y == 2)
        def _():
            for j in range(CHUNKS):
                for copy in self.up(j):
                    copy.wait_recv()
                self.total(j, True)
                for copy in self.up(j):
                    copy.start()

        @pl.when(self.here.y == 3)
        def _():
            for j in range(CHUNKS):
                for copy in self.down(j, False):
                    copy.wait_recv()
                for copy in self.down(j, True):
                    copy.start()

    def give(self, j):
        heads = self.heads(j)
        there = self.state_in.at[self.here.c, heads]
        copies = [remote(self.stage.at[heads], there, self.fsend.at[0], self.frecv.at[0], self.partner)]
        if j == 0:
            copies.append(
                remote(self.kstage, self.sum_in.at[self.here.c], self.fsend.at[1], self.frecv.at[1], self.partner)
            )
        return copies

    def finish(self):
        here = self.here
        second = (here.c == 1).astype(jnp.float32)
        for j in range(CHUNKS):

            @pl.when(jnp.logical_or(here.y == 1, here.y == 3))
            def _():
                for copy in self.up(j):
                    copy.wait_recv()

            @pl.when(here.y == 2)
            def _():
                for copy in self.down(j, False):
                    copy.wait_recv()

            heads = self.heads(j)
            before = self.below[heads].astype(jnp.float32) + self.above[heads].astype(jnp.float32)
            own, other = self.state[here.c, heads], self.part[heads]
            self.stage[heads] = (before + own * (1.0 - second)).astype(jnp.bfloat16)
            self.state_in[here.c, heads] = (before + other * second).astype(jnp.bfloat16)
            if j == 0:
                kbefore = self.kbelow[...] + self.kabove[...]
                self.kstage[...] = kbefore + self.sums[here.c] * (1.0 - second)
                self.sum_in[here.c] = kbefore + self.ksum[...] * second
            for copy in self.give(j):
                copy.start()

    def take(self):
        all_here(self.stage, self.frecv.at[0], self.here)
        all_here(self.kstage, self.frecv.at[1], self.here)

    def finish_send(self):
        for copy in self.exchange():
            copy.wait_send()
        all_sent(self.stage, self.fsend.at[0], self.here)
        all_sent(self.kstage, self.fsend.at[1], self.here)

        @pl.when(self.here.y < NY - 1)
        def _():
            all_sent(self.cout, self.usend.at[0], self.here)
            all_sent(self.kout, self.usend.at[1], self.here)

        @pl.when(jnp.logical_or(self.here.y == 0, self.here.y == 3))
        def _():
            all_sent(self.above, self.dsend.at[0], self.here)
            all_sent(self.kabove, self.dsend.at[1], self.here)


def normalise(projected, gain, out):
    def rows(r, _):
        some = pl.ds(pl.multiple_of(r * 16, 16), 16)
        wide = projected[some].astype(jnp.float32)
        scale = lax.rsqrt(jnp.mean(wide * wide, axis=1, keepdims=True) + 1e-05)
        out[some] = (wide * scale * gain[...]).astype(jnp.bfloat16)
        return 0

    lax.fori_loop(0, BLOCK // 16, rows, 0)


def whole_kernel(
    q_hbm, k_hbm, v_hbm, gain_hbm, targets, domains, wo_hbm, w_hbm, projected, small,
    queries, keys, values, gain, qf, kf, probs, numer, state, sums, part, ksum, below, kbelow, above, kabove, cout, kout,
    stage, kstage, state_in, sum_in, attended, wo, halves, given, acts, wv, tg, tcol, out_stats, in_stats, dom,
    near, xsend, xrecv, usend, urecv, downsend, downrecv, fsend, frecv, zsend, zrecv, hsend, hrecv, psend, precv,
    gsend, grecv, rsend, rrecv, rprecv, tsend, trecv, ssend, srecv, dsend, drecv,
):
    here = Place()
    for ref in (below, kbelow, above, kabove):
        ref[...] = jnp.zeros_like(ref)
    greet_all(here)
    moves = ((k_hbm, keys), (v_hbm, values), (q_hbm, queries), (gain_hbm, gain), (targets, tg.at[here.pos]))
    loads = [pltpu.make_async_copy(src, dst, near.at[2 + n]) for n, (src, dst) in enumerate(moves)]
    for load in loads:
        load.start()
    partner = here.at(c=1 - here.c)
    half = D // 2
    wo_rows = pl.ds(pl.multiple_of(here.y * 16, 16), 16)
    wo_own = wo_hbm.at[wo_rows, pl.ds(pl.multiple_of(here.c * half, half), half)]
    wo_place = wo.at[here.x, 0, here.y]
    own_wo = pltpu.make_async_copy(wo_own, wo_place, near.at[1])
    own_wo.start()

    ring = VocabRing(here, w_hbm, wv, near.at[0], rsend, rrecv, rprecv)
    loads[0].wait()
    loads[1].wait()
    local_states(keys, values, kf, state, sums)
    for load in loads[2:]:
        load.wait()
    await_all()
    for i in (2, 6, 1, 7, 4, 3, 5):
        place = NEAR.index(-i if i < 4 else NZ - i)
        to = here.at(z=lax.rem(here.z + i, NZ))
        remote(wo_own, wo.at[here.x, place, here.y], zsend, zrecv.at[0 if place < 5 else 1], to).start()
    prefix = Prefix(
        here,
        (state, sums, part, ksum, below, kbelow, above, kabove, cout, kout, stage, kstage, state_in, sum_in),
        (xsend, xrecv, usend, urecv, downsend, downrecv, fsend, frecv),
    )
    weights = PlaneGather(
        here, lambda x, y, start, count: wo.at[x, pl.ds(start, count), y],
        WO_CUTS, functools.partial(places_of_event, wo), True, psend, precv,
    )
    mine, theirs = attended.at[here.c], attended.at[1 - here.c]
    rows_over = remote(mine, mine, hsend.at[0], hrecv.at[0], partner)

    def give_targets(i, _):
        slot, peer = here.plane_peer(i)
        own = tg.at[here.pos]
        remote(own, own, tsend, trecv, peer).start()
        return 0

    for copy in prefix.exchange():
        copy.start()
    inner_blocks(0, queries, kf, values, qf, probs, numer)
    for copy in prefix.exchange():
        copy.wait_recv()
    prefix.start()
    inner_blocks(HALF_HEADS, queries, kf, values, qf, probs, numer)
    own_wo.wait()
    all_here(wo.at[0, 0:4, 0], zrecv.at[0], here)
    weights.start(1, "B1+o")
    weights.start(1, "B1-o")

    @pl.when(here.y != 2)
    def _():
        weights.start(1, "A1+")

    @pl.when(here.y != 3)
    def _():
        weights.start(1, "A1-")

    prefix.relay()

    @pl.when(here.y == 2)
    def _():
        weights.start(1, "A1+")

    @pl.when(here.y == 3)
    def _():
        weights.start(1, "A1-")

    ring.begin()
    all_here(wo.at[0, 0:3, 0], zrecv.at[1], here)
    weights.start(0, "A1+")
    weights.start(0, "A1-")
    weights.start(0, "B1+o")
    weights.start(0, "B1-o")
    lax.fori_loop(1, 16, give_targets, 0)
    weights.event(1, (1,))
    weights.event(1, (0,))
    prefix.finish()
    weights.event(2)
    prefix.take()
    outer_blocks(0, qf, probs, numer, state_in, sum_in, mine)
    ring.advance(1)
    weights.event(3)
    outer_blocks(HALF_HEADS, qf, probs, numer, state_in, sum_in, mine)
    rows_over.start()
    weights.event(4)
    target_columns(here, tg, tcol, tsend, trecv)
    weights.event(5)
    weights.event(6)
    weights.event(7)
    ring.advance(2)
    weights.event(8)
    remote(theirs, theirs, hsend.at[0], hrecv.at[0], partner).wait_recv()
    weights.event(9)

    order = [pick((0, 2, 4, 6, 7, 5, 3, 1), lax.rem(n - here.z + NZ, NZ)) for n in range(NZ)]

    def project(n, _):
        cols = pl.ds(pl.multiple_of(n * TILE, TILE), TILE)
        rows = jnp.concatenate([attended[0], attended[1]], axis=0)
        w = jnp.concatenate(
            [wo[x, place, :, :, cols].reshape(NY * 16, TILE) for x in range(NX) for place in order], axis=0
        )
        both = jnp.dot(rows, w, preferred_element_type=jnp.float32).astype(jnp.bfloat16)
        low = here.c == 0
        halves[here.c, :, cols] = jnp.where(low, both[:BLOCK], both[BLOCK:])
        given[:, cols] = jnp.where(low, both[BLOCK:], both[:BLOCK])
        remote(given.at[:, cols], halves.at[here.c, :, cols], hsend.at[1], hrecv.at[1], partner).start()
        return 0

    lax.fori_loop(0, half // TILE, project, 0)
    all_here(given, hrecv.at[1], here)
    projected[:, :half] = halves[0]
    projected[:, half:] = halves[1]
    normalise(projected, gain, acts.at[here.pos])
    gather = PlaneGather(
        here, lambda x, y, start, count: acts.at[x * NY + y, pl.ds(start, count)],
        ROW_CUTS, functools.partial(rows_of_event, acts), False, gsend, grecv,
    )
    gather.begin()
    ring.own().wait()
    ring.advance(3)
    ring.shared(False)
    vocab_part(here, gather, ring, acts, wv, tcol, out_stats, in_stats, ssend, srecv)
    losses = losses_of(here, out_stats, in_stats, ssend, srecv)
    means = domain_part(here, losses, domains, dom, dsend, drecv)
    first = lax.broadcasted_iota(jnp.int32, (8, 128), 0) == 0
    small[...] = jnp.where(first, losses, means)
    all_sent(wo.at[0, 0:7, 0], zsend, here)
    prefix.finish_send()
    all_sent(acts.at[0:15, 0:64], psend, here)
    rows_over.wait_send()
    all_sent(given, hsend.at[1], here)
    all_sent(acts.at[0:15], gsend, here)
    ring.finish_send()
    finish_sends(here, in_stats, ssend, tg, tsend, dom, dsend)


def outputs_kernel(projected, small, projected_out, loss_out, mean_out):
    projected_out[...] = projected[...]
    loss_out[...] = small[0:1]
    mean_out[...] = small[1, :DOMAINS]


def on_device(queries, keys, values, w_out, norm_gain, w_vocab, targets, domains):
    vmem = pl.BlockSpec(memory_space=pltpu.VMEM)
    dma = pltpu.SemaphoreType.DMA
    low, wide = jnp.bfloat16, jnp.float32
    anywhere = pl.BlockSpec(memory_space=pl.ANY)
    projected, small = pl.pallas_call(
        whole_kernel,
        out_shape=(
            jax.ShapeDtypeStruct((BLOCK, D), low),
            jax.ShapeDtypeStruct((8, BLOCK), wide),
        ),
        in_specs=[anywhere] * 5 + [pl.BlockSpec(memory_space=pltpu.SMEM), anywhere, anywhere],
        out_specs=(vmem, vmem),
        scratch_shapes=[
            pltpu.VMEM((BLOCK, D), low),
            pltpu.VMEM((BLOCK, D), low),
            pltpu.VMEM((BLOCK, D), low),
            pltpu.VMEM((1, D), wide),
            pltpu.VMEM((BLOCK, D), low),
            pltpu.VMEM((BLOCK, D), low),
            pltpu.VMEM((HEADS, BLOCK, BLOCK), low),
            pltpu.VMEM((BLOCK, D), wide),
            pltpu.VMEM((2, HALF_HEADS, HD, HD), wide),
            pltpu.VMEM((2, HALF_HEADS, 1, HD), wide),
            pltpu.VMEM((HALF_HEADS, HD, HD), wide),
            pltpu.VMEM((HALF_HEADS, 1, HD), wide),
            pltpu.VMEM((HALF_HEADS, HD, HD), low),
            pltpu.VMEM((HALF_HEADS, 1, HD), wide),
            pltpu.VMEM((HALF_HEADS, HD, HD), low),
            pltpu.VMEM((HALF_HEADS, 1, HD), wide),
            pltpu.VMEM((HALF_HEADS, HD, HD), low),
            pltpu.VMEM((HALF_HEADS, 1, HD), wide),
            pltpu.VMEM((HALF_HEADS, HD, HD), low),
            pltpu.VMEM((HALF_HEADS, 1, HD), wide),
            pltpu.VMEM((2, HALF_HEADS, HD, HD), low),
            pltpu.VMEM((2, HALF_HEADS, 1, HD), wide),
            pltpu.VMEM((2, BLOCK, D), low),
            pltpu.VMEM((NX, NZ, NY, 16, D // 2), low),
            pltpu.VMEM((2, BLOCK, D // 2), low),
            pltpu.VMEM((BLOCK, D // 2), low),
            pltpu.VMEM((16, BLOCK, D), low),
            pltpu.VMEM((NZ, D, TILE), low),
            pltpu.VMEM((16, 1, BLOCK), jnp.int32),
            pltpu.VMEM((16, BLOCK, BLOCK), wide),
            pltpu.VMEM((8, 2, 8, 128), wide),
            pltpu.VMEM((2, 16, 8, 128), wide),
            pltpu.VMEM((2, 16, 8, 128), wide),
            dma((7,)),
            dma((2,)),
            dma((2,)),
            dma((2,)),
            dma((CHUNKS + 1,)),
            dma((2,)),
            dma((CHUNKS + 1,)),
            dma((2,)),
            dma((2,)),
            dma(()),
            dma((2,)),
            dma((2,)),
            dma((2,)),
            dma(()),
            dma((len(EVENT) + 1,)),
            dma(()),
            dma((len(EVENT),)),
            dma(()),
            dma((4,)),
            dma((2,)),
            dma(()),
            dma(()),
            dma(()),
            dma(()),
            dma((2,)),
            dma((2,)),
        ],
        compiler_params=pltpu.CompilerParams(
            collective_id=0, has_side_effects=True, vmem_limit_bytes=60 * 1024 * 1024
        ),
    )(queries[0], keys[0], values[0], norm_gain[None], targets, domains, w_out, w_vocab)
    projected, losses, means = pl.pallas_call(
        outputs_kernel,
        out_shape=(
            jax.ShapeDtypeStruct((BLOCK, D), low),
            jax.ShapeDtypeStruct((1, BLOCK), wide),
            jax.ShapeDtypeStruct((DOMAINS,), wide),
        ),
        in_specs=[vmem, vmem],
        out_specs=(vmem, vmem, vmem),
    )(projected, small)
    return (projected[None], losses, means)


def solution(mesh):
    return jax.shard_map(
        on_device,
        mesh=mesh,
        in_specs=(
            P("doc", "seq", None),
            P("doc", "seq", None),
            P("doc", "seq", None),
            P("doc", None),
            P(),
            P(None, "doc"),
            P("doc", "seq"),
            P(),
        ),
        out_specs=(P("doc", "seq", None), P("doc", "seq"), P()),
        check_vma=False,
    )
```

```python
import functools

import jax
import jax.numpy as jnp
from jax import lax
from jax.experimental import pallas as pl
from jax.experimental.pallas import tpu as pltpu
from jax.sharding import PartitionSpec as P

HEADS = 16
HD = 128
DOMAINS = 7
BLOCK = 128
D = 2048
SHARD = 896
DOCS = 32
TILE = 256
NX, NY, NZ = 4, 4, 8
MESH = pl.DeviceIdType.MESH


class Place:
    def __init__(self):
        seq, doc = lax.axis_index("seq"), lax.axis_index("doc")
        self.y, self.c = lax.div(seq, 2), lax.rem(seq, 2)
        self.x, self.z = lax.div(doc, NZ), lax.rem(doc, NZ)
        self.pos = self.x * NY + self.y

    def at(self, x=None, y=None, z=None, c=None):
        x = self.x if x is None else x
        y = self.y if y is None else y
        z = self.z if z is None else z
        c = self.c if c is None else c
        return {"seq": y * 2 + c, "doc": x * NZ + z}

    def step(self, axis, by):
        if axis == "x":
            return self.at(x=lax.rem(self.x + by + NX, NX))
        if axis == "y":
            return self.at(y=lax.rem(self.y + by + NY, NY))
        return self.at(z=lax.rem(self.z + by + NZ, NZ))

    def slot(self, dx, dy):
        return lax.rem(self.x + dx + NX, NX) * NY + lax.rem(self.y + dy + NY, NY)

    def plane_peer(self, i):
        other = lax.rem(self.pos + i, NX * NY)
        return other, self.at(x=lax.div(other, NY), y=lax.rem(other, NY))

    def column_peer(self, i):
        mine = self.z * 2 + self.c
        other = lax.rem(mine + i, NZ * 2)
        return other, self.at(z=lax.div(other, 2), c=lax.rem(other, 2))


def remote(src, dst, send, recv, to):
    return pltpu.make_async_remote_copy(
        src_ref=src, dst_ref=dst, send_sem=send, recv_sem=recv, device_id=to, device_id_type=MESH
    )


def all_sent(ref, sem, here):
    remote(ref, ref, sem, sem, here.at(c=1 - here.c)).wait_send()


def all_here(ref, sem, here):
    remote(ref, ref, sem, sem, here.at(c=1 - here.c)).wait_recv()


def greet_all(here):
    barrier = pltpu.get_barrier_semaphore()

    def greet(i, _):
        pl.semaphore_signal(barrier, 1, device_id=here.plane_peer(i)[1], device_id_type=MESH)
        pl.semaphore_signal(barrier, 1, device_id=here.column_peer(i)[1], device_id_type=MESH)
        return 0

    lax.fori_loop(1, 16, greet, 0)


def await_all():
    pl.semaphore_wait(pltpu.get_barrier_semaphore(), 30)


class VocabRing:
    def __init__(self, here, w_hbm, wv, near, send, recv, precv):
        self.here, self.w, self.wv, self.near = here, w_hbm, wv, near
        self.send, self.recv, self.precv = send, recv, precv
        self.first = pl.multiple_of(here.c * (D // 2), D // 2)
        self.column = pl.multiple_of(jnp.minimum(here.y * TILE, SHARD - TILE), 128)

    def rows(self, part):
        if part == "lo":
            return pl.ds(self.first, D // 4)
        if part == "hi":
            return pl.ds(self.first + D // 4, D // 4)
        return pl.ds(self.first, D // 2)

    def slot(self, off):
        return lax.rem(self.here.z + off + NZ, NZ)

    def hop(self, k, by):
        part = "all" if k < 4 else ("lo" if by > 0 else "hi")
        dst = self.wv.at[self.slot(-by * (k - 1)), self.rows(part)]
        src = self.w.at[self.rows(part), pl.ds(self.column, TILE)] if k == 1 else dst
        return remote(src, dst, self.send, self.recv.at[k - 1], self.here.step("z", by))

    def share(self, k, by):
        part = "all" if k < 4 else ("lo" if by > 0 else "hi")
        ref = self.wv.at[self.slot(-by * k), self.rows(part)]
        return remote(ref, ref, self.send, self.precv.at[k // 4], self.here.at(c=1 - self.here.c))

    def own(self):
        return pltpu.make_async_copy(self.w.at[:, pl.ds(self.column, TILE)], self.wv.at[self.here.z], self.near)

    def begin(self):
        for by in (1, -1):
            self.hop(1, by).start()
        self.own().start()

    def advance(self, k):
        all_here(self.wv.at[0] if k < 4 else self.wv.at[0, : D // 2], self.recv.at[k - 1], self.here)
        for by in (1, -1):
            if k < 4:
                self.hop(k + 1, by).start()
            self.share(k, by).start()

    def shared(self, last):
        if last:
            all_here(self.wv.at[0, : D // 2], self.precv.at[1], self.here)
        else:
            all_here(self.wv.at[0:3], self.precv.at[0], self.here)

    def finish_send(self):
        all_sent(self.wv.at[0:7], self.send, self.here)


HALF = {
    "A1+": (0, 0, "all", "A", 1),
    "A1-": (0, 0, "all", "A", -1),
    "B1+o": (0, 0, "all", "B", 1),
    "B1-o": (0, 0, "all", "B", -1),
    "A2+": (-1, 0, "lo", "A", 1),
    "A2-": (1, 0, "hi", "A", -1),
    "B1+m": (-1, 0, "all", "B", 1),
    "B1-m": (-1, 0, "all", "B", -1),
    "B1+p": (1, 0, "all", "B", 1),
    "B1-p": (1, 0, "all", "B", -1),
    "B1+l": (-2, 0, "lo", "B", 1),
    "B1-l": (-2, 0, "lo", "B", -1),
    "B1+h": (2, 0, "hi", "B", 1),
    "B1-h": (2, 0, "hi", "B", -1),
    "B2+o": (0, -1, "lo", "B", 1),
    "B2-o": (0, 1, "hi", "B", -1),
    "B2+p": (1, -1, "all", "B", 1),
    "B2-m": (-1, 1, "all", "B", -1),
    "B2+l": (-2, -1, "lo", "B", 1),
    "B2-h": (2, 1, "hi", "B", -1),
}
EVENT = {
    1: (("A1+", "A1-"), ("A2+", "A2-", "B1+m", "B1-m", "B1+p", "B1-p")),
    2: (("B1+o", "B1-o"), ("B2+o", "B2-o")),
    3: (("A2+", "A2-"), ("B1+l", "B1-l", "B1+h", "B1-h")),
    4: (("B1+m", "B1-m"), ("B2-m",)),
    5: (("B1+p", "B1-p"), ("B2+p",)),
    6: (("B2+o", "B2-o"), ()),
    7: (("B1+l", "B1-l", "B1+h", "B1-h"), ("B2+l", "B2-h")),
    8: (("B2+p", "B2-m"), ()),
    9: (("B2+l", "B2-h"), ()),
}
EVENT_OF = {name: e for e, (names, _) in EVENT.items() for name in names}
WO_CUTS = ((5, 6, 8), (0, 2, 5))
ROW_CUTS = ((0, 32, 64), (64, 96, 128))


class PlaneGather:
    def __init__(self, here, view, cuts, amount, apart, send, recv):
        self.here, self.view, self.cuts, self.amount, self.apart = here, view, cuts, amount, apart
        self.send_sem, self.recv_sem = send, recv

    def start(self, half, name):
        a, b, part, axis, by = HALF[name]
        first, second = ("x", "y") if half == 0 else ("y", "x")
        dx, dy = (a, b) if half == 0 else (b, a)
        first_row, middle, last_row = self.cuts[half]
        begin, end = {"all": (first_row, last_row), "lo": (first_row, middle), "hi": (middle, last_row)}[part]
        column, row = lax.rem(self.here.x + dx + NX, NX), lax.rem(self.here.y + dy + NY, NY)
        ref = self.view(column, row, begin, end - begin)
        to = self.here.step(first if axis == "A" else second, by)
        remote(ref, ref, self.send_sem, self.recv_sem.at[self.index(EVENT_OF[name], half)], to).start()

    def index(self, e, half):
        return len(EVENT) if e == 1 and half == 1 and self.apart else e - 1

    def begin_along(self, axis):
        half = 0 if axis == "x" else 1
        for name in ("A1+", "A1-"):
            self.start(half, name)
        for name in ("B1+o", "B1-o"):
            self.start(1 - half, name)

    def begin(self):
        self.begin_along("x")
        self.begin_along("y")

    def event(self, e, halves=(0, 1)):
        apart = len(halves) == 1
        all_here(self.amount(e, halves[0] if apart else None), self.recv_sem.at[self.index(e, halves[0])], self.here)
        for name in EVENT[e][1]:
            for half in halves:
                self.start(half, name)


def rows_of_event(acts, e, half):
    blocks = {1: 2, 2: 2, 3: 1, 4: 2, 5: 2, 6: 1, 7: 2, 8: 2, 9: 1}[e]
    return acts.at[0:blocks]


def places_of_event(wo, e, half):
    if half is not None:
        return wo.at[0, 0:6, 0] if half == 0 else wo.at[0, 0:5, 0:2]
    places = {2: 4, 3: 2, 4: 4, 5: 4, 6: 2, 7: 4, 8: 4, 9: 2}[e]
    return wo.at[0, 0:places]


PIECES = (
    ((0, 0), (0, 0), (-1, 0), (0, -1)),
    ((1, 0), (0, 1), (0, -1), (-1, 0)),
    ((0, 1), (1, 0), (2, 0), (0, 2)),
    ((-1, -1), (-1, -1), (-1, 1), (1, -1)),
    ((1, -1), (-1, 1), (1, 1), (1, 1)),
    ((0, 2), (2, 0), (2, -1), (-1, 2)),
    ((2, 1), (1, 2), (-1, 2), (2, -1)),
    ((1, 2), (2, 1), (2, 2), (2, 2)),
)
EVENTS = ((1, 2, 3), (), (4,), (5,), (), (6, 7), (8,), (9,))
NEAR = (0, -1, 1, -2, 2, -3, 3, 4)


def pick(table, i):
    value = table[0]
    for n in range(1, len(table)):
        value = jnp.where(i == n, table[n], value)
    return value


def stats_of(here, acts, wv, tcol, slots):
    rows = 2 * BLOCK
    lane = lax.broadcasted_iota(jnp.int32, (rows, 128), 1)
    whole = here.y < NY - 1
    column = jnp.minimum(here.y * TILE, SHARD - TILE)
    middle = BLOCK // 2

    def joined(ref):
        return jnp.concatenate(
            [ref[slot, (n % 2) * middle : (n % 2 + 1) * middle] for n, slot in enumerate(slots)], axis=0
        )

    wanted = joined(tcol) - lane.astype(jnp.float32)

    def tile(n, carry):
        top, total, hit = carry
        shard = lax.rem(here.z + NEAR[n] + NZ, NZ)
        logits = jnp.dot(joined(acts), wv[shard], preferred_element_type=jnp.float32)
        base = ((here.x * NZ + shard) * SHARD + column).astype(jnp.float32)
        one, two = logits[:, :128], logits[:, 128:]
        now = jnp.maximum(top, jnp.maximum(jnp.where(whole, one, two), two))
        add = jnp.exp(one - now)
        total = total * jnp.exp(top - now) + jnp.exp(two - now) + jnp.where(whole, add, 0.0)
        hit = hit + jnp.where(wanted == jnp.where(whole, base, -1e6), one, 0.0)
        hit = hit + jnp.where(wanted == base + 128.0, two, 0.0)
        return now, total, hit

    carry = (
        jnp.full((rows, 128), -jnp.inf, jnp.float32),
        jnp.zeros((rows, 128), jnp.float32),
        jnp.zeros((rows, 128), jnp.float32),
    )
    for n in range(NZ):
        carry = tile(n, carry)
    top, total, hit = carry
    peak = jnp.max(top, axis=1, keepdims=True)
    total = jnp.sum(total * jnp.exp(top - peak), axis=1, keepdims=True)
    hit = jnp.sum(hit, axis=1, keepdims=True)
    return jnp.where(lane == 0, peak, jnp.where(lane == 1, total, jnp.where(lane == 2, hit, 0.0)))


def target_columns(here, tg, tcol, tsend, trecv):
    def columns(slot):
        wide = jnp.broadcast_to(tg[slot].astype(jnp.float32), (BLOCK, BLOCK))
        tcol[slot] = wide.T

    def take_targets(i, _):
        columns(i)
        return 0

    all_here(tg.at[0:15], trecv, here)
    lax.fori_loop(0, 16, take_targets, 0)


def stat_copies(here, i, pair, slots, out_stats, in_stats, ssend, srecv):
    for half in (0, 1):
        slot = slots[2 * pair + half]
        to = here.at(x=lax.div(slot, NY), y=lax.rem(slot, NY))
        yield remote(
            out_stats.at[i, pair], in_stats.at[half, here.pos], ssend, srecv, to
        )


def slots_of(here, i):
    return [
        here.slot(pick([four[n][0] for four in PIECES], i), pick([four[n][1] for four in PIECES], i)) for n in range(4)
    ]


def vocab_part(here, gather, ring, acts, wv, tcol, out_stats, in_stats, ssend, srecv):
    def batch(i, _):
        for n, events in enumerate(EVENTS):
            if events:

                @pl.when(i == n)
                def _():
                    for e in events:
                        gather.event(e)
                        if e == 1:
                            ring.advance(3)
                    if n == 0:
                        ring.shared(False)
                        ring.advance(4)
                        ring.shared(True)

        slots = slots_of(here, i)
        table = stats_of(here, acts, wv, tcol, slots)
        for pair in (0, 1):
            out_stats[i, pair] = table[pair * BLOCK : (pair + 1) * BLOCK].T[:8]

        @pl.when(i > 0)
        def _():
            for copy in stat_copies(here, i, 0, slots, out_stats, in_stats, ssend, srecv):
                copy.start()

        for copy in stat_copies(here, i, 1, slots, out_stats, in_stats, ssend, srecv):
            copy.start()
        return 0

    lax.fori_loop(0, len(PIECES), batch, 0)


def losses_of(here, out_stats, in_stats, ssend, srecv):
    for half in (0, 1):
        in_stats[half, here.pos] = out_stats[0, 0]

    all_here(in_stats.at[:, 0:15], srecv, here)
    early = lax.broadcasted_iota(jnp.int32, (8, BLOCK), 1) < BLOCK // 2
    stats = [jnp.where(early, in_stats[0, n], in_stats[1, n]) for n in range(16)]
    top = functools.reduce(jnp.maximum, [s[0:1] for s in stats])
    total = sum(s[1:2] * jnp.exp(s[0:1] - top) for s in stats)
    hit = sum(s[2:3] for s in stats)
    return top + jnp.log(total) - hit


def domain_part(here, losses, domains, dom, dsend, drecv):
    lane = lax.broadcasted_iota(jnp.int32, (8, 128), 1)
    mine = domains[here.x * NZ + here.z]
    value = jnp.broadcast_to(jnp.sum(losses, axis=1, keepdims=True), (8, 128))
    value = jnp.where(lane == mine, value, 0.0)
    for stage in (0, 1):
        peers = here.plane_peer if stage == 0 else here.column_peer
        own = here.pos if stage == 0 else here.z * 2 + here.c
        dom[stage, own] = value

        def give(i, _):
            slot, peer = peers(i)
            remote(dom.at[stage, own], dom.at[stage, own], dsend.at[stage], drecv.at[stage], peer).start()
            return 0

        lax.fori_loop(1, 16, give, 0)
        all_here(dom.at[stage, 0:15], drecv.at[stage], here)
        value = sum(dom[stage, n] for n in range(16))
    counts = jnp.zeros((8, 128), jnp.float32)
    for n in range(DOCS):
        counts = counts + jnp.where(lane == domains[n], 1.0, 0.0)
    return value / jnp.maximum(counts * (NY * 2 * BLOCK), 1.0)


def finish_sends(here, in_stats, ssend, tg, tsend, dom, dsend):
    all_sent(in_stats.at[:, 0:15], ssend, here)
    all_sent(tg.at[0:15], tsend, here)
    for stage in (0, 1):
        all_sent(dom.at[stage, 0:15], dsend.at[stage], here)


HALF_HEADS = HEADS // 2
CHUNKS = 4
PER = HALF_HEADS // CHUNKS


def feature(inputs):
    wide = inputs.astype(jnp.float32)
    return jnp.where(wide > 0.0, wide + 1.0, jnp.exp(jnp.minimum(wide, 0.0))).astype(jnp.bfloat16)


def head_slice(h):
    return pl.ds(pl.multiple_of(h * HD, HD), HD)


def by_four(one, count):
    def turn(t, _):
        for n in range(4):
            one(t * 4 + n, 0)
        return 0

    lax.fori_loop(0, count // 4, turn, 0)


def local_states(keys, values, kf, state, sums):
    def one(h, _):
        cols = head_slice(h)
        feat = feature(keys[:, cols])
        kf[:, cols] = feat
        group, n = lax.div(h, HALF_HEADS), lax.rem(h, HALF_HEADS)
        state[group, n] = lax.dot_general(
            feat, values[:, cols], (((0,), (0,)), ((), ())), preferred_element_type=jnp.float32
        )
        sums[group, n] = jnp.sum(feat.astype(jnp.float32), axis=0, keepdims=True)
        return 0

    by_four(one, HEADS)


def inner_blocks(first, queries, kf, values, qf, probs, numer):
    row = lax.broadcasted_iota(jnp.int32, (BLOCK, BLOCK), 0)
    causal = row >= lax.broadcasted_iota(jnp.int32, (BLOCK, BLOCK), 1)

    def one(n, _):
        h = first + n
        cols = head_slice(h)
        feat = feature(queries[:, cols])
        qf[:, cols] = feat
        scores = lax.dot_general(feat, kf[:, cols], (((1,), (1,)), ((), ())), preferred_element_type=jnp.float32)
        prob = jnp.where(causal, scores, 0.0).astype(jnp.bfloat16)
        probs[h] = prob
        numer[:, cols] = jnp.dot(prob, values[:, cols], preferred_element_type=jnp.float32)
        return 0

    by_four(one, HALF_HEADS)


def outer_blocks(first, qf, probs, numer, state_in, sum_in, out):
    def one(n, _):
        h = first + n
        cols = head_slice(h)
        group, n = lax.div(h, HALF_HEADS), lax.rem(h, HALF_HEADS)
        feat = qf[:, cols]
        top = numer[:, cols] + jnp.dot(feat, state_in[group, n], preferred_element_type=jnp.float32)
        below = probs[h].astype(jnp.float32) + feat.astype(jnp.float32) * sum_in[group, n]
        out[:, cols] = (top / jnp.sum(below, axis=1, keepdims=True)).astype(jnp.bfloat16)
        return 0

    by_four(one, HALF_HEADS)


class Prefix:
    def __init__(self, here, refs, sems):
        self.here = here
        (self.state, self.sums, self.part, self.ksum, self.below, self.kbelow, self.above, self.kabove, self.cout, self.kout,
         self.stage, self.kstage, self.state_in, self.sum_in) = refs
        (self.xsend, self.xrecv, self.usend, self.urecv, self.dsend, self.drecv, self.fsend, self.frecv) = sems
        self.partner = here.at(c=1 - here.c)

    def exchange(self):
        other = 1 - self.here.c
        return (
            remote(self.state.at[other], self.part, self.xsend.at[0], self.xrecv.at[0], self.partner),
            remote(self.sums.at[other], self.ksum, self.xsend.at[1], self.xrecv.at[1], self.partner),
        )

    def heads(self, j):
        return pl.ds(j * PER, PER)

    def move(self, j, src, ksrc, dst, kdst, send, recv, to):
        heads = self.heads(j)
        copies = [remote(src.at[heads], dst.at[heads], send.at[0], recv.at[j], to)]
        if j == 0:
            copies.append(remote(ksrc, kdst, send.at[1], recv.at[CHUNKS], to))
        return copies

    def up(self, j):
        return self.move(
            j, self.cout, self.kout, self.below, self.kbelow, self.usend, self.urecv, self.here.step("y", 1)
        )

    def down(self, j, relay):
        src, ksrc = (self.above, self.kabove) if relay else (self.cout, self.kout)
        return self.move(j, src, ksrc, self.above, self.kabove, self.dsend, self.drecv, self.here.step("y", -1))

    def total(self, j, add):
        heads = self.heads(j)
        value = self.state[self.here.c, heads] + self.part[heads]
        if add:
            value = value + self.below[heads].astype(jnp.float32)
        self.cout[heads] = value.astype(jnp.bfloat16)
        if j == 0:
            value = self.sums[self.here.c] + self.ksum[...]
            self.kout[...] = value + self.kbelow[...] if add else value

    def start(self):
        @pl.when(self.here.y < 2)
        def _():
            for j in range(CHUNKS):
                self.total(j, False)
                for copy in self.up(j):
                    copy.start()

                @pl.when(self.here.y == 0)
                def _():
                    for copy in self.down(j, False):
                        copy.start()

    def relay(self):
        @pl.when(self.here.y == 2)
        def _():
            for j in range(CHUNKS):
                for copy in self.up(j):
                    copy.wait_recv()
                self.total(j, True)
                for copy in self.up(j):
                    copy.start()

        @pl.when(self.here.y == 3)
        def _():
            for j in range(CHUNKS):
                for copy in self.down(j, False):
                    copy.wait_recv()
                for copy in self.down(j, True):
                    copy.start()

    def give(self, j):
        heads = self.heads(j)
        there = self.state_in.at[self.here.c, heads]
        copies = [remote(self.stage.at[heads], there, self.fsend.at[0], self.frecv.at[0], self.partner)]
        if j == 0:
            copies.append(
                remote(self.kstage, self.sum_in.at[self.here.c], self.fsend.at[1], self.frecv.at[1], self.partner)
            )
        return copies

    def finish(self):
        here = self.here
        second = (here.c == 1).astype(jnp.float32)
        for j in range(CHUNKS):

            @pl.when(jnp.logical_or(here.y == 1, here.y == 3))
            def _():
                for copy in self.up(j):
                    copy.wait_recv()

            @pl.when(here.y == 2)
            def _():
                for copy in self.down(j, False):
                    copy.wait_recv()

            heads = self.heads(j)
            before = self.below[heads].astype(jnp.float32) + self.above[heads].astype(jnp.float32)
            own, other = self.state[here.c, heads], self.part[heads]
            self.stage[heads] = (before + own * (1.0 - second)).astype(jnp.bfloat16)
            self.state_in[here.c, heads] = (before + other * second).astype(jnp.bfloat16)
            if j == 0:
                kbefore = self.kbelow[...] + self.kabove[...]
                self.kstage[...] = kbefore + self.sums[here.c] * (1.0 - second)
                self.sum_in[here.c] = kbefore + self.ksum[...] * second
            for copy in self.give(j):
                copy.start()

    def take(self):
        all_here(self.stage, self.frecv.at[0], self.here)
        all_here(self.kstage, self.frecv.at[1], self.here)

    def finish_send(self):
        for copy in self.exchange():
            copy.wait_send()
        all_sent(self.stage, self.fsend.at[0], self.here)
        all_sent(self.kstage, self.fsend.at[1], self.here)

        @pl.when(self.here.y < NY - 1)
        def _():
            all_sent(self.cout, self.usend.at[0], self.here)
            all_sent(self.kout, self.usend.at[1], self.here)

        @pl.when(jnp.logical_or(self.here.y == 0, self.here.y == 3))
        def _():
            all_sent(self.above, self.dsend.at[0], self.here)
            all_sent(self.kabove, self.dsend.at[1], self.here)


def normalise(projected, gain, out):
    def rows(r, _):
        some = pl.ds(pl.multiple_of(r * 16, 16), 16)
        wide = projected[some].astype(jnp.float32)
        scale = lax.rsqrt(jnp.mean(wide * wide, axis=1, keepdims=True) + 1e-05)
        out[some] = (wide * scale * gain[...]).astype(jnp.bfloat16)
        return 0

    lax.fori_loop(0, BLOCK // 16, rows, 0)


def whole_kernel(
    q_hbm, k_hbm, v_hbm, gain_hbm, targets, domains, wo_hbm, w_hbm, projected, small,
    queries, keys, values, gain, qf, kf, probs, numer, state, sums, part, ksum, below, kbelow, above, kabove, cout, kout,
    stage, kstage, state_in, sum_in, attended, wo, halves, given, acts, wv, tg, tcol, out_stats, in_stats, dom,
    near, xsend, xrecv, usend, urecv, downsend, downrecv, fsend, frecv, zsend, zrecv, hsend, hrecv, psend, precv,
    gsend, grecv, rsend, rrecv, rprecv, tsend, trecv, ssend, srecv, dsend, drecv,
):
    here = Place()
    for ref in (below, kbelow, above, kabove):
        ref[...] = jnp.zeros_like(ref)
    greet_all(here)
    moves = ((k_hbm, keys), (v_hbm, values), (q_hbm, queries), (gain_hbm, gain), (targets, tg.at[here.pos]))
    loads = [pltpu.make_async_copy(src, dst, near.at[2 + n]) for n, (src, dst) in enumerate(moves)]
    for load in loads:
        load.start()
    partner = here.at(c=1 - here.c)
    half = D // 2
    wo_rows = pl.ds(pl.multiple_of(here.y * 16, 16), 16)
    wo_own = wo_hbm.at[wo_rows, pl.ds(pl.multiple_of(here.c * half, half), half)]
    wo_place = wo.at[here.x, 0, here.y]
    own_wo = pltpu.make_async_copy(wo_own, wo_place, near.at[1])
    own_wo.start()

    ring = VocabRing(here, w_hbm, wv, near.at[0], rsend, rrecv, rprecv)
    loads[0].wait()
    loads[1].wait()
    local_states(keys, values, kf, state, sums)
    for load in loads[2:]:
        load.wait()
    await_all()
    def wo_give(*steps):
        for i in steps:
            place = NEAR.index(-i if i < 4 else NZ - i)
            to = here.at(z=lax.rem(here.z + i, NZ))
            remote(wo_own, wo.at[here.x, place, here.y], zsend, zrecv.at[0 if place < 5 else 1], to).start()

    wo_give(2, 6, 1, 7)
    prefix = Prefix(
        here,
        (state, sums, part, ksum, below, kbelow, above, kabove, cout, kout, stage, kstage, state_in, sum_in),
        (xsend, xrecv, usend, urecv, downsend, downrecv, fsend, frecv),
    )
    weights = PlaneGather(
        here, lambda x, y, start, count: wo.at[x, pl.ds(start, count), y],
        WO_CUTS, functools.partial(places_of_event, wo), True, psend, precv,
    )
    mine, theirs = attended.at[here.c], attended.at[1 - here.c]
    rows_over = remote(mine, mine, hsend.at[0], hrecv.at[0], partner)

    def give_targets(i, _):
        slot, peer = here.plane_peer(i)
        own = tg.at[here.pos]
        remote(own, own, tsend, trecv, peer).start()
        return 0

    for copy in prefix.exchange():
        copy.start()
    inner_blocks(0, queries, kf, values, qf, probs, numer)
    for copy in prefix.exchange():
        copy.wait_recv()
    prefix.start()
    wo_give(4, 3, 5)
    ring.begin()
    inner_blocks(HALF_HEADS, queries, kf, values, qf, probs, numer)
    own_wo.wait()
    all_here(wo.at[0, 0:4, 0], zrecv.at[0], here)
    weights.start(1, "B1+o")
    weights.start(1, "B1-o")
    weights.start(1, "A1+")
    weights.start(1, "A1-")
    prefix.relay()
    all_here(wo.at[0, 0:3, 0], zrecv.at[1], here)
    weights.start(0, "A1+")
    weights.start(0, "A1-")
    weights.start(0, "B1+o")
    weights.start(0, "B1-o")
    lax.fori_loop(1, 16, give_targets, 0)
    weights.event(1, (1,))
    weights.event(1, (0,))
    weights.event(2)
    ring.advance(1)
    weights.event(3)
    prefix.finish()
    prefix.take()
    outer_blocks(0, qf, probs, numer, state_in, sum_in, mine)
    outer_blocks(HALF_HEADS, qf, probs, numer, state_in, sum_in, mine)
    rows_over.start()
    weights.event(4)
    target_columns(here, tg, tcol, tsend, trecv)
    weights.event(5)
    weights.event(6)
    weights.event(7)
    weights.event(8)
    remote(theirs, theirs, hsend.at[0], hrecv.at[0], partner).wait_recv()
    weights.event(9)

    order = [pick((0, 2, 4, 6, 7, 5, 3, 1), lax.rem(n - here.z + NZ, NZ)) for n in range(NZ)]

    def project(n, _):
        cols = pl.ds(pl.multiple_of(n * TILE, TILE), TILE)
        rows = jnp.concatenate([attended[0], attended[1]], axis=0)
        w = jnp.concatenate(
            [wo[x, place, :, :, cols].reshape(NY * 16, TILE) for x in range(NX) for place in order], axis=0
        )
        both = jnp.dot(rows, w, preferred_element_type=jnp.float32).astype(jnp.bfloat16)
        low = here.c == 0
        halves[here.c, :, cols] = jnp.where(low, both[:BLOCK], both[BLOCK:])
        given[:, cols] = jnp.where(low, both[BLOCK:], both[:BLOCK])
        remote(given.at[:, cols], halves.at[here.c, :, cols], hsend.at[1], hrecv.at[1], partner).start()
        return 0

    lax.fori_loop(0, half // TILE, project, 0)
    all_here(given, hrecv.at[1], here)
    projected[:, :half] = halves[0]
    projected[:, half:] = halves[1]
    normalise(projected, gain, acts.at[here.pos])
    gather = PlaneGather(
        here, lambda x, y, start, count: acts.at[x * NY + y, pl.ds(start, count)],
        ROW_CUTS, functools.partial(rows_of_event, acts), False, gsend, grecv,
    )
    gather.begin()
    ring.own().wait()
    ring.advance(2)
    vocab_part(here, gather, ring, acts, wv, tcol, out_stats, in_stats, ssend, srecv)
    losses = losses_of(here, out_stats, in_stats, ssend, srecv)
    means = domain_part(here, losses, domains, dom, dsend, drecv)
    first = lax.broadcasted_iota(jnp.int32, (8, 128), 0) == 0
    small[...] = jnp.where(first, losses, means)
    all_sent(wo.at[0, 0:7, 0], zsend, here)
    prefix.finish_send()
    all_sent(acts.at[0:15, 0:64], psend, here)
    rows_over.wait_send()
    all_sent(given, hsend.at[1], here)
    all_sent(acts.at[0:15], gsend, here)
    ring.finish_send()
    finish_sends(here, in_stats, ssend, tg, tsend, dom, dsend)


def outputs_kernel(projected, small, projected_out, loss_out, mean_out):
    projected_out[...] = projected[...]
    loss_out[...] = small[0:1]
    mean_out[...] = small[1, :DOMAINS]


def on_device(queries, keys, values, w_out, norm_gain, w_vocab, targets, domains):
    vmem = pl.BlockSpec(memory_space=pltpu.VMEM)
    dma = pltpu.SemaphoreType.DMA
    low, wide = jnp.bfloat16, jnp.float32
    anywhere = pl.BlockSpec(memory_space=pl.ANY)
    projected, small = pl.pallas_call(
        whole_kernel,
        out_shape=(
            jax.ShapeDtypeStruct((BLOCK, D), low),
            jax.ShapeDtypeStruct((8, BLOCK), wide),
        ),
        in_specs=[anywhere] * 5 + [pl.BlockSpec(memory_space=pltpu.SMEM), anywhere, anywhere],
        out_specs=(vmem, vmem),
        scratch_shapes=[
            pltpu.VMEM((BLOCK, D), low),
            pltpu.VMEM((BLOCK, D), low),
            pltpu.VMEM((BLOCK, D), low),
            pltpu.VMEM((1, D), wide),
            pltpu.VMEM((BLOCK, D), low),
            pltpu.VMEM((BLOCK, D), low),
            pltpu.VMEM((HEADS, BLOCK, BLOCK), low),
            pltpu.VMEM((BLOCK, D), wide),
            pltpu.VMEM((2, HALF_HEADS, HD, HD), wide),
            pltpu.VMEM((2, HALF_HEADS, 1, HD), wide),
            pltpu.VMEM((HALF_HEADS, HD, HD), wide),
            pltpu.VMEM((HALF_HEADS, 1, HD), wide),
            pltpu.VMEM((HALF_HEADS, HD, HD), low),
            pltpu.VMEM((HALF_HEADS, 1, HD), wide),
            pltpu.VMEM((HALF_HEADS, HD, HD), low),
            pltpu.VMEM((HALF_HEADS, 1, HD), wide),
            pltpu.VMEM((HALF_HEADS, HD, HD), low),
            pltpu.VMEM((HALF_HEADS, 1, HD), wide),
            pltpu.VMEM((HALF_HEADS, HD, HD), low),
            pltpu.VMEM((HALF_HEADS, 1, HD), wide),
            pltpu.VMEM((2, HALF_HEADS, HD, HD), low),
            pltpu.VMEM((2, HALF_HEADS, 1, HD), wide),
            pltpu.VMEM((2, BLOCK, D), low),
            pltpu.VMEM((NX, NZ, NY, 16, D // 2), low),
            pltpu.VMEM((2, BLOCK, D // 2), low),
            pltpu.VMEM((BLOCK, D // 2), low),
            pltpu.VMEM((16, BLOCK, D), low),
            pltpu.VMEM((NZ, D, TILE), low),
            pltpu.VMEM((16, 1, BLOCK), jnp.int32),
            pltpu.VMEM((16, BLOCK, BLOCK), wide),
            pltpu.VMEM((8, 2, 8, 128), wide),
            pltpu.VMEM((2, 16, 8, 128), wide),
            pltpu.VMEM((2, 16, 8, 128), wide),
            dma((7,)),
            dma((2,)),
            dma((2,)),
            dma((2,)),
            dma((CHUNKS + 1,)),
            dma((2,)),
            dma((CHUNKS + 1,)),
            dma((2,)),
            dma((2,)),
            dma(()),
            dma((2,)),
            dma((2,)),
            dma((2,)),
            dma(()),
            dma((len(EVENT) + 1,)),
            dma(()),
            dma((len(EVENT),)),
            dma(()),
            dma((4,)),
            dma((2,)),
            dma(()),
            dma(()),
            dma(()),
            dma(()),
            dma((2,)),
            dma((2,)),
        ],
        compiler_params=pltpu.CompilerParams(
            collective_id=0, has_side_effects=True, vmem_limit_bytes=60 * 1024 * 1024
        ),
    )(queries[0], keys[0], values[0], norm_gain[None], targets, domains, w_out, w_vocab)
    projected, losses, means = pl.pallas_call(
        outputs_kernel,
        out_shape=(
            jax.ShapeDtypeStruct((BLOCK, D), low),
            jax.ShapeDtypeStruct((1, BLOCK), wide),
            jax.ShapeDtypeStruct((DOMAINS,), wide),
        ),
        in_specs=[vmem, vmem],
        out_specs=(vmem, vmem, vmem),
    )(projected, small)
    return (projected[None], losses, means)


def solution(mesh):
    return jax.shard_map(
        on_device,
        mesh=mesh,
        in_specs=(
            P("doc", "seq", None),
            P("doc", "seq", None),
            P("doc", "seq", None),
            P("doc", None),
            P(),
            P(None, "doc"),
            P("doc", "seq"),
            P(),
        ),
        out_specs=(P("doc", "seq", None), P("doc", "seq"), P()),
        check_vma=False,
    )
```

```python
import functools

import jax
import jax.numpy as jnp
from jax import lax
from jax.experimental import pallas as pl
from jax.experimental.pallas import tpu as pltpu
from jax.sharding import PartitionSpec as P

HEADS = 16
HD = 128
DOMAINS = 7
BLOCK = 128
D = 2048
SHARD = 896
DOCS = 32
TILE = 256
NX, NY, NZ = 4, 4, 8
MESH = pl.DeviceIdType.MESH


def around(count):
    return [(n + count // 2 - 1) % count - (count // 2 - 1) for n in range(count)]


PLANE = sorted(
    ((dx, dy) for dx in around(NX) for dy in around(NY) if (dx, dy) != (0, 0)), key=lambda at: -abs(at[0]) - abs(at[1])
)
COLUMN = sorted(
    ((dz, dc) for dz in around(NZ) for dc in (0, 1) if (dz, dc) != (0, 0)), key=lambda at: -2 * abs(at[0]) - at[1]
)


class Place:
    def __init__(self):
        seq, doc = lax.axis_index("seq"), lax.axis_index("doc")
        self.y, self.c = lax.div(seq, 2), lax.rem(seq, 2)
        self.x, self.z = lax.div(doc, NZ), lax.rem(doc, NZ)
        self.pos = self.x * NY + self.y

    def at(self, x=None, y=None, z=None, c=None):
        x = self.x if x is None else x
        y = self.y if y is None else y
        z = self.z if z is None else z
        c = self.c if c is None else c
        return {"seq": y * 2 + c, "doc": x * NZ + z}

    def step(self, axis, by):
        if axis == "x":
            return self.at(x=lax.rem(self.x + by + NX, NX))
        if axis == "y":
            return self.at(y=lax.rem(self.y + by + NY, NY))
        return self.at(z=lax.rem(self.z + by + NZ, NZ))

    def slot(self, dx, dy):
        return lax.rem(self.x + dx + NX, NX) * NY + lax.rem(self.y + dy + NY, NY)

    def plane_peer(self, i):
        other = lax.rem(self.pos + i, NX * NY)
        return other, self.at(x=lax.div(other, NY), y=lax.rem(other, NY))

    def plane_at(self, dx, dy):
        return self.at(x=lax.rem(self.x + dx + NX, NX), y=lax.rem(self.y + dy + NY, NY))

    def column_at(self, dz, dc):
        return self.at(z=lax.rem(self.z + dz + NZ, NZ), c=lax.rem(self.c + dc, 2))


def remote(src, dst, send, recv, to):
    return pltpu.make_async_remote_copy(
        src_ref=src, dst_ref=dst, send_sem=send, recv_sem=recv, device_id=to, device_id_type=MESH
    )


def all_sent(ref, sem, here):
    remote(ref, ref, sem, sem, here.at(c=1 - here.c)).wait_send()


def all_here(ref, sem, here):
    remote(ref, ref, sem, sem, here.at(c=1 - here.c)).wait_recv()


def greet_all(here):
    barrier = pltpu.get_barrier_semaphore()

    for near, far in zip(PLANE, COLUMN):
        pl.semaphore_signal(barrier, 1, device_id=here.column_at(*far), device_id_type=MESH)
        pl.semaphore_signal(barrier, 1, device_id=here.plane_at(*near), device_id_type=MESH)


def await_all():
    pl.semaphore_wait(pltpu.get_barrier_semaphore(), 30)


class VocabRing:
    def __init__(self, here, w_hbm, wv, near, send, recv, precv):
        self.here, self.w, self.wv, self.near = here, w_hbm, wv, near
        self.send, self.recv, self.precv = send, recv, precv
        self.first = pl.multiple_of(here.c * (D // 2), D // 2)
        self.column = pl.multiple_of(jnp.minimum(here.y * TILE, SHARD - TILE), 128)

    def rows(self, part):
        if part == "lo":
            return pl.ds(self.first, D // 4)
        if part == "hi":
            return pl.ds(self.first + D // 4, D // 4)
        return pl.ds(self.first, D // 2)

    def slot(self, off):
        return lax.rem(self.here.z + off + NZ, NZ)

    def hop(self, k, by):
        part = "all" if k < 4 else ("lo" if by > 0 else "hi")
        dst = self.wv.at[self.slot(-by * (k - 1)), self.rows(part)]
        src = self.w.at[self.rows(part), pl.ds(self.column, TILE)] if k == 1 else dst
        return remote(src, dst, self.send, self.recv.at[k - 1], self.here.step("z", by))

    def share(self, k, by):
        part = "all" if k < 4 else ("lo" if by > 0 else "hi")
        ref = self.wv.at[self.slot(-by * k), self.rows(part)]
        return remote(ref, ref, self.send, self.precv.at[k // 4], self.here.at(c=1 - self.here.c))

    def own(self):
        return pltpu.make_async_copy(self.w.at[:, pl.ds(self.column, TILE)], self.wv.at[self.here.z], self.near)

    def begin(self):
        for by in (1, -1):
            self.hop(1, by).start()
        self.own().start()

    def advance(self, k):
        all_here(self.wv.at[0] if k < 4 else self.wv.at[0, : D // 2], self.recv.at[k - 1], self.here)
        for by in (1, -1):
            if k < 4:
                self.hop(k + 1, by).start()
            self.share(k, by).start()

    def shared(self, last):
        if last:
            all_here(self.wv.at[0, : D // 2], self.precv.at[1], self.here)
        else:
            all_here(self.wv.at[0:3], self.precv.at[0], self.here)

    def finish_send(self):
        all_sent(self.wv.at[0:7], self.send, self.here)


HALF = {
    "A1+": (0, 0, "all", "A", 1),
    "A1-": (0, 0, "all", "A", -1),
    "B1+o": (0, 0, "all", "B", 1),
    "B1-o": (0, 0, "all", "B", -1),
    "A2+": (-1, 0, "lo", "A", 1),
    "A2-": (1, 0, "hi", "A", -1),
    "B1+m": (-1, 0, "all", "B", 1),
    "B1-m": (-1, 0, "all", "B", -1),
    "B1+p": (1, 0, "all", "B", 1),
    "B1-p": (1, 0, "all", "B", -1),
    "B1+l": (-2, 0, "lo", "B", 1),
    "B1-l": (-2, 0, "lo", "B", -1),
    "B1+h": (2, 0, "hi", "B", 1),
    "B1-h": (2, 0, "hi", "B", -1),
    "B2+o": (0, -1, "lo", "B", 1),
    "B2-o": (0, 1, "hi", "B", -1),
    "B2+p": (1, -1, "all", "B", 1),
    "B2-m": (-1, 1, "all", "B", -1),
    "B2+l": (-2, -1, "lo", "B", 1),
    "B2-h": (2, 1, "hi", "B", -1),
}
EVENT = {
    1: (("A1+", "A1-"), ("A2+", "A2-", "B1+m", "B1-m", "B1+p", "B1-p")),
    2: (("B1+o", "B1-o"), ("B2+o", "B2-o")),
    3: (("A2+", "A2-"), ("B1+l", "B1-l", "B1+h", "B1-h")),
    4: (("B1+m", "B1-m"), ("B2-m",)),
    5: (("B1+p", "B1-p"), ("B2+p",)),
    6: (("B2+o", "B2-o"), ()),
    7: (("B1+l", "B1-l", "B1+h", "B1-h"), ("B2+l", "B2-h")),
    8: (("B2+p", "B2-m"), ()),
    9: (("B2+l", "B2-h"), ()),
}
EVENT_OF = {name: e for e, (names, _) in EVENT.items() for name in names}
WO_CUTS = ((5, 6, 8), (0, 2, 5))
ROW_CUTS = ((0, 32, 64), (64, 96, 128))


class PlaneGather:
    def __init__(self, here, view, cuts, amount, apart, send, recv):
        self.here, self.view, self.cuts, self.amount, self.apart = here, view, cuts, amount, apart
        self.send_sem, self.recv_sem = send, recv

    def start(self, half, name):
        a, b, part, axis, by = HALF[name]
        first, second = ("x", "y") if half == 0 else ("y", "x")
        dx, dy = (a, b) if half == 0 else (b, a)
        first_row, middle, last_row = self.cuts[half]
        begin, end = {"all": (first_row, last_row), "lo": (first_row, middle), "hi": (middle, last_row)}[part]
        column, row = lax.rem(self.here.x + dx + NX, NX), lax.rem(self.here.y + dy + NY, NY)
        ref = self.view(column, row, begin, end - begin)
        to = self.here.step(first if axis == "A" else second, by)
        remote(ref, ref, self.send_sem, self.recv_sem.at[self.index(EVENT_OF[name], half)], to).start()

    def index(self, e, half):
        return len(EVENT) if e == 1 and half == 1 and self.apart else e - 1

    def begin_along(self, axis):
        half = 0 if axis == "x" else 1
        for name in ("A1+", "A1-"):
            self.start(half, name)
        for name in ("B1+o", "B1-o"):
            self.start(1 - half, name)

    def begin(self):
        self.begin_along("x")
        self.begin_along("y")

    def event(self, e, halves=(0, 1)):
        apart = len(halves) == 1
        all_here(self.amount(e, halves[0] if apart else None), self.recv_sem.at[self.index(e, halves[0])], self.here)
        for name in EVENT[e][1]:
            for half in halves:
                self.start(half, name)


def rows_of_event(acts, e, half):
    blocks = {1: 2, 2: 2, 3: 1, 4: 2, 5: 2, 6: 1, 7: 2, 8: 2, 9: 1}[e]
    return acts.at[0:blocks]


def places_of_event(wo, e, half):
    if half is not None:
        return wo.at[0, 0:6, 0] if half == 0 else wo.at[0, 0:5, 0:2]
    places = {2: 4, 3: 2, 4: 4, 5: 4, 6: 2, 7: 4, 8: 4, 9: 2}[e]
    return wo.at[0, 0:places]


PIECES = (
    ((0, 0), (0, 0), (-1, 0), (0, -1)),
    ((1, 0), (0, 1), (0, -1), (-1, 0)),
    ((0, 1), (1, 0), (2, 0), (0, 2)),
    ((-1, -1), (-1, -1), (-1, 1), (1, -1)),
    ((1, -1), (-1, 1), (1, 1), (1, 1)),
    ((0, 2), (2, 0), (2, -1), (-1, 2)),
    ((2, 1), (1, 2), (-1, 2), (2, -1)),
    ((1, 2), (2, 1), (2, 2), (2, 2)),
)
EVENTS = ((1, 2, 3), (), (4,), (5,), (), (6, 7), (8,), (9,))
NEAR = (0, -1, 1, -2, 2, -3, 3, 4)


def pick(table, i):
    value = table[0]
    for n in range(1, len(table)):
        value = jnp.where(i == n, table[n], value)
    return value


def stats_of(here, acts, wv, tcol, slots):
    rows = 2 * BLOCK
    lane = lax.broadcasted_iota(jnp.int32, (rows, 128), 1)
    whole = here.y < NY - 1
    column = jnp.minimum(here.y * TILE, SHARD - TILE)
    middle = BLOCK // 2

    def joined(ref):
        return jnp.concatenate(
            [ref[slot, (n % 2) * middle : (n % 2 + 1) * middle] for n, slot in enumerate(slots)], axis=0
        )

    wanted = joined(tcol) - lane.astype(jnp.float32)

    def tile(n, carry):
        top, total, hit = carry
        shard = lax.rem(here.z + NEAR[n] + NZ, NZ)
        logits = jnp.dot(joined(acts), wv[shard], preferred_element_type=jnp.float32)
        base = ((here.x * NZ + shard) * SHARD + column).astype(jnp.float32)
        one, two = logits[:, :128], logits[:, 128:]
        now = jnp.maximum(top, jnp.maximum(jnp.where(whole, one, two), two))
        add = jnp.exp(one - now)
        total = total * jnp.exp(top - now) + jnp.exp(two - now) + jnp.where(whole, add, 0.0)
        hit = hit + jnp.where(wanted == jnp.where(whole, base, -1e6), one, 0.0)
        hit = hit + jnp.where(wanted == base + 128.0, two, 0.0)
        return now, total, hit

    carry = (
        jnp.full((rows, 128), -jnp.inf, jnp.float32),
        jnp.zeros((rows, 128), jnp.float32),
        jnp.zeros((rows, 128), jnp.float32),
    )
    for n in range(NZ):
        carry = tile(n, carry)
    top, total, hit = carry
    peak = jnp.max(top, axis=1, keepdims=True)
    total = jnp.sum(total * jnp.exp(top - peak), axis=1, keepdims=True)
    hit = jnp.sum(hit, axis=1, keepdims=True)
    return jnp.where(lane == 0, peak, jnp.where(lane == 1, total, jnp.where(lane == 2, hit, 0.0)))


def target_columns(here, tg, tcol, tsend, trecv):
    def columns(slot):
        wide = jnp.broadcast_to(tg[slot].astype(jnp.float32), (BLOCK, BLOCK))
        tcol[slot] = wide.T

    def take_targets(i, _):
        columns(i)
        return 0

    all_here(tg.at[0:15], trecv, here)
    lax.fori_loop(0, 16, take_targets, 0)


def stat_copies(here, i, pair, slots, out_stats, in_stats, ssend, srecv):
    for half in (0, 1):
        slot = slots[2 * pair + half]
        to = here.at(x=lax.div(slot, NY), y=lax.rem(slot, NY))
        yield remote(
            out_stats.at[i, pair], in_stats.at[half, here.pos], ssend, srecv, to
        )


def slots_of(here, i):
    return [
        here.slot(pick([four[n][0] for four in PIECES], i), pick([four[n][1] for four in PIECES], i)) for n in range(4)
    ]


def vocab_part(here, gather, ring, acts, wv, tcol, out_stats, in_stats, ssend, srecv):
    def batch(i, _):
        for n, events in enumerate(EVENTS):
            if events:

                @pl.when(i == n)
                def _():
                    for e in events:
                        gather.event(e)
                        if e == 1:
                            ring.advance(3)
                    if n == 0:
                        ring.shared(False)
                        ring.advance(4)
                        ring.shared(True)

        slots = slots_of(here, i)
        table = stats_of(here, acts, wv, tcol, slots)
        for pair in (0, 1):
            out_stats[i, pair] = table[pair * BLOCK : (pair + 1) * BLOCK].T[:8]

        @pl.when(i > 0)
        def _():
            for copy in stat_copies(here, i, 0, slots, out_stats, in_stats, ssend, srecv):
                copy.start()

        for copy in stat_copies(here, i, 1, slots, out_stats, in_stats, ssend, srecv):
            copy.start()
        return 0

    lax.fori_loop(0, len(PIECES), batch, 0)


def losses_of(here, out_stats, in_stats, ssend, srecv):
    for half in (0, 1):
        in_stats[half, here.pos] = out_stats[0, 0]

    all_here(in_stats.at[:, 0:15], srecv, here)
    early = lax.broadcasted_iota(jnp.int32, (8, BLOCK), 1) < BLOCK // 2
    stats = [jnp.where(early, in_stats[0, n], in_stats[1, n]) for n in range(16)]
    top = functools.reduce(jnp.maximum, [s[0:1] for s in stats])
    total = sum(s[1:2] * jnp.exp(s[0:1] - top) for s in stats)
    hit = sum(s[2:3] for s in stats)
    return top + jnp.log(total) - hit


def domain_part(here, losses, domains, dom, dsend, drecv):
    lane = lax.broadcasted_iota(jnp.int32, (8, 128), 1)
    mine = domains[here.x * NZ + here.z]
    value = jnp.broadcast_to(jnp.sum(losses, axis=1, keepdims=True), (8, 128))
    value = jnp.where(lane == mine, value, 0.0)
    for stage in (0, 1):
        peers = [here.plane_at(*at) for at in PLANE] if stage == 0 else [here.column_at(*at) for at in COLUMN]
        own = here.pos if stage == 0 else here.z * 2 + here.c
        dom[stage, own] = value
        for peer in peers:
            remote(dom.at[stage, own], dom.at[stage, own], dsend.at[stage], drecv.at[stage], peer).start()
        all_here(dom.at[stage, 0:15], drecv.at[stage], here)
        value = sum(dom[stage, n] for n in range(16))
    counts = jnp.zeros((8, 128), jnp.float32)
    for n in range(DOCS):
        counts = counts + jnp.where(lane == domains[n], 1.0, 0.0)
    return value / jnp.maximum(counts * (NY * 2 * BLOCK), 1.0)


def finish_sends(here, in_stats, ssend, tg, tsend, dom, dsend):
    all_sent(in_stats.at[:, 0:15], ssend, here)
    all_sent(tg.at[0:15], tsend, here)
    for stage in (0, 1):
        all_sent(dom.at[stage, 0:15], dsend.at[stage], here)


HALF_HEADS = HEADS // 2
CHUNKS = 4
PER = HALF_HEADS // CHUNKS


def feature(inputs):
    wide = inputs.astype(jnp.float32)
    return jnp.where(wide > 0.0, wide + 1.0, jnp.exp(jnp.minimum(wide, 0.0))).astype(jnp.bfloat16)


def head_slice(h):
    return pl.ds(pl.multiple_of(h * HD, HD), HD)


def by_four(one, count):
    def turn(t, _):
        for n in range(4):
            one(t * 4 + n, 0)
        return 0

    lax.fori_loop(0, count // 4, turn, 0)


def local_states(keys, values, kf, state, sums):
    def one(h, _):
        cols = head_slice(h)
        feat = feature(keys[:, cols])
        kf[:, cols] = feat
        group, n = lax.div(h, HALF_HEADS), lax.rem(h, HALF_HEADS)
        state[group, n] = lax.dot_general(
            feat, values[:, cols], (((0,), (0,)), ((), ())), preferred_element_type=jnp.float32
        )
        sums[group, n] = jnp.sum(feat.astype(jnp.float32), axis=0, keepdims=True)
        return 0

    by_four(one, HEADS)


def inner_blocks(first, queries, kf, values, qf, probs, numer):
    row = lax.broadcasted_iota(jnp.int32, (BLOCK, BLOCK), 0)
    causal = row >= lax.broadcasted_iota(jnp.int32, (BLOCK, BLOCK), 1)

    def one(n, _):
        h = first + n
        cols = head_slice(h)
        feat = feature(queries[:, cols])
        qf[:, cols] = feat
        scores = lax.dot_general(feat, kf[:, cols], (((1,), (1,)), ((), ())), preferred_element_type=jnp.float32)
        prob = jnp.where(causal, scores, 0.0).astype(jnp.bfloat16)
        probs[h] = prob
        numer[:, cols] = jnp.dot(prob, values[:, cols], preferred_element_type=jnp.float32)
        return 0

    by_four(one, HALF_HEADS)


def outer_blocks(first, qf, probs, numer, state_in, sum_in, out):
    def one(n, _):
        h = first + n
        cols = head_slice(h)
        group, n = lax.div(h, HALF_HEADS), lax.rem(h, HALF_HEADS)
        feat = qf[:, cols]
        top = numer[:, cols] + jnp.dot(feat, state_in[group, n], preferred_element_type=jnp.float32)
        below = probs[h].astype(jnp.float32) + feat.astype(jnp.float32) * sum_in[group, n]
        out[:, cols] = (top / jnp.sum(below, axis=1, keepdims=True)).astype(jnp.bfloat16)
        return 0

    by_four(one, HALF_HEADS)


class Prefix:
    def __init__(self, here, refs, sems):
        self.here = here
        (self.state, self.sums, self.part, self.ksum, self.below, self.kbelow, self.above, self.kabove, self.cout, self.kout,
         self.stage, self.kstage, self.state_in, self.sum_in) = refs
        (self.xsend, self.xrecv, self.usend, self.urecv, self.dsend, self.drecv, self.fsend, self.frecv) = sems
        self.partner = here.at(c=1 - here.c)

    def exchange(self):
        other = 1 - self.here.c
        return (
            remote(self.state.at[other], self.part, self.xsend.at[0], self.xrecv.at[0], self.partner),
            remote(self.sums.at[other], self.ksum, self.xsend.at[1], self.xrecv.at[1], self.partner),
        )

    def heads(self, j):
        return pl.ds(j * PER, PER)

    def move(self, j, src, ksrc, dst, kdst, send, recv, to):
        heads = self.heads(j)
        copies = [remote(src.at[heads], dst.at[heads], send.at[0], recv.at[j], to)]
        if j == 0:
            copies.append(remote(ksrc, kdst, send.at[1], recv.at[CHUNKS], to))
        return copies

    def up(self, j):
        return self.move(
            j, self.cout, self.kout, self.below, self.kbelow, self.usend, self.urecv, self.here.step("y", 1)
        )

    def down(self, j, relay):
        src, ksrc = (self.above, self.kabove) if relay else (self.cout, self.kout)
        return self.move(j, src, ksrc, self.above, self.kabove, self.dsend, self.drecv, self.here.step("y", -1))

    def total(self, j, add):
        heads = self.heads(j)
        value = self.state[self.here.c, heads] + self.part[heads]
        if add:
            value = value + self.below[heads].astype(jnp.float32)
        self.cout[heads] = value.astype(jnp.bfloat16)
        if j == 0:
            value = self.sums[self.here.c] + self.ksum[...]
            self.kout[...] = value + self.kbelow[...] if add else value

    def start(self):
        @pl.when(self.here.y < 2)
        def _():
            for j in range(CHUNKS):
                self.total(j, False)
                for copy in self.up(j):
                    copy.start()

                @pl.when(self.here.y == 0)
                def _():
                    for copy in self.down(j, False):
                        copy.start()

    def relay(self):
        @pl.when(self.here.y == 2)
        def _():
            for j in range(CHUNKS):
                for copy in self.up(j):
                    copy.wait_recv()
                self.total(j, True)
                for copy in self.up(j):
                    copy.start()

        @pl.when(self.here.y == 3)
        def _():
            for j in range(CHUNKS):
                for copy in self.down(j, False):
                    copy.wait_recv()
                for copy in self.down(j, True):
                    copy.start()

    def give(self, j):
        heads = self.heads(j)
        there = self.state_in.at[self.here.c, heads]
        copies = [remote(self.stage.at[heads], there, self.fsend.at[0], self.frecv.at[0], self.partner)]
        if j == 0:
            copies.append(
                remote(self.kstage, self.sum_in.at[self.here.c], self.fsend.at[1], self.frecv.at[1], self.partner)
            )
        return copies

    def finish(self):
        here = self.here
        second = (here.c == 1).astype(jnp.float32)
        for j in range(CHUNKS):

            @pl.when(jnp.logical_or(here.y == 1, here.y == 3))
            def _():
                for copy in self.up(j):
                    copy.wait_recv()

            @pl.when(here.y == 2)
            def _():
                for copy in self.down(j, False):
                    copy.wait_recv()

            heads = self.heads(j)
            before = self.below[heads].astype(jnp.float32) + self.above[heads].astype(jnp.float32)
            own, other = self.state[here.c, heads], self.part[heads]
            self.stage[heads] = (before + own * (1.0 - second)).astype(jnp.bfloat16)
            self.state_in[here.c, heads] = (before + other * second).astype(jnp.bfloat16)
            if j == 0:
                kbefore = self.kbelow[...] + self.kabove[...]
                self.kstage[...] = kbefore + self.sums[here.c] * (1.0 - second)
                self.sum_in[here.c] = kbefore + self.ksum[...] * second
            for copy in self.give(j):
                copy.start()

    def take(self):
        all_here(self.stage, self.frecv.at[0], self.here)
        all_here(self.kstage, self.frecv.at[1], self.here)

    def finish_send(self):
        for copy in self.exchange():
            copy.wait_send()
        all_sent(self.stage, self.fsend.at[0], self.here)
        all_sent(self.kstage, self.fsend.at[1], self.here)

        @pl.when(self.here.y < NY - 1)
        def _():
            all_sent(self.cout, self.usend.at[0], self.here)
            all_sent(self.kout, self.usend.at[1], self.here)

        @pl.when(jnp.logical_or(self.here.y == 0, self.here.y == 3))
        def _():
            all_sent(self.above, self.dsend.at[0], self.here)
            all_sent(self.kabove, self.dsend.at[1], self.here)


def normalise(projected, gain, out):
    def rows(r, _):
        some = pl.ds(pl.multiple_of(r * 16, 16), 16)
        wide = projected[some].astype(jnp.float32)
        scale = lax.rsqrt(jnp.mean(wide * wide, axis=1, keepdims=True) + 1e-05)
        out[some] = (wide * scale * gain[...]).astype(jnp.bfloat16)
        return 0

    lax.fori_loop(0, BLOCK // 16, rows, 0)


def whole_kernel(
    q_hbm, k_hbm, v_hbm, gain_hbm, targets, domains_hbm, wo_hbm, w_hbm, projected, small,
    queries, keys, values, gain, domains, qf, kf, probs, numer, state, sums, part, ksum, below, kbelow, above, kabove, cout, kout,
    stage, kstage, state_in, sum_in, attended, wo, halves, given, acts, wv, tg, tcol, out_stats, in_stats, dom,
    near, xsend, xrecv, usend, urecv, downsend, downrecv, fsend, frecv, zsend, zrecv, hsend, hrecv, psend, precv,
    gsend, grecv, rsend, rrecv, rprecv, tsend, trecv, ssend, srecv, dsend, drecv,
):
    here = Place()
    for ref in (below, kbelow, above, kabove):
        ref[...] = jnp.zeros_like(ref)
    moves = (
        (k_hbm, keys), (v_hbm, values), (q_hbm, queries), (gain_hbm, gain), (targets, tg.at[here.pos]),
        (domains_hbm, domains),
    )
    loads = [pltpu.make_async_copy(src, dst, near.at[2 + n]) for n, (src, dst) in enumerate(moves)]
    for load in loads:
        load.start()
    greet_all(here)
    partner = here.at(c=1 - here.c)
    half = D // 2
    wo_rows = pl.ds(pl.multiple_of(here.y * 16, 16), 16)
    wo_own = wo_hbm.at[wo_rows, pl.ds(pl.multiple_of(here.c * half, half), half)]
    wo_place = wo.at[here.x, 0, here.y]
    own_wo = pltpu.make_async_copy(wo_own, wo_place, near.at[1])
    own_wo.start()

    ring = VocabRing(here, w_hbm, wv, near.at[0], rsend, rrecv, rprecv)
    loads[0].wait()
    loads[1].wait()
    local_states(keys, values, kf, state, sums)
    for load in loads[2:]:
        load.wait()
    await_all()
    def wo_give(*steps):
        for i in steps:
            place = NEAR.index(-i if i < 4 else NZ - i)
            to = here.at(z=lax.rem(here.z + i, NZ))
            remote(wo_own, wo.at[here.x, place, here.y], zsend, zrecv.at[0 if place < 5 else 1], to).start()

    wo_give(2, 6, 1, 7)
    prefix = Prefix(
        here,
        (state, sums, part, ksum, below, kbelow, above, kabove, cout, kout, stage, kstage, state_in, sum_in),
        (xsend, xrecv, usend, urecv, downsend, downrecv, fsend, frecv),
    )
    weights = PlaneGather(
        here, lambda x, y, start, count: wo.at[x, pl.ds(start, count), y],
        WO_CUTS, functools.partial(places_of_event, wo), True, psend, precv,
    )
    mine, theirs = attended.at[here.c], attended.at[1 - here.c]
    rows_over = remote(mine, mine, hsend.at[0], hrecv.at[0], partner)

    def give_targets(i, _):
        slot, peer = here.plane_peer(i)
        own = tg.at[here.pos]
        remote(own, own, tsend, trecv, peer).start()
        return 0

    for copy in prefix.exchange():
        copy.start()
    inner_blocks(0, queries, kf, values, qf, probs, numer)
    for copy in prefix.exchange():
        copy.wait_recv()
    prefix.start()
    wo_give(4, 3, 5)
    ring.begin()
    inner_blocks(HALF_HEADS, queries, kf, values, qf, probs, numer)
    own_wo.wait()
    all_here(wo.at[0, 0:4, 0], zrecv.at[0], here)
    weights.start(1, "B1+o")
    weights.start(1, "B1-o")
    weights.start(1, "A1+")
    weights.start(1, "A1-")
    prefix.relay()
    all_here(wo.at[0, 0:3, 0], zrecv.at[1], here)
    weights.start(0, "A1+")
    weights.start(0, "A1-")
    weights.start(0, "B1+o")
    weights.start(0, "B1-o")
    lax.fori_loop(1, 16, give_targets, 0)
    weights.event(1, (1,))
    weights.event(1, (0,))
    weights.event(2)
    ring.advance(1)
    weights.event(3)
    prefix.finish()
    prefix.take()
    outer_blocks(0, qf, probs, numer, state_in, sum_in, mine)
    outer_blocks(HALF_HEADS, qf, probs, numer, state_in, sum_in, mine)
    rows_over.start()
    weights.event(4)
    target_columns(here, tg, tcol, tsend, trecv)
    weights.event(5)
    weights.event(6)
    weights.event(7)
    weights.event(8)
    remote(theirs, theirs, hsend.at[0], hrecv.at[0], partner).wait_recv()
    weights.event(9)

    order = [pick((0, 2, 4, 6, 7, 5, 3, 1), lax.rem(n - here.z + NZ, NZ)) for n in range(NZ)]

    def project(n, _):
        cols = pl.ds(pl.multiple_of(n * TILE, TILE), TILE)
        rows = jnp.concatenate([attended[0], attended[1]], axis=0)
        w = jnp.concatenate(
            [wo[x, place, :, :, cols].reshape(NY * 16, TILE) for x in range(NX) for place in order], axis=0
        )
        both = jnp.dot(rows, w, preferred_element_type=jnp.float32).astype(jnp.bfloat16)
        low = here.c == 0
        halves[here.c, :, cols] = jnp.where(low, both[:BLOCK], both[BLOCK:])
        given[:, cols] = jnp.where(low, both[BLOCK:], both[:BLOCK])
        remote(given.at[:, cols], halves.at[here.c, :, cols], hsend.at[1], hrecv.at[1], partner).start()
        return 0

    lax.fori_loop(0, half // TILE, project, 0)
    ring.advance(2)
    all_here(given, hrecv.at[1], here)
    projected[:, :half] = halves[0]
    projected[:, half:] = halves[1]
    normalise(projected, gain, acts.at[here.pos])
    gather = PlaneGather(
        here, lambda x, y, start, count: acts.at[x * NY + y, pl.ds(start, count)],
        ROW_CUTS, functools.partial(rows_of_event, acts), False, gsend, grecv,
    )
    gather.begin()
    ring.own().wait()
    vocab_part(here, gather, ring, acts, wv, tcol, out_stats, in_stats, ssend, srecv)
    losses = losses_of(here, out_stats, in_stats, ssend, srecv)
    means = domain_part(here, losses, domains, dom, dsend, drecv)
    first = lax.broadcasted_iota(jnp.int32, (8, 128), 0) == 0
    small[...] = jnp.where(first, losses, means)
    all_sent(wo.at[0, 0:7, 0], zsend, here)
    prefix.finish_send()
    all_sent(acts.at[0:15, 0:64], psend, here)
    rows_over.wait_send()
    all_sent(given, hsend.at[1], here)
    all_sent(acts.at[0:15], gsend, here)
    ring.finish_send()
    finish_sends(here, in_stats, ssend, tg, tsend, dom, dsend)


def outputs_kernel(projected, small, projected_out, loss_out, mean_out):
    projected_out[...] = projected[...]
    loss_out[...] = small[0:1]
    mean_out[...] = small[1, :DOMAINS]


def on_device(queries, keys, values, w_out, norm_gain, w_vocab, targets, domains):
    vmem = pl.BlockSpec(memory_space=pltpu.VMEM)
    dma = pltpu.SemaphoreType.DMA
    low, wide = jnp.bfloat16, jnp.float32
    anywhere = pl.BlockSpec(memory_space=pl.ANY)
    projected, small = pl.pallas_call(
        whole_kernel,
        out_shape=(
            jax.ShapeDtypeStruct((BLOCK, D), low),
            jax.ShapeDtypeStruct((8, BLOCK), wide),
        ),
        in_specs=[anywhere] * 8,
        out_specs=(vmem, vmem),
        scratch_shapes=[
            pltpu.VMEM((BLOCK, D), low),
            pltpu.VMEM((BLOCK, D), low),
            pltpu.VMEM((BLOCK, D), low),
            pltpu.VMEM((1, D), wide),
            pltpu.SMEM((DOCS,), jnp.int32),
            pltpu.VMEM((BLOCK, D), low),
            pltpu.VMEM((BLOCK, D), low),
            pltpu.VMEM((HEADS, BLOCK, BLOCK), low),
            pltpu.VMEM((BLOCK, D), wide),
            pltpu.VMEM((2, HALF_HEADS, HD, HD), wide),
            pltpu.VMEM((2, HALF_HEADS, 1, HD), wide),
            pltpu.VMEM((HALF_HEADS, HD, HD), wide),
            pltpu.VMEM((HALF_HEADS, 1, HD), wide),
            pltpu.VMEM((HALF_HEADS, HD, HD), low),
            pltpu.VMEM((HALF_HEADS, 1, HD), wide),
            pltpu.VMEM((HALF_HEADS, HD, HD), low),
            pltpu.VMEM((HALF_HEADS, 1, HD), wide),
            pltpu.VMEM((HALF_HEADS, HD, HD), low),
            pltpu.VMEM((HALF_HEADS, 1, HD), wide),
            pltpu.VMEM((HALF_HEADS, HD, HD), low),
            pltpu.VMEM((HALF_HEADS, 1, HD), wide),
            pltpu.VMEM((2, HALF_HEADS, HD, HD), low),
            pltpu.VMEM((2, HALF_HEADS, 1, HD), wide),
            pltpu.VMEM((2, BLOCK, D), low),
            pltpu.VMEM((NX, NZ, NY, 16, D // 2), low),
            pltpu.VMEM((2, BLOCK, D // 2), low),
            pltpu.VMEM((BLOCK, D // 2), low),
            pltpu.VMEM((16, BLOCK, D), low),
            pltpu.VMEM((NZ, D, TILE), low),
            pltpu.VMEM((16, 1, BLOCK), jnp.int32),
            pltpu.VMEM((16, BLOCK, BLOCK), wide),
            pltpu.VMEM((8, 2, 8, 128), wide),
            pltpu.VMEM((2, 16, 8, 128), wide),
            pltpu.VMEM((2, 16, 8, 128), wide),
            dma((8,)),
            dma((2,)),
            dma((2,)),
            dma((2,)),
            dma((CHUNKS + 1,)),
            dma((2,)),
            dma((CHUNKS + 1,)),
            dma((2,)),
            dma((2,)),
            dma(()),
            dma((2,)),
            dma((2,)),
            dma((2,)),
            dma(()),
            dma((len(EVENT) + 1,)),
            dma(()),
            dma((len(EVENT),)),
            dma(()),
            dma((4,)),
            dma((2,)),
            dma(()),
            dma(()),
            dma(()),
            dma(()),
            dma((2,)),
            dma((2,)),
        ],
        compiler_params=pltpu.CompilerParams(
            collective_id=0, has_side_effects=True, vmem_limit_bytes=60 * 1024 * 1024
        ),
    )(queries[0], keys[0], values[0], norm_gain[None], targets, domains, w_out, w_vocab)
    projected, losses, means = pl.pallas_call(
        outputs_kernel,
        out_shape=(
            jax.ShapeDtypeStruct((BLOCK, D), low),
            jax.ShapeDtypeStruct((1, BLOCK), wide),
            jax.ShapeDtypeStruct((DOMAINS,), wide),
        ),
        in_specs=[vmem, vmem],
        out_specs=(vmem, vmem, vmem),
    )(projected, small)
    return (projected[None], losses, means)


def solution(mesh):
    return jax.shard_map(
        on_device,
        mesh=mesh,
        in_specs=(
            P("doc", "seq", None),
            P("doc", "seq", None),
            P("doc", "seq", None),
            P("doc", None),
            P(),
            P(None, "doc"),
            P("doc", "seq"),
            P(),
        ),
        out_specs=(P("doc", "seq", None), P("doc", "seq"), P()),
        check_vma=False,
    )
```

```python
import functools

import jax
import jax.numpy as jnp
from jax import lax
from jax.experimental import pallas as pl
from jax.experimental.pallas import tpu as pltpu
from jax.sharding import PartitionSpec as P

HEADS = 16
HD = 128
DOMAINS = 7
BLOCK = 128
D = 2048
SHARD = 896
DOCS = 32
TILE = 256
NX, NY, NZ = 4, 4, 8
MESH = pl.DeviceIdType.MESH


def around(count):
    return [(n + count // 2 - 1) % count - (count // 2 - 1) for n in range(count)]


PLANE = sorted(
    ((dx, dy) for dx in around(NX) for dy in around(NY) if (dx, dy) != (0, 0)), key=lambda at: -abs(at[0]) - abs(at[1])
)
COLUMN = sorted(
    ((dz, dc) for dz in around(NZ) for dc in (0, 1) if (dz, dc) != (0, 0)), key=lambda at: -2 * abs(at[0]) - at[1]
)


class Place:
    def __init__(self):
        seq, doc = lax.axis_index("seq"), lax.axis_index("doc")
        self.y, self.c = lax.div(seq, 2), lax.rem(seq, 2)
        self.x, self.z = lax.div(doc, NZ), lax.rem(doc, NZ)
        self.pos = self.x * NY + self.y

    def at(self, x=None, y=None, z=None, c=None):
        x = self.x if x is None else x
        y = self.y if y is None else y
        z = self.z if z is None else z
        c = self.c if c is None else c
        return {"seq": y * 2 + c, "doc": x * NZ + z}

    def step(self, axis, by):
        if axis == "x":
            return self.at(x=lax.rem(self.x + by + NX, NX))
        if axis == "y":
            return self.at(y=lax.rem(self.y + by + NY, NY))
        return self.at(z=lax.rem(self.z + by + NZ, NZ))

    def slot(self, dx, dy):
        return lax.rem(self.x + dx + NX, NX) * NY + lax.rem(self.y + dy + NY, NY)

    def plane_peer(self, i):
        other = lax.rem(self.pos + i, NX * NY)
        return other, self.at(x=lax.div(other, NY), y=lax.rem(other, NY))

    def plane_at(self, dx, dy):
        return self.at(x=lax.rem(self.x + dx + NX, NX), y=lax.rem(self.y + dy + NY, NY))

    def column_at(self, dz, dc):
        return self.at(z=lax.rem(self.z + dz + NZ, NZ), c=lax.rem(self.c + dc, 2))


def remote(src, dst, send, recv, to):
    return pltpu.make_async_remote_copy(
        src_ref=src, dst_ref=dst, send_sem=send, recv_sem=recv, device_id=to, device_id_type=MESH
    )


def all_sent(ref, sem, here):
    remote(ref, ref, sem, sem, here.at(c=1 - here.c)).wait_send()


def all_here(ref, sem, here):
    remote(ref, ref, sem, sem, here.at(c=1 - here.c)).wait_recv()


def greet_all(here):
    barrier = pltpu.get_barrier_semaphore()

    for near, far in zip(PLANE, COLUMN):
        pl.semaphore_signal(barrier, 1, device_id=here.column_at(*far), device_id_type=MESH)
        pl.semaphore_signal(barrier, 1, device_id=here.plane_at(*near), device_id_type=MESH)


def await_all():
    pl.semaphore_wait(pltpu.get_barrier_semaphore(), 30)


class VocabRing:
    def __init__(self, here, w_hbm, wv, near, send, recv, precv):
        self.here, self.w, self.wv, self.near = here, w_hbm, wv, near
        self.send, self.recv, self.precv = send, recv, precv
        self.first = pl.multiple_of(here.c * (D // 2), D // 2)
        self.column = pl.multiple_of(jnp.minimum(here.y * TILE, SHARD - TILE), 128)

    def rows(self, part):
        if part == "lo":
            return pl.ds(self.first, D // 4)
        if part == "hi":
            return pl.ds(self.first + D // 4, D // 4)
        return pl.ds(self.first, D // 2)

    def slot(self, off):
        return lax.rem(self.here.z + off + NZ, NZ)

    def hop(self, k, by):
        part = "all" if k < 4 else ("lo" if by > 0 else "hi")
        dst = self.wv.at[self.slot(-by * (k - 1)), self.rows(part)]
        src = self.w.at[self.rows(part), pl.ds(self.column, TILE)] if k == 1 else dst
        return remote(src, dst, self.send, self.recv.at[k - 1], self.here.step("z", by))

    def share(self, k, by):
        part = "all" if k < 4 else ("lo" if by > 0 else "hi")
        ref = self.wv.at[self.slot(-by * k), self.rows(part)]
        return remote(ref, ref, self.send, self.precv.at[k // 4], self.here.at(c=1 - self.here.c))

    def own(self):
        return pltpu.make_async_copy(self.w.at[:, pl.ds(self.column, TILE)], self.wv.at[self.here.z], self.near)

    def begin(self):
        for by in (1, -1):
            self.hop(1, by).start()
        self.own().start()

    def advance(self, k):
        all_here(self.wv.at[0] if k < 4 else self.wv.at[0, : D // 2], self.recv.at[k - 1], self.here)
        for by in (1, -1):
            if k < 4:
                self.hop(k + 1, by).start()
            self.share(k, by).start()

    def shared(self, last):
        if last:
            all_here(self.wv.at[0, : D // 2], self.precv.at[1], self.here)
        else:
            all_here(self.wv.at[0:3], self.precv.at[0], self.here)

    def finish_send(self):
        all_sent(self.wv.at[0:7], self.send, self.here)


HALF = {
    "A1+": (0, 0, "all", "A", 1),
    "A1-": (0, 0, "all", "A", -1),
    "B1+o": (0, 0, "all", "B", 1),
    "B1-o": (0, 0, "all", "B", -1),
    "A2+": (-1, 0, "lo", "A", 1),
    "A2-": (1, 0, "hi", "A", -1),
    "B1+m": (-1, 0, "all", "B", 1),
    "B1-m": (-1, 0, "all", "B", -1),
    "B1+p": (1, 0, "all", "B", 1),
    "B1-p": (1, 0, "all", "B", -1),
    "B1+l": (-2, 0, "lo", "B", 1),
    "B1-l": (-2, 0, "lo", "B", -1),
    "B1+h": (2, 0, "hi", "B", 1),
    "B1-h": (2, 0, "hi", "B", -1),
    "B2+o": (0, -1, "lo", "B", 1),
    "B2-o": (0, 1, "hi", "B", -1),
    "B2+p": (1, -1, "all", "B", 1),
    "B2-m": (-1, 1, "all", "B", -1),
    "B2+l": (-2, -1, "lo", "B", 1),
    "B2-h": (2, 1, "hi", "B", -1),
}
EVENT = {
    1: (("A1+", "A1-"), ("A2+", "A2-", "B1+m", "B1-m", "B1+p", "B1-p")),
    2: (("B1+o", "B1-o"), ("B2+o", "B2-o")),
    3: (("A2+", "A2-"), ("B1+l", "B1-l", "B1+h", "B1-h")),
    4: (("B1+m", "B1-m"), ("B2-m",)),
    5: (("B1+p", "B1-p"), ("B2+p",)),
    6: (("B2+o", "B2-o"), ()),
    7: (("B1+l", "B1-l", "B1+h", "B1-h"), ("B2+l", "B2-h")),
    8: (("B2+p", "B2-m"), ()),
    9: (("B2+l", "B2-h"), ()),
}
EVENT_OF = {name: e for e, (names, _) in EVENT.items() for name in names}
WO_CUTS = ((5, 6, 8), (0, 2, 5))
ROW_CUTS = ((0, 32, 64), (64, 96, 128))


class PlaneGather:
    def __init__(self, here, view, cuts, amount, apart, send, recv):
        self.here, self.view, self.cuts, self.amount, self.apart = here, view, cuts, amount, apart
        self.send_sem, self.recv_sem = send, recv

    def start(self, half, name):
        a, b, part, axis, by = HALF[name]
        first, second = ("x", "y") if half == 0 else ("y", "x")
        dx, dy = (a, b) if half == 0 else (b, a)
        first_row, middle, last_row = self.cuts[half]
        begin, end = {"all": (first_row, last_row), "lo": (first_row, middle), "hi": (middle, last_row)}[part]
        column, row = lax.rem(self.here.x + dx + NX, NX), lax.rem(self.here.y + dy + NY, NY)
        ref = self.view(column, row, begin, end - begin)
        to = self.here.step(first if axis == "A" else second, by)
        remote(ref, ref, self.send_sem, self.recv_sem.at[self.index(EVENT_OF[name], half)], to).start()

    def index(self, e, half):
        return len(EVENT) if e == 1 and half == 1 and self.apart else e - 1

    def begin_along(self, axis):
        half = 0 if axis == "x" else 1
        for name in ("A1+", "A1-"):
            self.start(half, name)
        for name in ("B1+o", "B1-o"):
            self.start(1 - half, name)

    def begin(self):
        self.begin_along("x")
        self.begin_along("y")

    def event(self, e, halves=(0, 1)):
        apart = len(halves) == 1
        all_here(self.amount(e, halves[0] if apart else None), self.recv_sem.at[self.index(e, halves[0])], self.here)
        for name in EVENT[e][1]:
            for half in halves:
                self.start(half, name)


def rows_of_event(acts, e, half):
    blocks = {1: 2, 2: 2, 3: 1, 4: 2, 5: 2, 6: 1, 7: 2, 8: 2, 9: 1}[e]
    return acts.at[0:blocks]


def places_of_event(wo, e, half):
    if half is not None:
        return wo.at[0, 0:6, 0] if half == 0 else wo.at[0, 0:5, 0:2]
    places = {2: 4, 3: 2, 4: 4, 5: 4, 6: 2, 7: 4, 8: 4, 9: 2}[e]
    return wo.at[0, 0:places]


PIECES = (
    ((0, 0), (0, 0), (-1, 0), (0, -1)),
    ((1, 0), (0, 1), (0, -1), (-1, 0)),
    ((0, 1), (1, 0), (2, 0), (0, 2)),
    ((-1, -1), (-1, -1), (-1, 1), (1, -1)),
    ((1, -1), (-1, 1), (1, 1), (1, 1)),
    ((0, 2), (2, 0), (2, -1), (-1, 2)),
    ((2, 1), (1, 2), (-1, 2), (2, -1)),
    ((1, 2), (2, 1), (2, 2), (2, 2)),
)
EVENTS = ((1, 2, 3), (), (4,), (5,), (), (6, 7), (8,), (9,))
NEAR = (0, -1, 1, -2, 2, -3, 3, 4)


def pick(table, i):
    value = table[0]
    for n in range(1, len(table)):
        value = jnp.where(i == n, table[n], value)
    return value


def stats_of(here, acts, wv, tcol, slots):
    rows = 2 * BLOCK
    lane = lax.broadcasted_iota(jnp.int32, (rows, 128), 1)
    whole = here.y < NY - 1
    column = jnp.minimum(here.y * TILE, SHARD - TILE)
    middle = BLOCK // 2

    def joined(ref):
        return jnp.concatenate(
            [ref[slot, (n % 2) * middle : (n % 2 + 1) * middle] for n, slot in enumerate(slots)], axis=0
        )

    wanted = joined(tcol) - lane.astype(jnp.float32)

    def tile(n, carry):
        top, total, hit = carry
        shard = lax.rem(here.z + NEAR[n] + NZ, NZ)
        logits = jnp.dot(joined(acts), wv[shard], preferred_element_type=jnp.float32)
        base = ((here.x * NZ + shard) * SHARD + column).astype(jnp.float32)
        one, two = logits[:, :128], logits[:, 128:]
        now = jnp.maximum(top, jnp.maximum(jnp.where(whole, one, two), two))
        add = jnp.exp(one - now)
        total = total * jnp.exp(top - now) + jnp.exp(two - now) + jnp.where(whole, add, 0.0)
        hit = hit + jnp.where(wanted == jnp.where(whole, base, -1e6), one, 0.0)
        hit = hit + jnp.where(wanted == base + 128.0, two, 0.0)
        return now, total, hit

    carry = (
        jnp.full((rows, 128), -jnp.inf, jnp.float32),
        jnp.zeros((rows, 128), jnp.float32),
        jnp.zeros((rows, 128), jnp.float32),
    )
    for n in range(NZ):
        carry = tile(n, carry)
    top, total, hit = carry
    peak = jnp.max(top, axis=1, keepdims=True)
    total = jnp.sum(total * jnp.exp(top - peak), axis=1, keepdims=True)
    hit = jnp.sum(hit, axis=1, keepdims=True)
    return jnp.where(lane == 0, peak, jnp.where(lane == 1, total, jnp.where(lane == 2, hit, 0.0)))


def target_columns(here, tg, tcol, tsend, trecv):
    def columns(slot):
        wide = jnp.broadcast_to(tg[slot].astype(jnp.float32), (BLOCK, BLOCK))
        tcol[slot] = wide.T

    def take_targets(i, _):
        columns(i)
        return 0

    all_here(tg.at[0:15], trecv, here)
    lax.fori_loop(0, 16, take_targets, 0)


def stat_copies(here, i, pair, slots, out_stats, in_stats, ssend, srecv):
    for half in (0, 1):
        slot = slots[2 * pair + half]
        to = here.at(x=lax.div(slot, NY), y=lax.rem(slot, NY))
        yield remote(
            out_stats.at[i, pair], in_stats.at[half, here.pos], ssend, srecv, to
        )


def slots_of(here, i):
    return [
        here.slot(pick([four[n][0] for four in PIECES], i), pick([four[n][1] for four in PIECES], i)) for n in range(4)
    ]


def vocab_part(here, gather, ring, acts, wv, tcol, out_stats, in_stats, ssend, srecv):
    def batch(i, _):
        for n, events in enumerate(EVENTS):
            if events:

                @pl.when(i == n)
                def _():
                    for e in events:
                        gather.event(e)
                        if e == 1:
                            ring.advance(3)
                    if n == 0:
                        ring.shared(False)
                        ring.advance(4)
                        ring.shared(True)

        slots = slots_of(here, i)
        table = stats_of(here, acts, wv, tcol, slots)
        for pair in (0, 1):
            out_stats[i, pair] = table[pair * BLOCK : (pair + 1) * BLOCK].T[:8]

        @pl.when(i > 0)
        def _():
            for copy in stat_copies(here, i, 0, slots, out_stats, in_stats, ssend, srecv):
                copy.start()

        for copy in stat_copies(here, i, 1, slots, out_stats, in_stats, ssend, srecv):
            copy.start()
        return 0

    lax.fori_loop(0, len(PIECES), batch, 0)


def losses_of(here, out_stats, in_stats, ssend, srecv):
    for half in (0, 1):
        in_stats[half, here.pos] = out_stats[0, 0]

    all_here(in_stats.at[:, 0:15], srecv, here)
    early = lax.broadcasted_iota(jnp.int32, (8, BLOCK), 1) < BLOCK // 2
    stats = [jnp.where(early, in_stats[0, n], in_stats[1, n]) for n in range(16)]
    top = functools.reduce(jnp.maximum, [s[0:1] for s in stats])
    total = sum(s[1:2] * jnp.exp(s[0:1] - top) for s in stats)
    hit = sum(s[2:3] for s in stats)
    return top + jnp.log(total) - hit


def domain_part(here, losses, domains, dom, dsend, drecv):
    lane = lax.broadcasted_iota(jnp.int32, (8, 128), 1)
    mine = domains[here.x * NZ + here.z]
    value = jnp.broadcast_to(jnp.sum(losses, axis=1, keepdims=True), (8, 128))
    value = jnp.where(lane == mine, value, 0.0)
    for stage in (0, 1):
        peers = [here.plane_at(*at) for at in PLANE] if stage == 0 else [here.column_at(*at) for at in COLUMN]
        own = here.pos if stage == 0 else here.z * 2 + here.c
        dom[stage, own] = value
        for peer in peers:
            remote(dom.at[stage, own], dom.at[stage, own], dsend.at[stage], drecv.at[stage], peer).start()
        all_here(dom.at[stage, 0:15], drecv.at[stage], here)
        value = sum(dom[stage, n] for n in range(16))
    counts = jnp.zeros((8, 128), jnp.float32)
    for n in range(DOCS):
        counts = counts + jnp.where(lane == domains[n], 1.0, 0.0)
    return value / jnp.maximum(counts * (NY * 2 * BLOCK), 1.0)


def finish_sends(here, in_stats, ssend, tg, tsend, dom, dsend):
    all_sent(in_stats.at[:, 0:15], ssend, here)
    all_sent(tg.at[0:15], tsend, here)
    for stage in (0, 1):
        all_sent(dom.at[stage, 0:15], dsend.at[stage], here)


HALF_HEADS = HEADS // 2
CHUNKS = 4
PER = HALF_HEADS // CHUNKS


def feature(inputs):
    wide = inputs.astype(jnp.float32)
    return jnp.where(wide > 0.0, wide + 1.0, jnp.exp(jnp.minimum(wide, 0.0))).astype(jnp.bfloat16)


def head_slice(h):
    return pl.ds(pl.multiple_of(h * HD, HD), HD)


def by_four(one, count):
    def turn(t, _):
        for n in range(4):
            one(t * 4 + n, 0)
        return 0

    lax.fori_loop(0, count // 4, turn, 0)


def local_states(keys, values, kf, state, sums):
    def one(h, _):
        cols = head_slice(h)
        feat = feature(keys[:, cols])
        kf[:, cols] = feat
        group, n = lax.div(h, HALF_HEADS), lax.rem(h, HALF_HEADS)
        state[group, n] = lax.dot_general(
            feat, values[:, cols], (((0,), (0,)), ((), ())), preferred_element_type=jnp.float32
        )
        sums[group, n] = jnp.sum(feat.astype(jnp.float32), axis=0, keepdims=True)
        return 0

    by_four(one, HEADS)


def inner_blocks(first, queries, kf, values, qf, probs, numer):
    row = lax.broadcasted_iota(jnp.int32, (BLOCK, BLOCK), 0)
    causal = row >= lax.broadcasted_iota(jnp.int32, (BLOCK, BLOCK), 1)

    def one(n, _):
        h = first + n
        cols = head_slice(h)
        feat = feature(queries[:, cols])
        qf[:, cols] = feat
        scores = lax.dot_general(feat, kf[:, cols], (((1,), (1,)), ((), ())), preferred_element_type=jnp.float32)
        prob = jnp.where(causal, scores, 0.0).astype(jnp.bfloat16)
        probs[h] = prob
        numer[:, cols] = jnp.dot(prob, values[:, cols], preferred_element_type=jnp.float32)
        return 0

    by_four(one, HALF_HEADS)


def outer_blocks(first, qf, probs, numer, state_in, sum_in, out):
    def one(n, _):
        h = first + n
        cols = head_slice(h)
        group, n = lax.div(h, HALF_HEADS), lax.rem(h, HALF_HEADS)
        feat = qf[:, cols]
        top = numer[:, cols] + jnp.dot(feat, state_in[group, n], preferred_element_type=jnp.float32)
        below = probs[h].astype(jnp.float32) + feat.astype(jnp.float32) * sum_in[group, n]
        out[:, cols] = (top / jnp.sum(below, axis=1, keepdims=True)).astype(jnp.bfloat16)
        return 0

    by_four(one, HALF_HEADS)


class Prefix:
    def __init__(self, here, refs, sems):
        self.here = here
        (self.state, self.sums, self.part, self.ksum, self.below, self.kbelow, self.above, self.kabove, self.cout, self.kout,
         self.stage, self.kstage, self.state_in, self.sum_in) = refs
        (self.xsend, self.xrecv, self.usend, self.urecv, self.dsend, self.drecv, self.fsend, self.frecv) = sems
        self.partner = here.at(c=1 - here.c)

    def exchange(self):
        other = 1 - self.here.c
        return (
            remote(self.state.at[other], self.part, self.xsend.at[0], self.xrecv.at[0], self.partner),
            remote(self.sums.at[other], self.ksum, self.xsend.at[1], self.xrecv.at[1], self.partner),
        )

    def heads(self, j):
        return pl.ds(j * PER, PER)

    def move(self, j, src, ksrc, dst, kdst, send, recv, to):
        heads = self.heads(j)
        copies = [remote(src.at[heads], dst.at[heads], send.at[0], recv.at[j], to)]
        if j == 0:
            copies.append(remote(ksrc, kdst, send.at[1], recv.at[CHUNKS], to))
        return copies

    def up(self, j):
        return self.move(
            j, self.cout, self.kout, self.below, self.kbelow, self.usend, self.urecv, self.here.step("y", 1)
        )

    def down(self, j, relay):
        src, ksrc = (self.above, self.kabove) if relay else (self.cout, self.kout)
        return self.move(j, src, ksrc, self.above, self.kabove, self.dsend, self.drecv, self.here.step("y", -1))

    def total(self, j, add):
        heads = self.heads(j)
        value = self.state[self.here.c, heads] + self.part[heads]
        if add:
            value = value + self.below[heads].astype(jnp.float32)
        self.cout[heads] = value.astype(jnp.bfloat16)
        if j == 0:
            value = self.sums[self.here.c] + self.ksum[...]
            self.kout[...] = value + self.kbelow[...] if add else value

    def start(self):
        @pl.when(self.here.y < 2)
        def _():
            for j in range(CHUNKS):
                self.total(j, False)
                for copy in self.up(j):
                    copy.start()

                @pl.when(self.here.y == 0)
                def _():
                    for copy in self.down(j, False):
                        copy.start()

    def relay(self):
        @pl.when(self.here.y == 2)
        def _():
            for j in range(CHUNKS):
                for copy in self.up(j):
                    copy.wait_recv()
                self.total(j, True)
                for copy in self.up(j):
                    copy.start()

        @pl.when(self.here.y == 3)
        def _():
            for j in range(CHUNKS):
                for copy in self.down(j, False):
                    copy.wait_recv()
                for copy in self.down(j, True):
                    copy.start()

    def give(self, j):
        heads = self.heads(j)
        there = self.state_in.at[self.here.c, heads]
        copies = [remote(self.stage.at[heads], there, self.fsend.at[0], self.frecv.at[0], self.partner)]
        if j == 0:
            copies.append(
                remote(self.kstage, self.sum_in.at[self.here.c], self.fsend.at[1], self.frecv.at[1], self.partner)
            )
        return copies

    def finish(self):
        here = self.here
        second = (here.c == 1).astype(jnp.float32)
        for j in range(CHUNKS):

            @pl.when(jnp.logical_or(here.y == 1, here.y == 3))
            def _():
                for copy in self.up(j):
                    copy.wait_recv()

            @pl.when(here.y == 2)
            def _():
                for copy in self.down(j, False):
                    copy.wait_recv()

            heads = self.heads(j)
            before = self.below[heads].astype(jnp.float32) + self.above[heads].astype(jnp.float32)
            own, other = self.state[here.c, heads], self.part[heads]
            self.stage[heads] = (before + own * (1.0 - second)).astype(jnp.bfloat16)
            self.state_in[here.c, heads] = (before + other * second).astype(jnp.bfloat16)
            if j == 0:
                kbefore = self.kbelow[...] + self.kabove[...]
                self.kstage[...] = kbefore + self.sums[here.c] * (1.0 - second)
                self.sum_in[here.c] = kbefore + self.ksum[...] * second
            for copy in self.give(j):
                copy.start()

    def take(self):
        all_here(self.stage, self.frecv.at[0], self.here)
        all_here(self.kstage, self.frecv.at[1], self.here)

    def finish_send(self):
        for copy in self.exchange():
            copy.wait_send()
        all_sent(self.stage, self.fsend.at[0], self.here)
        all_sent(self.kstage, self.fsend.at[1], self.here)

        @pl.when(self.here.y < NY - 1)
        def _():
            all_sent(self.cout, self.usend.at[0], self.here)
            all_sent(self.kout, self.usend.at[1], self.here)

        @pl.when(jnp.logical_or(self.here.y == 0, self.here.y == 3))
        def _():
            all_sent(self.above, self.dsend.at[0], self.here)
            all_sent(self.kabove, self.dsend.at[1], self.here)


def normalise(projected, gain, out):
    def rows(r, _):
        some = pl.ds(pl.multiple_of(r * 16, 16), 16)
        wide = projected[some].astype(jnp.float32)
        scale = lax.rsqrt(jnp.mean(wide * wide, axis=1, keepdims=True) + 1e-05)
        out[some] = (wide * scale * gain[...]).astype(jnp.bfloat16)
        return 0

    by_four(rows, BLOCK // 16)


def whole_kernel(
    q_hbm, k_hbm, v_hbm, gain_hbm, targets, domains_hbm, wo_hbm, w_hbm, projected_hbm, small,
    queries, keys, values, projected, gain, domains, qf, kf, probs, numer, state, sums, part, ksum, below, kbelow, above, kabove, cout, kout,
    stage, kstage, state_in, sum_in, attended, wo, halves, given, acts, wv, tg, tcol, out_stats, in_stats, dom,
    near, xsend, xrecv, usend, urecv, downsend, downrecv, fsend, frecv, zsend, zrecv, hsend, hrecv, psend, precv,
    gsend, grecv, rsend, rrecv, rprecv, tsend, trecv, ssend, srecv, dsend, drecv,
):
    here = Place()
    for ref in (below, kbelow, above, kabove):
        ref[...] = jnp.zeros_like(ref)
    moves = (
        (k_hbm, keys), (v_hbm, values), (q_hbm, queries), (gain_hbm, gain), (targets, tg.at[here.pos]),
        (domains_hbm, domains),
    )
    loads = [pltpu.make_async_copy(src, dst, near.at[2 + n]) for n, (src, dst) in enumerate(moves)]
    for load in loads:
        load.start()
    greet_all(here)
    partner = here.at(c=1 - here.c)
    half = D // 2
    wo_rows = pl.ds(pl.multiple_of(here.y * 16, 16), 16)
    wo_own = wo_hbm.at[wo_rows, pl.ds(pl.multiple_of(here.c * half, half), half)]
    wo_place = wo.at[here.x, 0, here.y]
    own_wo = pltpu.make_async_copy(wo_own, wo_place, near.at[1])
    own_wo.start()

    ring = VocabRing(here, w_hbm, wv, near.at[0], rsend, rrecv, rprecv)
    loads[0].wait()
    loads[1].wait()
    local_states(keys, values, kf, state, sums)
    for load in loads[2:]:
        load.wait()
    await_all()
    def wo_give(*steps):
        for i in steps:
            place = NEAR.index(-i if i < 4 else NZ - i)
            to = here.at(z=lax.rem(here.z + i, NZ))
            remote(wo_own, wo.at[here.x, place, here.y], zsend, zrecv.at[0 if place < 5 else 1], to).start()

    wo_give(2, 6, 1, 7)
    prefix = Prefix(
        here,
        (state, sums, part, ksum, below, kbelow, above, kabove, cout, kout, stage, kstage, state_in, sum_in),
        (xsend, xrecv, usend, urecv, downsend, downrecv, fsend, frecv),
    )
    weights = PlaneGather(
        here, lambda x, y, start, count: wo.at[x, pl.ds(start, count), y],
        WO_CUTS, functools.partial(places_of_event, wo), True, psend, precv,
    )
    mine, theirs = attended.at[here.c], attended.at[1 - here.c]
    rows_over = remote(mine, mine, hsend.at[0], hrecv.at[0], partner)

    def give_targets(i, _):
        slot, peer = here.plane_peer(i)
        own = tg.at[here.pos]
        remote(own, own, tsend, trecv, peer).start()
        return 0

    for copy in prefix.exchange():
        copy.start()
    inner_blocks(0, queries, kf, values, qf, probs, numer)
    for copy in prefix.exchange():
        copy.wait_recv()
    prefix.start()
    wo_give(4, 3, 5)
    ring.begin()
    inner_blocks(HALF_HEADS, queries, kf, values, qf, probs, numer)
    own_wo.wait()
    all_here(wo.at[0, 0:4, 0], zrecv.at[0], here)
    weights.start(1, "B1+o")
    weights.start(1, "B1-o")
    weights.start(1, "A1+")
    weights.start(1, "A1-")
    prefix.relay()
    all_here(wo.at[0, 0:3, 0], zrecv.at[1], here)
    weights.start(0, "A1+")
    weights.start(0, "A1-")
    weights.start(0, "B1+o")
    weights.start(0, "B1-o")
    lax.fori_loop(1, 16, give_targets, 0)
    weights.event(1, (1,))
    weights.event(1, (0,))
    weights.event(2)
    ring.advance(1)
    weights.event(3)
    prefix.finish()
    prefix.take()
    outer_blocks(0, qf, probs, numer, state_in, sum_in, mine)
    outer_blocks(HALF_HEADS, qf, probs, numer, state_in, sum_in, mine)
    rows_over.start()
    weights.event(4)
    target_columns(here, tg, tcol, tsend, trecv)
    weights.event(5)
    weights.event(6)
    weights.event(7)
    weights.event(8)
    remote(theirs, theirs, hsend.at[0], hrecv.at[0], partner).wait_recv()
    weights.event(9)

    order = [pick((0, 2, 4, 6, 7, 5, 3, 1), lax.rem(n - here.z + NZ, NZ)) for n in range(NZ)]

    def project(n, _):
        cols = pl.ds(pl.multiple_of(n * TILE, TILE), TILE)
        rows = jnp.concatenate([attended[0], attended[1]], axis=0)
        w = jnp.concatenate(
            [wo[x, place, :, :, cols].reshape(NY * 16, TILE) for x in range(NX) for place in order], axis=0
        )
        both = jnp.dot(rows, w, preferred_element_type=jnp.float32).astype(jnp.bfloat16)
        low = here.c == 0
        halves[here.c, :, cols] = jnp.where(low, both[:BLOCK], both[BLOCK:])
        given[:, cols] = jnp.where(low, both[BLOCK:], both[:BLOCK])
        remote(given.at[:, cols], halves.at[here.c, :, cols], hsend.at[1], hrecv.at[1], partner).start()
        return 0

    lax.fori_loop(0, half // TILE, project, 0)
    ring.advance(2)
    all_here(given, hrecv.at[1], here)
    projected[:, :half] = halves[0]
    projected[:, half:] = halves[1]
    normalise(projected, gain, acts.at[here.pos])
    gather = PlaneGather(
        here, lambda x, y, start, count: acts.at[x * NY + y, pl.ds(start, count)],
        ROW_CUTS, functools.partial(rows_of_event, acts), False, gsend, grecv,
    )
    gather.begin()
    keep = pltpu.make_async_copy(projected, projected_hbm, near.at[8])
    keep.start()
    ring.own().wait()
    vocab_part(here, gather, ring, acts, wv, tcol, out_stats, in_stats, ssend, srecv)
    losses = losses_of(here, out_stats, in_stats, ssend, srecv)
    means = domain_part(here, losses, domains, dom, dsend, drecv)
    first = lax.broadcasted_iota(jnp.int32, (8, 128), 0) == 0
    small[...] = jnp.where(first, losses, means)
    all_sent(wo.at[0, 0:7, 0], zsend, here)
    prefix.finish_send()
    all_sent(acts.at[0:15, 0:64], psend, here)
    keep.wait()
    rows_over.wait_send()
    all_sent(given, hsend.at[1], here)
    all_sent(acts.at[0:15], gsend, here)
    ring.finish_send()
    finish_sends(here, in_stats, ssend, tg, tsend, dom, dsend)


def outputs_kernel(projected, small, projected_out, loss_out, mean_out):
    projected_out[...] = projected[...]
    loss_out[...] = small[0:1]
    mean_out[...] = small[1, :DOMAINS]


def on_device(queries, keys, values, w_out, norm_gain, w_vocab, targets, domains):
    vmem = pl.BlockSpec(memory_space=pltpu.VMEM)
    dma = pltpu.SemaphoreType.DMA
    low, wide = jnp.bfloat16, jnp.float32
    anywhere = pl.BlockSpec(memory_space=pl.ANY)
    projected, small = pl.pallas_call(
        whole_kernel,
        out_shape=(
            jax.ShapeDtypeStruct((BLOCK, D), low),
            jax.ShapeDtypeStruct((8, BLOCK), wide),
        ),
        in_specs=[anywhere] * 8,
        out_specs=(anywhere, vmem),
        scratch_shapes=[
            pltpu.VMEM((BLOCK, D), low),
            pltpu.VMEM((BLOCK, D), low),
            pltpu.VMEM((BLOCK, D), low),
            pltpu.VMEM((BLOCK, D), low),
            pltpu.VMEM((1, D), wide),
            pltpu.SMEM((DOCS,), jnp.int32),
            pltpu.VMEM((BLOCK, D), low),
            pltpu.VMEM((BLOCK, D), low),
            pltpu.VMEM((HEADS, BLOCK, BLOCK), low),
            pltpu.VMEM((BLOCK, D), wide),
            pltpu.VMEM((2, HALF_HEADS, HD, HD), wide),
            pltpu.VMEM((2, HALF_HEADS, 1, HD), wide),
            pltpu.VMEM((HALF_HEADS, HD, HD), wide),
            pltpu.VMEM((HALF_HEADS, 1, HD), wide),
            pltpu.VMEM((HALF_HEADS, HD, HD), low),
            pltpu.VMEM((HALF_HEADS, 1, HD), wide),
            pltpu.VMEM((HALF_HEADS, HD, HD), low),
            pltpu.VMEM((HALF_HEADS, 1, HD), wide),
            pltpu.VMEM((HALF_HEADS, HD, HD), low),
            pltpu.VMEM((HALF_HEADS, 1, HD), wide),
            pltpu.VMEM((HALF_HEADS, HD, HD), low),
            pltpu.VMEM((HALF_HEADS, 1, HD), wide),
            pltpu.VMEM((2, HALF_HEADS, HD, HD), low),
            pltpu.VMEM((2, HALF_HEADS, 1, HD), wide),
            pltpu.VMEM((2, BLOCK, D), low),
            pltpu.VMEM((NX, NZ, NY, 16, D // 2), low),
            pltpu.VMEM((2, BLOCK, D // 2), low),
            pltpu.VMEM((BLOCK, D // 2), low),
            pltpu.VMEM((16, BLOCK, D), low),
            pltpu.VMEM((NZ, D, TILE), low),
            pltpu.VMEM((16, 1, BLOCK), jnp.int32),
            pltpu.VMEM((16, BLOCK, BLOCK), wide),
            pltpu.VMEM((8, 2, 8, 128), wide),
            pltpu.VMEM((2, 16, 8, 128), wide),
            pltpu.VMEM((2, 16, 8, 128), wide),
            dma((9,)),
            dma((2,)),
            dma((2,)),
            dma((2,)),
            dma((CHUNKS + 1,)),
            dma((2,)),
            dma((CHUNKS + 1,)),
            dma((2,)),
            dma((2,)),
            dma(()),
            dma((2,)),
            dma((2,)),
            dma((2,)),
            dma(()),
            dma((len(EVENT) + 1,)),
            dma(()),
            dma((len(EVENT),)),
            dma(()),
            dma((4,)),
            dma((2,)),
            dma(()),
            dma(()),
            dma(()),
            dma(()),
            dma((2,)),
            dma((2,)),
        ],
        compiler_params=pltpu.CompilerParams(
            collective_id=0, has_side_effects=True, vmem_limit_bytes=60 * 1024 * 1024
        ),
    )(queries[0], keys[0], values[0], norm_gain[None], targets, domains, w_out, w_vocab)
    projected, losses, means = pl.pallas_call(
        outputs_kernel,
        out_shape=(
            jax.ShapeDtypeStruct((BLOCK, D), low),
            jax.ShapeDtypeStruct((1, BLOCK), wide),
            jax.ShapeDtypeStruct((DOMAINS,), wide),
        ),
        in_specs=[vmem, vmem],
        out_specs=(vmem, vmem, vmem),
    )(projected, small)
    return (projected[None], losses, means)


def solution(mesh):
    return jax.shard_map(
        on_device,
        mesh=mesh,
        in_specs=(
            P("doc", "seq", None),
            P("doc", "seq", None),
            P("doc", "seq", None),
            P("doc", None),
            P(),
            P(None, "doc"),
            P("doc", "seq"),
            P(),
        ),
        out_specs=(P("doc", "seq", None), P("doc", "seq"), P()),
        check_vma=False,
    )
```
